32 devices in a mesh: groups: 2 (over x), seq: 16 (over z, y, core).
Axes of the slice: x: 2, y: 2, z: 4, core: 2. Of those that a mesh axis runs over, the one named last changes fastest.
Arguments:
- queries: bfloat16 [64, 4, 8192], P(('groups', 'seq')), parts along dimension 0, may hold values from -128 to 128
- step_keys: bfloat16 [64, 4, 1024], P(('groups', 'seq')), parts along dimension 0, may hold values from -15 to 15
- step_values: bfloat16 [64, 4, 1024], P(('groups', 'seq')), parts along dimension 0, may hold values from -48 to 48
- sample_keys: bfloat16 [64, 1024, 1024], P(('groups', 'seq')), parts along dimension 0, may hold values from -6 to 6
- sample_values: bfloat16 [64, 1024, 1024], P(('groups', 'seq')), parts along dimension 0, may hold values from -48 to 48
- suffix_len: int32 [64], P(('groups', 'seq')), parts along dimension 0, may hold values from 128 to 1024
- prompt_id: int32 [64], P(('groups', 'seq')), parts along dimension 0, may hold values from 0 to 1, as said below
- document_keys: bfloat16 [4, 4096, 1024], P('groups', 'seq'), parts along dimension 0, may hold values from -6 to 6
- document_values: bfloat16 [4, 4096, 1024], P('groups', 'seq'), parts along dimension 0, may hold values from -48 to 48
Outputs:
- attended: bfloat16 [64, 4, 8192], P(('groups', 'seq')), parts along dimension 0
The draws below stay inside these ranges and needn't reach their ends.
There are 2 independent parts, one for each index of `groups`. The reference program is written for one: setup_inputs(seed, part) draws one part's arguments, and reference() takes and returns one part's arrays. A program takes and returns all parts, laid end to end along the dimension named above; each array names one. Nothing has to cross between parts.
Inputs may be any that keep to these rules, and one draw needn't show every extreme that they name: `prompt_id`: each prompt id is held by exactly 16 samples.
All inputs are finite; a program needn't handle non-finite values.
Results may differ from the reference program's by a relative error of at most 0.0013.
Values may be sent and summed in bfloat16 or wider, within the bound.
A program may use at most 192 MiB of HBM per device.

```python
import jax
import jax.numpy as jnp
from jax import lax

QUERY_HEADS = 64
KEY_VALUE_HEADS = 8
HEAD_SIZE = 128
GROUP_PROMPTS = 2
DECODE_STEPS = 4
BLOCK_PREFIX = 256
SUFFIX_SLOTS = 1024
GROUP_SAMPLES = 32
PREFIX_LENGTH = 4096


def draw_queries(key, part):
    leading_key = jax.random.fold_in(jax.random.fold_in(key, 101), 0)
    entry_list = jnp.clip(2.0 * jax.random.normal(leading_key, (GROUP_SAMPLES, DECODE_STEPS, QUERY_HEADS, HEAD_SIZE), jnp.float32), -12.0, 12.0)
    return entry_list.reshape(GROUP_SAMPLES, DECODE_STEPS, QUERY_HEADS * HEAD_SIZE).astype(jnp.bfloat16)


def draw_document_keys(key, part):
    leading_key = jax.random.fold_in(key, 202)
    entry_list = jnp.clip(jax.random.normal(leading_key, (GROUP_PROMPTS, PREFIX_LENGTH, KEY_VALUE_HEADS, HEAD_SIZE), jnp.float32), -6.0, 6.0)
    return entry_list.reshape(GROUP_PROMPTS, PREFIX_LENGTH, KEY_VALUE_HEADS * HEAD_SIZE).astype(jnp.bfloat16)


def draw_prompt_id(key, part):
    shuffled = jax.random.permutation(jax.random.fold_in(key, 303), GROUP_SAMPLES)
    return (shuffled // (GROUP_SAMPLES // GROUP_PROMPTS)).astype(jnp.int32)


def with_ends(entries, key, low, high):
    spot = [jax.random.randint(jax.random.fold_in(key, axis), (), 0, length) for axis, length in enumerate(entries.shape)]
    widest = entries.shape.index(max(entries.shape))
    beside = spot[:widest] + [(spot[widest] + 1) % entries.shape[widest]] + spot[widest + 1:]
    return entries.at[tuple(spot)].set(low).at[tuple(beside)].set(high)


def block_scale(stream_key, dims, cuts, least, top_value):
    loudness = 1.0
    for dim, parts in cuts:
        draws = jax.random.uniform(jax.random.fold_in(jax.random.fold_in(stream_key, 6), dim), (parts,), jnp.float32, least / len(cuts), top_value / len(cuts))
        loudness = loudness * jnp.repeat(jnp.exp(draws), dims[dim] // parts).reshape((-1,) + (1,) * (len(dims) - 1 - dim))
    return loudness


def centred(own_key, extent, scale, most, cuts=(), held_as=jnp.bfloat16):
    result = jax.random.normal(own_key, extent, jnp.float32) * scale
    if len(cuts) > 0:
        result = block_scale(own_key, extent, cuts, -0.22, 0.18) * result
    return jnp.clip(result, min=-most, max=most).astype(held_as)


def setup_inputs(seed: int = 0, part: int = 0) -> dict:
    keys = jax.random.split(jax.random.key(seed), 10)
    part_splits = jax.random.split(jax.random.fold_in(keys[9], part), 10)
    queries = draw_queries(jax.random.fold_in(jax.random.fold_in(keys[9], part), 71), part)
    step_keys = centred(part_splits[1], (GROUP_SAMPLES, DECODE_STEPS, KEY_VALUE_HEADS * HEAD_SIZE), 2.5, 15.0, ((0, 16),))
    step_values = centred(part_splits[2], (GROUP_SAMPLES, DECODE_STEPS, KEY_VALUE_HEADS * HEAD_SIZE), 8.0, 48.0, ((0, 16),))
    sample_keys = centred(part_splits[3], (GROUP_SAMPLES, SUFFIX_SLOTS, KEY_VALUE_HEADS * HEAD_SIZE), 1.0, 6.0, ((0, 16),))
    sample_values = centred(part_splits[4], (GROUP_SAMPLES, SUFFIX_SLOTS, KEY_VALUE_HEADS * HEAD_SIZE), 8.0, 48.0, ((0, 16),))
    suffix_len = with_ends(jax.random.randint(part_splits[5], (GROUP_SAMPLES,), SUFFIX_SLOTS // 8, SUFFIX_SLOTS + 1), jax.random.fold_in(part_splits[5], 1), SUFFIX_SLOTS // 8, SUFFIX_SLOTS).astype(jnp.int32)
    prompt_id = draw_prompt_id(jax.random.fold_in(jax.random.fold_in(keys[9], part), 71), part)
    document_keys = draw_document_keys(jax.random.fold_in(jax.random.fold_in(keys[9], part), 71), part)
    document_values = centred(part_splits[8], (GROUP_PROMPTS, PREFIX_LENGTH, KEY_VALUE_HEADS * HEAD_SIZE), 8.0, 48.0, ((1, 16),))
    return dict(queries=queries, step_keys=step_keys, step_values=step_values, sample_keys=sample_keys, sample_values=sample_values, suffix_len=suffix_len, prompt_id=prompt_id, document_keys=document_keys, document_values=document_values)


def rounded(values):
    return lax.optimization_barrier(values.astype(jnp.bfloat16)).astype(jnp.float32)


def reference(queries, step_keys, step_values, sample_keys, sample_values, suffix_len, prompt_id, document_keys, document_values):
    group_count = QUERY_HEADS // KEY_VALUE_HEADS
    block_list = PREFIX_LENGTH // BLOCK_PREFIX
    scaling = HEAD_SIZE ** -0.5

    def per_sample(members):
        query_vector, recent_key_rows, recent_value_rows, cache_key_rows, cache_value_rows, length, prompt_row = members
        query_matrix = query_vector.astype(jnp.float32).reshape(DECODE_STEPS, KEY_VALUE_HEADS, group_count, HEAD_SIZE)
        present_keys = lax.dynamic_index_in_dim(document_keys, prompt_row, 0, keepdims=False)
        present_values = lax.dynamic_index_in_dim(document_values, prompt_row, 0, keepdims=False)
        present_keys = present_keys.astype(jnp.float32).reshape(block_list, BLOCK_PREFIX, KEY_VALUE_HEADS, HEAD_SIZE)
        present_values = present_values.astype(jnp.float32).reshape(block_list, BLOCK_PREFIX, KEY_VALUE_HEADS, HEAD_SIZE)
        prefix_score = jnp.einsum('tgrd,bkgd->btgrk', query_matrix, present_keys) * scaling
        prefix_max = jnp.max(prefix_score, axis=-1)
        prefix_exp = jnp.exp(prefix_score - prefix_max[..., None])
        prefix_total = jnp.sum(prefix_exp, axis=-1)
        prefix_out = jnp.einsum('btgrk,bkgd->btgrd', rounded(prefix_exp), present_values)

        cached_key_set = cache_key_rows.astype(jnp.float32).reshape(SUFFIX_SLOTS, KEY_VALUE_HEADS, HEAD_SIZE)
        cached_value_set = cache_value_rows.astype(jnp.float32).reshape(SUFFIX_SLOTS, KEY_VALUE_HEADS, HEAD_SIZE)
        recent_keys = recent_key_rows.astype(jnp.float32).reshape(DECODE_STEPS, KEY_VALUE_HEADS, HEAD_SIZE)
        recent_values = recent_value_rows.astype(jnp.float32).reshape(DECODE_STEPS, KEY_VALUE_HEADS, HEAD_SIZE)
        cache_score = jnp.einsum('tgrd,kgd->tgrk', query_matrix, cached_key_set) * scaling
        fresh_score = jnp.einsum('tgrd,ugd->tgru', query_matrix, recent_keys) * scaling
        cache_live = (jnp.arange(SUFFIX_SLOTS, dtype=jnp.int32) < length)[None, None, None, :]
        fresh_live = (jnp.arange(DECODE_STEPS)[None, :] <= jnp.arange(DECODE_STEPS)[:, None])[:, None, None, :]
        suffix_max = jnp.maximum(jnp.max(jnp.where(cache_live, cache_score, -jnp.inf), axis=-1),
                                 jnp.max(jnp.where(fresh_live, fresh_score, -jnp.inf), axis=-1))
        cache_exp = jnp.where(cache_live, jnp.exp(cache_score - suffix_max[..., None]), 0.0)
        fresh_exp = jnp.where(fresh_live, jnp.exp(fresh_score - suffix_max[..., None]), 0.0)
        suffix_total = jnp.sum(cache_exp, axis=-1) + jnp.sum(fresh_exp, axis=-1)
        suffix_out = (jnp.einsum('tgrk,kgd->tgrd', rounded(cache_exp), cached_value_set)
                      + jnp.einsum('tgru,ugd->tgrd', rounded(fresh_exp), recent_values))

        highest = jnp.maximum(jnp.max(prefix_max, axis=0), suffix_max)
        prefix_scale = jnp.exp(prefix_max - highest[None])
        suffix_scale = jnp.exp(suffix_max - highest)
        numerator = jnp.sum(prefix_out * prefix_scale[..., None], axis=0) + suffix_out * suffix_scale[..., None]
        denominator = jnp.sum(prefix_total * prefix_scale, axis=0) + suffix_total * suffix_scale
        return (numerator / denominator[..., None]).reshape(DECODE_STEPS, QUERY_HEADS * HEAD_SIZE).astype(jnp.bfloat16)

    return lax.map(per_sample, (queries, step_keys, step_values, sample_keys, sample_values, suffix_len, prompt_id))
```

```python
import functools

import jax
import jax.numpy as jnp
from jax import lax
from jax.experimental import pallas as pl
from jax.experimental.pallas import tpu as pltpu
from jax.sharding import PartitionSpec as P

QUERY_HEADS = 64
KEY_VALUE_HEADS = 8
HEAD_SIZE = 128
HALF = KEY_VALUE_HEADS // 2
GROUP = QUERY_HEADS // KEY_VALUE_HEADS
LOG2E = 1.4426950408889634
FACTOR = (HEAD_SIZE ** (-0.5)) * LOG2E
ID_ROWS = 16
LEVELS = 32767.0
MESH = pl.DeviceIdType.MESH
NT = (((1,), (1,)), ((), ()))
NN = (((1,), (0,)), ((), ()))
F32, BF16, I16 = jnp.float32, jnp.bfloat16, jnp.int16


def quantize(values):
    scale = jnp.maximum(jnp.max(jnp.abs(values), axis=0, keepdims=True), 1e-30)
    return jnp.round(values * (LEVELS / scale)).astype(jnp.int32).astype(I16), scale


def kernel(
    n,
    len_ref,
    id_ref,
    query_ref,
    step_key_ref,
    step_value_ref,
    sample_keys,
    sample_values,
    document_keys,
    document_values,
    out_ref,
    key_buf,
    value_buf,
    doc_keys,
    doc_values,
    value_t,
    query_msg,
    query_pair,
    query_buf,
    own_part,
    own_stat,
    y_send,
    y_send_stat,
    y_got,
    y_got_stat,
    z_send,
    z_send_stat,
    z_got,
    z_got_stat,
    suffix_out,
    suffix_max,
    suffix_total,
    local_sem,
    doc_send,
    doc_recv,
    query_send,
    query_recv,
    y_send_sem,
    y_stat_sem,
    y_recv,
    y_stat_recv,
    z_send_sem,
    z_stat_sem,
    z_recv,
    z_stat_recv,
):
    me = lax.axis_index("seq")
    core = lax.rem(me, 2)
    row = lax.rem(lax.div(me, 2), 2)
    line = lax.div(me, 4)
    lines = n // 4
    samples, cache = sample_keys.shape[0], sample_keys.shape[1]
    steps = step_key_ref.shape[1]
    rows = steps * GROUP
    core_rows = samples * rows
    chip_rows = 2 * core_rows
    prompts, block = document_keys.shape[:2]
    half_width = HALF * HEAD_SIZE
    padded = key_buf.shape[1]

    def device(at_line, at_row, at_core):
        return at_line * 4 + at_row * 2 + at_core

    def line_at(step):
        return lax.rem(line + step, lines)

    def remote(source, target, send, recv, other):
        return pltpu.make_async_remote_copy(
            src_ref=source,
            dst_ref=target,
            send_sem=send,
            recv_sem=recv,
            device_id={"seq": other},
            device_id_type=MESH,
        )

    def arrived(ref, sem):
        pltpu.make_async_copy(ref, ref, sem).wait()

    partner = device(line, row, 1 - core)
    across = device(line, 1 - row, core)

    barrier = pltpu.get_barrier_semaphore()

    def greet(other):
        pl.semaphore_signal(barrier, inc=1, device_id={"seq": other}, device_id_type=MESH)

    greet(partner)
    for c in range(2):
        greet(device(line, 1 - row, c))

    def greet_line(step, carry):
        for c in range(2):
            greet(device(line_at(step), row, c))
        return carry

    lax.fori_loop(1, lines, greet_line, 0)

    def half_of(ref, half):
        return ref.at[:, :, pl.ds(pl.multiple_of(half * half_width, half_width), half_width)]

    def own_rows(ref):
        return ref.at[:, pl.ds(pl.multiple_of(core * block, block), block), :]

    local = [
        pltpu.make_async_copy(half_of(document_keys, core), own_rows(doc_keys), local_sem.at[0]),
        pltpu.make_async_copy(half_of(document_values, core), own_rows(doc_values), local_sem.at[1]),
        pltpu.make_async_copy(sample_keys, key_buf.at[:, pl.ds(0, cache), :], local_sem.at[2]),
        pltpu.make_async_copy(sample_values, value_buf.at[:, pl.ds(0, cache), :], local_sem.at[3]),
    ]
    for copy in local:
        copy.start()

    query_pair[...] = jnp.zeros(query_pair.shape, BF16)
    for s in range(samples):
        for g in range(KEY_VALUE_HEADS):
            first = g * GROUP
            part = jnp.concatenate(
                [
                    query_ref[s, :, (first + r) * HEAD_SIZE : (first + r + 1) * HEAD_SIZE].astype(F32)
                    for r in range(GROUP)
                ],
                axis=0,
            ).astype(BF16)
            query_msg[g // HALF, pl.ds((g % HALF) * core_rows + s * rows, rows), :] = part
            side = g % 2
            query_pair[
                g // 2, s, pl.ds(side * rows, rows), pl.ds(side * HEAD_SIZE, HEAD_SIZE)
            ] = part
    tile_row = lax.broadcasted_iota(jnp.int32, (ID_ROWS, HEAD_SIZE), 0)
    tile_lane = lax.broadcasted_iota(jnp.int32, (ID_ROWS, HEAD_SIZE), 1)
    tile_sample = lax.rem(tile_lane, core_rows) // rows
    marks = jnp.zeros((ID_ROWS, HEAD_SIZE), F32)
    for s in range(samples):
        mine = (tile_row == s) | ((tile_row >= samples) & (tile_sample == s))
        marks = jnp.where(mine, id_ref[s].astype(F32), marks)
    for half in range(2):
        query_msg[half, pl.ds(HALF * core_rows, ID_ROWS), :] = marks.astype(BF16)

    pl.semaphore_wait(barrier, 2 * lines + 1)

    def send_query(half, other):
        remote(query_msg.at[half], query_buf.at[me], query_send, query_recv.at[me], other).start()

    for c in range(2):
        send_query(c, device(line, 1 - row, c))

    def send_line(step, carry):
        target = lax.rem(line + lines - step, lines)
        for c in range(2):
            send_query(c, device(target, row, c))
        return carry

    lax.fori_loop(1, lines, send_line, 0)
    send_query(1 - core, partner)
    swaps = [
        remote(half_of(source, 1 - core), own_rows(target), doc_send.at[k], doc_recv.at[k], partner)
        for k, (source, target) in enumerate(
            ((document_keys, doc_keys), (document_values, doc_values))
        )
    ]
    for copy in swaps:
        copy.start()

    query_buf[me] = query_msg[core]
    for s in range(samples):
        for buf, step_ref in ((key_buf, step_key_ref), (value_buf, step_value_ref)):
            buf[s, pl.ds(cache, padded - cache), :] = jnp.zeros(
                (padded - cache, buf.shape[2]), buf.dtype
            )
            buf[s, pl.ds(cache, steps), :] = step_ref[s]
    local[2].wait()
    local[3].wait()

    slot = lax.broadcasted_iota(jnp.int32, (2 * rows, padded), 1)
    now = lax.rem(lax.broadcasted_iota(jnp.int32, (2 * rows, padded), 0), steps)
    fresh = (slot >= cache) & (slot - cache <= now)

    def suffix(pair, carry=0):
        wide = pl.ds(pl.multiple_of(pair * 2 * HEAD_SIZE, 2 * HEAD_SIZE), 2 * HEAD_SIZE)
        for s in range(samples):
            scores = lax.dot_general(
                query_pair[pair, s], key_buf[s, :, wide], NT, preferred_element_type=F32
            )
            scores = jnp.where((slot < len_ref[s]) | fresh, scores, -jnp.inf)
            peak = jnp.max(scores, axis=1, keepdims=True)
            expo = jnp.exp2((scores - peak) * FACTOR)
            total = jnp.sum(expo, axis=1, keepdims=True)
            result = lax.dot_general(
                expo.astype(BF16), value_buf[s, :, wide], NN, preferred_element_type=F32
            )
            for side in range(2):
                part = pl.ds(side * core_rows + s * rows, rows)
                cut = slice(side * rows, (side + 1) * rows)
                suffix_max[pair, part, :] = peak[cut]
                suffix_total[pair, part, :] = total[cut]
                suffix_out[pair, part, :] = result[
                    cut, side * HEAD_SIZE : (side + 1) * HEAD_SIZE
                ]
        return carry

    lax.fori_loop(0, HALF // 2, suffix, 0)

    local[0].wait()
    local[1].wait()
    for copy in swaps:
        copy.wait_recv()
    for h in range(HALF):
        for p in range(prompts):
            value_t[h, pl.ds(p * HEAD_SIZE, HEAD_SIZE), :] = doc_values[
                p, :, h * HEAD_SIZE : (h + 1) * HEAD_SIZE
            ].T

    lane = lax.broadcasted_iota(jnp.int32, (1, chip_rows), 1)

    def relay(step):
        for c in range(2):
            source = device(line_at(step), row, c)
            arrived(query_buf.at[source], query_recv.at[source])
            remote(
                query_buf.at[source],
                query_buf.at[source],
                query_send,
                query_recv.at[source],
                across,
            ).start()

    def attend(step):
        there = line_at(step)
        mine = [device(there, row, c) for c in range(2)]
        theirs = [device(there, 1 - row, c) for c in range(2)]

        @pl.when(step == 0)
        def _():
            arrived(query_buf.at[partner], query_recv.at[partner])

        for source in theirs:
            arrived(query_buf.at[source], query_recv.at[source])
        sources = mine + theirs
        tiles = [
            query_buf[source, pl.ds(HALF * core_rows, ID_ROWS), :].astype(F32)
            for source in sources
        ]
        masks = [
            jnp.concatenate(
                [
                    jnp.broadcast_to(
                        jnp.where(tile[s : s + 1] == p, 1.0, 0.0), (rows, HEAD_SIZE)
                    )
                    for tile in tiles
                    for s in range(samples)
                ],
                axis=0,
            ).astype(BF16)
            for p in range(prompts)
        ]
        marks = jnp.concatenate(
            [
                jnp.where(
                    lane < core_rows,
                    tiles[2 * k][samples : samples + 1],
                    tiles[2 * k + 1][samples : samples + 1],
                )
                for k in range(2)
            ],
            axis=1,
        )
        for pair in range(HALF // 2):
            stats = []
            for h in (2 * pair, 2 * pair + 1):
                query = jnp.concatenate(
                    [query_buf[source, pl.ds(h * core_rows, core_rows), :] for source in sources],
                    axis=0,
                )
                query = jnp.concatenate([query * mask for mask in masks], axis=1)
                cols = slice(h * HEAD_SIZE, (h + 1) * HEAD_SIZE)
                keys = jnp.concatenate([doc_keys[p, :, cols] for p in range(prompts)], axis=1)
                scores = lax.dot_general(keys, query, NT, preferred_element_type=F32)
                peak = jnp.max(scores, axis=0, keepdims=True)
                expo = jnp.exp2((scores - peak) * FACTOR)
                total = jnp.sum(expo, axis=0, keepdims=True)
                both = lax.dot_general(
                    value_t[h], expo.astype(BF16), NN, preferred_element_type=F32
                )
                result = both[:HEAD_SIZE]
                for p in range(1, prompts):
                    result = jnp.where(
                        marks == p, both[p * HEAD_SIZE : (p + 1) * HEAD_SIZE], result
                    )
                own_part[step, h] = result[:, :chip_rows]
                own_stat[step, h, 0:1, :] = peak[:, :chip_rows]
                own_stat[step, h, 1:2, :] = total[:, :chip_rows]
                y_send[step, h], scale = quantize(result[:, chip_rows:])
                stats += [peak[:, chip_rows:], total[:, chip_rows:], scale]
            y_send_stat[step, pair] = jnp.concatenate(
                stats + [jnp.zeros((2, chip_rows), F32)], axis=0
            )
            heads = pl.ds(2 * pair, 2)
            remote(
                y_send.at[step, heads],
                y_got.at[step, heads],
                y_send_sem,
                y_recv.at[step, pair],
                across,
            ).start()
            remote(
                y_send_stat.at[step, pair],
                y_got_stat.at[step, pair],
                y_stat_sem,
                y_stat_recv.at[step, pair],
                across,
            ).start()

    def give(source, target, send, recv, other):
        @pl.when(other != me)
        def _():
            remote(source, target, send, recv, other).start()

        @pl.when(other == me)
        def _():
            pltpu.make_async_copy(source, target, recv).start()

    def combine(step):
        there = line_at(step)
        stats = [[], []]
        for pair in range(HALF // 2):
            arrived(y_got.at[step, pl.ds(2 * pair, 2)], y_recv.at[step, pair])
            arrived(y_got_stat.at[step, pair], y_stat_recv.at[step, pair])
            merged = []
            got = y_got_stat[step, pair]
            for side in range(2):
                h = 2 * pair + side
                peak_a, total_a = own_stat[step, h, 0:1, :], own_stat[step, h, 1:2, :]
                peak_b, total_b, scale_b = (
                    got[3 * side : 3 * side + 1],
                    got[3 * side + 1 : 3 * side + 2],
                    got[3 * side + 2 : 3 * side + 3],
                )
                top = jnp.maximum(peak_a, peak_b)
                weight_a = jnp.exp2((peak_a - top) * FACTOR)
                weight_b = jnp.exp2((peak_b - top) * FACTOR)
                result = own_part[step, h] * weight_a + y_got[step, h].astype(jnp.int32).astype(
                    F32
                ) * (weight_b * (scale_b * (1.0 / LEVELS)))
                merged.append((result, top, total_a * weight_a + total_b * weight_b))
            for c in range(2):
                mixed = []
                for low, high in zip(*merged):
                    wide = jnp.broadcast_to(low, (max(8, low.shape[0]), chip_rows))
                    wide_high = jnp.broadcast_to(high, wide.shape)
                    if c == 0:
                        wide_high = pltpu.roll(wide_high, core_rows, 1)
                    else:
                        wide = pltpu.roll(wide, core_rows, 1)
                    mixed.append(
                        jnp.where(lane < core_rows, wide, wide_high)[: low.shape[0]]
                    )
                result, top, total = mixed
                at = (step * 2 + c) * 2 + pair
                z_send[at], scale = quantize(result)
                stats[c] += [top, total, scale]
                give(
                    z_send.at[at],
                    z_got.at[step, core, pair],
                    z_send_sem,
                    z_recv.at[step, core, pair],
                    device(there, row, c),
                )
        for c in range(2):
            z_send_stat[step * 2 + c] = jnp.concatenate(
                stats[c] + [jnp.zeros((2, chip_rows), F32)], axis=0
            )
            give(
                z_send_stat.at[step * 2 + c],
                z_got_stat.at[step, core],
                z_stat_sem,
                z_stat_recv.at[step, core],
                device(there, row, c),
            )

    def advance(step, carry):
        @pl.when(step + 1 < lines)
        def _():
            relay(step + 1)

        attend(step)

        @pl.when(step >= 1)
        def _():
            combine(step - 1)

        return carry

    lax.fori_loop(0, lines, advance, 0)
    suffix(HALF // 2)
    combine(lines - 1)
    lax.fori_loop(HALF // 2 + 1, HALF, suffix, 0)

    for half in range(2):
        for step in range(lines):
            arrived(z_got_stat.at[step, half], z_stat_recv.at[step, half])
        for pair in range(HALF // 2):
            for step in range(lines):
                arrived(z_got.at[step, half, pair], z_recv.at[step, half, pair])
            tops = [z_got_stat[step, half, 3 * pair : 3 * pair + 1, :] for step in range(lines)]
            top = functools.reduce(jnp.maximum, tops)
            above, below = 0.0, 0.0
            for step in range(lines):
                weight = jnp.exp2((tops[step] - top) * FACTOR)
                below = below + z_got_stat[step, half, 3 * pair + 1 : 3 * pair + 2, :] * weight
                scale = z_got_stat[step, half, 3 * pair + 2 : 3 * pair + 3, :]
                above = above + z_got[step, half, pair].astype(jnp.int32).astype(F32) * (
                    weight * (scale * (1.0 / LEVELS))
                )
            turned = jnp.concatenate([top, below, jnp.zeros((6, chip_rows), F32)], axis=0).T
            peak, total = turned[:, 0:1], turned[:, 1:2]
            at = half * (HALF // 2) + pair
            top = jnp.maximum(peak, suffix_max[at])
            weight = jnp.exp2((peak - top) * FACTOR)
            weight_own = jnp.exp2((suffix_max[at] - top) * FACTOR)
            out_ref[at] = (
                (above.T * weight + suffix_out[at] * weight_own)
                / (total * weight + suffix_total[at] * weight_own)
            ).astype(out_ref.dtype)

    sent = query_buf.at[pl.ds(0, n - 1)]
    pltpu.make_async_copy(sent, sent, query_send).wait()
    pltpu.make_async_copy(y_send, y_send, y_send_sem).wait()
    pltpu.make_async_copy(y_send_stat, y_send_stat, y_stat_sem).wait()
    sent = z_send.at[pl.ds(0, 4 * lines - 2)]
    pltpu.make_async_copy(sent, sent, z_send_sem).wait()
    sent = z_send_stat.at[pl.ds(0, 2 * lines - 1)]
    pltpu.make_async_copy(sent, sent, z_stat_sem).wait()
    for copy in swaps:
        copy.wait_send()


def body(
    queries,
    step_keys,
    step_values,
    sample_keys,
    sample_values,
    suffix_len,
    prompt_id,
    document_keys,
    document_values,
):
    n = lax.axis_size("seq")
    samples, steps = queries.shape[:2]
    cache = sample_keys.shape[1]
    width = KEY_VALUE_HEADS * HEAD_SIZE
    half_width = HALF * HEAD_SIZE
    prompts, block = document_keys.shape[:2]
    rows = steps * GROUP
    core_rows = samples * rows
    chip_rows = 2 * core_rows
    lines = n // 4
    padded = cache + 128
    pairs = HALF // 2
    vmem = pl.BlockSpec(memory_space=pltpu.VMEM)
    smem = pl.BlockSpec(memory_space=pltpu.SMEM)
    hbm = pl.BlockSpec(memory_space=pl.ANY)
    dma = pltpu.SemaphoreType.DMA
    result = pl.pallas_call(
        functools.partial(kernel, n),
        out_shape=jax.ShapeDtypeStruct((2 * pairs, 2 * core_rows, HEAD_SIZE), BF16),
        in_specs=[smem, smem, vmem, vmem, vmem, hbm, hbm, hbm, hbm],
        out_specs=vmem,
        scratch_shapes=[
            pltpu.VMEM((samples, padded, width), BF16),
            pltpu.VMEM((samples, padded, width), BF16),
            pltpu.VMEM((prompts, 2 * block, half_width), BF16),
            pltpu.VMEM((prompts, 2 * block, half_width), BF16),
            pltpu.VMEM((HALF, prompts * HEAD_SIZE, 2 * block), BF16),
            pltpu.VMEM((2, HALF * core_rows + ID_ROWS, HEAD_SIZE), BF16),
            pltpu.VMEM((2 * pairs, samples, 2 * rows, 2 * HEAD_SIZE), BF16),
            pltpu.VMEM((n, HALF * core_rows + ID_ROWS, HEAD_SIZE), BF16),
            pltpu.VMEM((lines, HALF, HEAD_SIZE, chip_rows), F32),
            pltpu.VMEM((lines, HALF, 8, chip_rows), F32),
            pltpu.VMEM((lines, HALF, HEAD_SIZE, chip_rows), I16),
            pltpu.VMEM((lines, pairs, 8, chip_rows), F32),
            pltpu.VMEM((lines, HALF, HEAD_SIZE, chip_rows), I16),
            pltpu.VMEM((lines, pairs, 8, chip_rows), F32),
            pltpu.VMEM((lines * 2 * pairs, HEAD_SIZE, chip_rows), I16),
            pltpu.VMEM((lines * 2, 8, chip_rows), F32),
            pltpu.VMEM((lines, 2, pairs, HEAD_SIZE, chip_rows), I16),
            pltpu.VMEM((lines, 2, 8, chip_rows), F32),
            pltpu.VMEM((2 * pairs, 2 * core_rows, HEAD_SIZE), F32),
            pltpu.VMEM((2 * pairs, 2 * core_rows, 1), F32),
            pltpu.VMEM((2 * pairs, 2 * core_rows, 1), F32),
            dma((4,)),
            dma((2,)),
            dma((2,)),
            dma,
            dma((n,)),
            dma,
            dma,
            dma((lines, pairs)),
            dma((lines, pairs)),
            dma,
            dma,
            dma((lines, 2, pairs)),
            dma((lines, 2)),
        ],
        compiler_params=pltpu.CompilerParams(
            collective_id=0, has_side_effects=True, vmem_limit_bytes=60 << 20
        ),
    )(
        suffix_len,
        prompt_id,
        queries,
        step_keys,
        step_values,
        sample_keys,
        sample_values,
        document_keys,
        document_values,
    )
    result = result.reshape(KEY_VALUE_HEADS, samples, GROUP, steps, HEAD_SIZE)
    return result.transpose(1, 3, 0, 2, 4).reshape(samples, steps, QUERY_HEADS * HEAD_SIZE)


def solution(mesh):
    return jax.shard_map(
        body,
        mesh=mesh,
        in_specs=(
            P(("groups", "seq"), None, None),
            P(("groups", "seq"), None, None),
            P(("groups", "seq"), None, None),
            P(("groups", "seq"), None, None),
            P(("groups", "seq"), None, None),
            P(("groups", "seq")),
            P(("groups", "seq")),
            P("groups", "seq", None),
            P("groups", "seq", None),
        ),
        out_specs=P(("groups", "seq"), None, None),
        check_vma=False,
    )
```

```python
import functools

import jax
import jax.numpy as jnp
from jax import lax
from jax.experimental import pallas as pl
from jax.experimental.pallas import tpu as pltpu
from jax.sharding import PartitionSpec as P

QUERY_HEADS = 64
KEY_VALUE_HEADS = 8
HEAD_SIZE = 128
HALF = KEY_VALUE_HEADS // 2
GROUP = QUERY_HEADS // KEY_VALUE_HEADS
LOG2E = 1.4426950408889634
FACTOR = (HEAD_SIZE ** (-0.5)) * LOG2E
ID_ROWS = 16
LEVELS = 32767.0
MESH = pl.DeviceIdType.MESH
NT = (((1,), (1,)), ((), ()))
NN = (((1,), (0,)), ((), ()))
F32, BF16, I16 = jnp.float32, jnp.bfloat16, jnp.int16


def quantize(values):
    scale = jnp.maximum(jnp.max(jnp.abs(values), axis=0, keepdims=True), 1e-30)
    return jnp.round(values * (LEVELS / scale)).astype(jnp.int32).astype(I16), scale


def kernel(
    n,
    len_ref,
    id_ref,
    queries,
    step_keys,
    step_values,
    sample_keys,
    sample_values,
    document_keys,
    document_values,
    out_ref,
    query_ref,
    step_key_ref,
    step_value_ref,
    key_buf,
    value_buf,
    doc_keys,
    doc_values,
    value_t,
    query_msg,
    query_pair,
    query_buf,
    own_part,
    own_stat,
    y_send,
    y_send_stat,
    y_got,
    y_got_stat,
    z_send,
    z_send_stat,
    z_got,
    z_got_stat,
    suffix_out,
    suffix_max,
    suffix_total,
    local_sem,
    doc_send,
    doc_recv,
    query_send,
    query_recv,
    y_send_sem,
    y_stat_sem,
    y_recv,
    y_stat_recv,
    z_send_sem,
    z_stat_sem,
    z_recv,
    z_stat_recv,
):
    me = lax.axis_index("seq")
    core = lax.rem(me, 2)
    row = lax.rem(lax.div(me, 2), 2)
    line = lax.div(me, 4)
    lines = n // 4
    samples, cache = sample_keys.shape[0], sample_keys.shape[1]
    steps = step_keys.shape[1]
    rows = steps * GROUP
    core_rows = samples * rows
    chip_rows = 2 * core_rows
    prompts, block = document_keys.shape[:2]
    half_width = HALF * HEAD_SIZE
    padded = key_buf.shape[1]

    def device(at_line, at_row, at_core):
        return at_line * 4 + at_row * 2 + at_core

    def line_at(step):
        return lax.rem(line + step, lines)

    def remote(source, target, send, recv, other):
        return pltpu.make_async_remote_copy(
            src_ref=source,
            dst_ref=target,
            send_sem=send,
            recv_sem=recv,
            device_id={"seq": other},
            device_id_type=MESH,
        )

    def arrived(ref, sem):
        pltpu.make_async_copy(ref, ref, sem).wait()

    partner = device(line, row, 1 - core)
    across = device(line, 1 - row, core)

    barrier = pltpu.get_barrier_semaphore()

    def greet(other):
        pl.semaphore_signal(barrier, inc=1, device_id={"seq": other}, device_id_type=MESH)

    greet(partner)
    for c in range(2):
        greet(device(line, 1 - row, c))

    def greet_line(step, carry):
        for c in range(2):
            greet(device(line_at(step), row, c))
        return carry

    lax.fori_loop(1, lines, greet_line, 0)

    def half_of(ref, half):
        return ref.at[:, :, pl.ds(pl.multiple_of(half * half_width, half_width), half_width)]

    def own_rows(ref):
        return ref.at[:, pl.ds(pl.multiple_of(core * block, block), block), :]

    small = [
        pltpu.make_async_copy(queries, query_ref, local_sem.at[4]),
        pltpu.make_async_copy(step_keys, step_key_ref, local_sem.at[5]),
        pltpu.make_async_copy(step_values, step_value_ref, local_sem.at[6]),
    ]
    local = [
        pltpu.make_async_copy(half_of(document_keys, core), own_rows(doc_keys), local_sem.at[0]),
        pltpu.make_async_copy(half_of(document_values, core), own_rows(doc_values), local_sem.at[1]),
        pltpu.make_async_copy(sample_keys, key_buf.at[:, pl.ds(0, cache), :], local_sem.at[2]),
        pltpu.make_async_copy(sample_values, value_buf.at[:, pl.ds(0, cache), :], local_sem.at[3]),
    ]
    for copy in small + local:
        copy.start()

    small[0].wait()
    query_pair[...] = jnp.zeros(query_pair.shape, BF16)
    for s in range(samples):
        for g in range(KEY_VALUE_HEADS):
            first = g * GROUP
            part = jnp.concatenate(
                [
                    query_ref[s, :, (first + r) * HEAD_SIZE : (first + r + 1) * HEAD_SIZE].astype(F32)
                    for r in range(GROUP)
                ],
                axis=0,
            ).astype(BF16)
            query_msg[g // HALF, pl.ds((g % HALF) * core_rows + s * rows, rows), :] = part
            side = g % 2
            query_pair[
                g // 2, s, pl.ds(side * rows, rows), pl.ds(side * HEAD_SIZE, HEAD_SIZE)
            ] = part
    tile_row = lax.broadcasted_iota(jnp.int32, (ID_ROWS, HEAD_SIZE), 0)
    tile_lane = lax.broadcasted_iota(jnp.int32, (ID_ROWS, HEAD_SIZE), 1)
    tile_sample = lax.rem(tile_lane, core_rows) // rows
    marks = jnp.zeros((ID_ROWS, HEAD_SIZE), F32)
    for s in range(samples):
        mine = (tile_row == s) | ((tile_row >= samples) & (tile_sample == s))
        marks = jnp.where(mine, id_ref[s].astype(F32), marks)
    for half in range(2):
        query_msg[half, pl.ds(HALF * core_rows, ID_ROWS), :] = marks.astype(BF16)

    pl.semaphore_wait(barrier, 2 * lines + 1)

    def send_query(half, other):
        remote(query_msg.at[half], query_buf.at[me], query_send, query_recv.at[me], other).start()

    for c in range(2):
        send_query(c, device(line, 1 - row, c))

    def send_line(step, carry):
        target = lax.rem(line + lines - step, lines)
        for c in range(2):
            send_query(c, device(target, row, c))
        return carry

    lax.fori_loop(1, lines, send_line, 0)
    send_query(1 - core, partner)
    swaps = [
        remote(half_of(source, 1 - core), own_rows(target), doc_send.at[k], doc_recv.at[k], partner)
        for k, (source, target) in enumerate(
            ((document_keys, doc_keys), (document_values, doc_values))
        )
    ]
    for copy in swaps:
        copy.start()

    query_buf[me] = query_msg[core]
    small[1].wait()
    small[2].wait()
    for s in range(samples):
        for buf, step_ref in ((key_buf, step_key_ref), (value_buf, step_value_ref)):
            buf[s, pl.ds(cache, padded - cache), :] = jnp.zeros(
                (padded - cache, buf.shape[2]), buf.dtype
            )
            buf[s, pl.ds(cache, steps), :] = step_ref[s]
    local[2].wait()
    local[3].wait()

    slot = lax.broadcasted_iota(jnp.int32, (2 * rows, padded), 1)
    now = lax.rem(lax.broadcasted_iota(jnp.int32, (2 * rows, padded), 0), steps)
    fresh = (slot >= cache) & (slot - cache <= now)

    def suffix(pair, carry=0):
        wide = pl.ds(pl.multiple_of(pair * 2 * HEAD_SIZE, 2 * HEAD_SIZE), 2 * HEAD_SIZE)
        for s in range(samples):
            scores = lax.dot_general(
                query_pair[pair, s], key_buf[s, :, wide], NT, preferred_element_type=F32
            )
            scores = jnp.where((slot < len_ref[s]) | fresh, scores, -jnp.inf)
            peak = jnp.max(scores, axis=1, keepdims=True)
            expo = jnp.exp2((scores - peak) * FACTOR)
            total = jnp.sum(expo, axis=1, keepdims=True)
            result = lax.dot_general(
                expo.astype(BF16), value_buf[s, :, wide], NN, preferred_element_type=F32
            )
            for side in range(2):
                part = pl.ds(side * core_rows + s * rows, rows)
                cut = slice(side * rows, (side + 1) * rows)
                suffix_max[pair, part, :] = peak[cut]
                suffix_total[pair, part, :] = total[cut]
                suffix_out[pair, part, :] = result[
                    cut, side * HEAD_SIZE : (side + 1) * HEAD_SIZE
                ]
        return carry

    lax.fori_loop(0, HALF // 2, suffix, 0)

    local[0].wait()
    local[1].wait()
    for copy in swaps:
        copy.wait_recv()
    for h in range(HALF):
        for p in range(prompts):
            value_t[h, pl.ds(p * HEAD_SIZE, HEAD_SIZE), :] = doc_values[
                p, :, h * HEAD_SIZE : (h + 1) * HEAD_SIZE
            ].T

    lane = lax.broadcasted_iota(jnp.int32, (1, chip_rows), 1)

    def relay(step):
        for c in range(2):
            source = device(line_at(step), row, c)
            arrived(query_buf.at[source], query_recv.at[source])
            remote(
                query_buf.at[source],
                query_buf.at[source],
                query_send,
                query_recv.at[source],
                across,
            ).start()

    def attend(step):
        there = line_at(step)
        mine = [device(there, row, c) for c in range(2)]
        theirs = [device(there, 1 - row, c) for c in range(2)]

        @pl.when(step == 0)
        def _():
            arrived(query_buf.at[partner], query_recv.at[partner])

        for source in theirs:
            arrived(query_buf.at[source], query_recv.at[source])
        sources = mine + theirs
        tiles = [
            query_buf[source, pl.ds(HALF * core_rows, ID_ROWS), :].astype(F32)
            for source in sources
        ]
        masks = [
            jnp.concatenate(
                [
                    jnp.broadcast_to(
                        jnp.where(tile[s : s + 1] == p, 1.0, 0.0), (rows, HEAD_SIZE)
                    )
                    for tile in tiles
                    for s in range(samples)
                ],
                axis=0,
            ).astype(BF16)
            for p in range(prompts)
        ]
        marks = jnp.concatenate(
            [
                jnp.where(
                    lane < core_rows,
                    tiles[2 * k][samples : samples + 1],
                    tiles[2 * k + 1][samples : samples + 1],
                )
                for k in range(2)
            ],
            axis=1,
        )
        for pair in range(HALF // 2):
            stats = []
            for h in (2 * pair, 2 * pair + 1):
                query = jnp.concatenate(
                    [query_buf[source, pl.ds(h * core_rows, core_rows), :] for source in sources],
                    axis=0,
                )
                query = jnp.concatenate([query * mask for mask in masks], axis=1)
                cols = slice(h * HEAD_SIZE, (h + 1) * HEAD_SIZE)
                keys = jnp.concatenate([doc_keys[p, :, cols] for p in range(prompts)], axis=1)
                scores = lax.dot_general(keys, query, NT, preferred_element_type=F32)
                peak = jnp.max(scores, axis=0, keepdims=True)
                expo = jnp.exp2((scores - peak) * FACTOR)
                total = jnp.sum(expo, axis=0, keepdims=True)
                both = lax.dot_general(
                    value_t[h], expo.astype(BF16), NN, preferred_element_type=F32
                )
                result = both[:HEAD_SIZE]
                for p in range(1, prompts):
                    result = jnp.where(
                        marks == p, both[p * HEAD_SIZE : (p + 1) * HEAD_SIZE], result
                    )
                own_part[step, h] = result[:, :chip_rows]
                own_stat[step, h, 0:1, :] = peak[:, :chip_rows]
                own_stat[step, h, 1:2, :] = total[:, :chip_rows]
                y_send[step, h], scale = quantize(result[:, chip_rows:])
                stats += [peak[:, chip_rows:], total[:, chip_rows:], scale]
            y_send_stat[step, pair] = jnp.concatenate(
                stats + [jnp.zeros((2, chip_rows), F32)], axis=0
            )
            heads = pl.ds(2 * pair, 2)
            remote(
                y_send.at[step, heads],
                y_got.at[step, heads],
                y_send_sem,
                y_recv.at[step, pair],
                across,
            ).start()
            remote(
                y_send_stat.at[step, pair],
                y_got_stat.at[step, pair],
                y_stat_sem,
                y_stat_recv.at[step, pair],
                across,
            ).start()

    def give(source, target, send, recv, other):
        @pl.when(other != me)
        def _():
            remote(source, target, send, recv, other).start()

        @pl.when(other == me)
        def _():
            pltpu.make_async_copy(source, target, recv).start()

    def combine(step):
        there = line_at(step)
        stats = [[], []]
        for pair in range(HALF // 2):
            arrived(y_got.at[step, pl.ds(2 * pair, 2)], y_recv.at[step, pair])
            arrived(y_got_stat.at[step, pair], y_stat_recv.at[step, pair])
            merged = []
            got = y_got_stat[step, pair]
            for side in range(2):
                h = 2 * pair + side
                peak_a, total_a = own_stat[step, h, 0:1, :], own_stat[step, h, 1:2, :]
                peak_b, total_b, scale_b = (
                    got[3 * side : 3 * side + 1],
                    got[3 * side + 1 : 3 * side + 2],
                    got[3 * side + 2 : 3 * side + 3],
                )
                top = jnp.maximum(peak_a, peak_b)
                weight_a = jnp.exp2((peak_a - top) * FACTOR)
                weight_b = jnp.exp2((peak_b - top) * FACTOR)
                result = own_part[step, h] * weight_a + y_got[step, h].astype(jnp.int32).astype(
                    F32
                ) * (weight_b * (scale_b * (1.0 / LEVELS)))
                merged.append((result, top, total_a * weight_a + total_b * weight_b))
            for c in range(2):
                mixed = []
                for low, high in zip(*merged):
                    wide = jnp.broadcast_to(low, (max(8, low.shape[0]), chip_rows))
                    wide_high = jnp.broadcast_to(high, wide.shape)
                    if c == 0:
                        wide_high = pltpu.roll(wide_high, core_rows, 1)
                    else:
                        wide = pltpu.roll(wide, core_rows, 1)
                    mixed.append(
                        jnp.where(lane < core_rows, wide, wide_high)[: low.shape[0]]
                    )
                result, top, total = mixed
                at = (step * 2 + c) * 2 + pair
                z_send[at], scale = quantize(result)
                stats[c] += [top, total, scale]
                give(
                    z_send.at[at],
                    z_got.at[step, core, pair],
                    z_send_sem,
                    z_recv.at[step, core, pair],
                    device(there, row, c),
                )
        for c in range(2):
            z_send_stat[step * 2 + c] = jnp.concatenate(
                stats[c] + [jnp.zeros((2, chip_rows), F32)], axis=0
            )
            give(
                z_send_stat.at[step * 2 + c],
                z_got_stat.at[step, core],
                z_stat_sem,
                z_stat_recv.at[step, core],
                device(there, row, c),
            )

    def advance(step, carry):
        @pl.when(step + 1 < lines)
        def _():
            relay(step + 1)

        @pl.when((step >= HALF // 2) & (step < HALF))
        def _():
            suffix(step)

        attend(step)

        @pl.when(step >= 1)
        def _():
            combine(step - 1)

        return carry

    lax.fori_loop(0, lines, advance, 0)
    combine(lines - 1)
    lax.fori_loop(min(lines, HALF), HALF, suffix, 0)

    for half in range(2):
        for step in range(lines):
            arrived(z_got_stat.at[step, half], z_stat_recv.at[step, half])
        for pair in range(HALF // 2):
            for step in range(lines):
                arrived(z_got.at[step, half, pair], z_recv.at[step, half, pair])
            tops = [z_got_stat[step, half, 3 * pair : 3 * pair + 1, :] for step in range(lines)]
            top = functools.reduce(jnp.maximum, tops)
            above, below = 0.0, 0.0
            for step in range(lines):
                weight = jnp.exp2((tops[step] - top) * FACTOR)
                below = below + z_got_stat[step, half, 3 * pair + 1 : 3 * pair + 2, :] * weight
                scale = z_got_stat[step, half, 3 * pair + 2 : 3 * pair + 3, :]
                above = above + z_got[step, half, pair].astype(jnp.int32).astype(F32) * (
                    weight * (scale * (1.0 / LEVELS))
                )
            turned = jnp.concatenate([top, below, jnp.zeros((6, chip_rows), F32)], axis=0).T
            peak, total = turned[:, 0:1], turned[:, 1:2]
            at = half * (HALF // 2) + pair
            top = jnp.maximum(peak, suffix_max[at])
            weight = jnp.exp2((peak - top) * FACTOR)
            weight_own = jnp.exp2((suffix_max[at] - top) * FACTOR)
            result = (above.T * weight + suffix_out[at] * weight_own) / (
                total * weight + suffix_total[at] * weight_own
            )
            for side in range(2):
                for s in range(samples):
                    for r in range(GROUP):
                        first = side * core_rows + s * rows + r * steps
                        head = (2 * at + side) * GROUP + r
                        out_ref[s, :, head * HEAD_SIZE : (head + 1) * HEAD_SIZE] = result[
                            first : first + steps
                        ].astype(out_ref.dtype)

    sent = query_buf.at[pl.ds(0, n - 1)]
    pltpu.make_async_copy(sent, sent, query_send).wait()
    pltpu.make_async_copy(y_send, y_send, y_send_sem).wait()
    pltpu.make_async_copy(y_send_stat, y_send_stat, y_stat_sem).wait()
    sent = z_send.at[pl.ds(0, 4 * lines - 2)]
    pltpu.make_async_copy(sent, sent, z_send_sem).wait()
    sent = z_send_stat.at[pl.ds(0, 2 * lines - 1)]
    pltpu.make_async_copy(sent, sent, z_stat_sem).wait()
    for copy in swaps:
        copy.wait_send()


def body(
    queries,
    step_keys,
    step_values,
    sample_keys,
    sample_values,
    suffix_len,
    prompt_id,
    document_keys,
    document_values,
):
    n = lax.axis_size("seq")
    samples, steps = queries.shape[:2]
    cache = sample_keys.shape[1]
    width = KEY_VALUE_HEADS * HEAD_SIZE
    half_width = HALF * HEAD_SIZE
    prompts, block = document_keys.shape[:2]
    rows = steps * GROUP
    core_rows = samples * rows
    chip_rows = 2 * core_rows
    lines = n // 4
    padded = cache + 128
    pairs = HALF // 2
    vmem = pl.BlockSpec(memory_space=pltpu.VMEM)
    smem = pl.BlockSpec(memory_space=pltpu.SMEM)
    hbm = pl.BlockSpec(memory_space=pl.ANY)
    dma = pltpu.SemaphoreType.DMA
    return pl.pallas_call(
        functools.partial(kernel, n),
        out_shape=jax.ShapeDtypeStruct(queries.shape, BF16),
        in_specs=[smem, smem, hbm, hbm, hbm, hbm, hbm, hbm, hbm],
        out_specs=vmem,
        scratch_shapes=[
            pltpu.VMEM(queries.shape, BF16),
            pltpu.VMEM(step_keys.shape, BF16),
            pltpu.VMEM(step_values.shape, BF16),
            pltpu.VMEM((samples, padded, width), BF16),
            pltpu.VMEM((samples, padded, width), BF16),
            pltpu.VMEM((prompts, 2 * block, half_width), BF16),
            pltpu.VMEM((prompts, 2 * block, half_width), BF16),
            pltpu.VMEM((HALF, prompts * HEAD_SIZE, 2 * block), BF16),
            pltpu.VMEM((2, HALF * core_rows + ID_ROWS, HEAD_SIZE), BF16),
            pltpu.VMEM((2 * pairs, samples, 2 * rows, 2 * HEAD_SIZE), BF16),
            pltpu.VMEM((n, HALF * core_rows + ID_ROWS, HEAD_SIZE), BF16),
            pltpu.VMEM((lines, HALF, HEAD_SIZE, chip_rows), F32),
            pltpu.VMEM((lines, HALF, 8, chip_rows), F32),
            pltpu.VMEM((lines, HALF, HEAD_SIZE, chip_rows), I16),
            pltpu.VMEM((lines, pairs, 8, chip_rows), F32),
            pltpu.VMEM((lines, HALF, HEAD_SIZE, chip_rows), I16),
            pltpu.VMEM((lines, pairs, 8, chip_rows), F32),
            pltpu.VMEM((lines * 2 * pairs, HEAD_SIZE, chip_rows), I16),
            pltpu.VMEM((lines * 2, 8, chip_rows), F32),
            pltpu.VMEM((lines, 2, pairs, HEAD_SIZE, chip_rows), I16),
            pltpu.VMEM((lines, 2, 8, chip_rows), F32),
            pltpu.VMEM((2 * pairs, 2 * core_rows, HEAD_SIZE), F32),
            pltpu.VMEM((2 * pairs, 2 * core_rows, 1), F32),
            pltpu.VMEM((2 * pairs, 2 * core_rows, 1), F32),
            dma((7,)),
            dma((2,)),
            dma((2,)),
            dma,
            dma((n,)),
            dma,
            dma,
            dma((lines, pairs)),
            dma((lines, pairs)),
            dma,
            dma,
            dma((lines, 2, pairs)),
            dma((lines, 2)),
        ],
        compiler_params=pltpu.CompilerParams(
            collective_id=0, has_side_effects=True, vmem_limit_bytes=60 << 20
        ),
    )(
        suffix_len,
        prompt_id,
        queries,
        step_keys,
        step_values,
        sample_keys,
        sample_values,
        document_keys,
        document_values,
    )


def solution(mesh):
    return jax.shard_map(
        body,
        mesh=mesh,
        in_specs=(
            P(("groups", "seq"), None, None),
            P(("groups", "seq"), None, None),
            P(("groups", "seq"), None, None),
            P(("groups", "seq"), None, None),
            P(("groups", "seq"), None, None),
            P(("groups", "seq")),
            P(("groups", "seq")),
            P("groups", "seq", None),
            P("groups", "seq", None),
        ),
        out_specs=P(("groups", "seq"), None, None),
        check_vma=False,
    )
```

```python
import functools

import jax
import jax.numpy as jnp
from jax import lax
from jax.experimental import pallas as pl
from jax.experimental.pallas import tpu as pltpu
from jax.sharding import PartitionSpec as P

QUERY_HEADS = 64
KEY_VALUE_HEADS = 8
HEAD_SIZE = 128
HALF = KEY_VALUE_HEADS // 2
GROUP = QUERY_HEADS // KEY_VALUE_HEADS
LOG2E = 1.4426950408889634
FACTOR = (HEAD_SIZE ** (-0.5)) * LOG2E
ID_ROWS = 16
LEVELS = 32767.0
MESH = pl.DeviceIdType.MESH
NT = (((1,), (1,)), ((), ()))
NN = (((1,), (0,)), ((), ()))
F32, BF16, I16 = jnp.float32, jnp.bfloat16, jnp.int16


def quantize(values):
    scale = jnp.maximum(jnp.max(jnp.abs(values), axis=0, keepdims=True), 1e-30)
    return jnp.round(values * (LEVELS / scale)).astype(jnp.int32).astype(I16), scale


def kernel(
    n,
    lengths,
    prompt_id,
    queries,
    step_keys,
    step_values,
    sample_keys,
    sample_values,
    document_keys,
    document_values,
    out_ref,
    len_ref,
    id_ref,
    query_ref,
    step_key_ref,
    step_value_ref,
    key_buf,
    value_buf,
    doc_keys,
    doc_values,
    value_t,
    query_msg,
    query_pair,
    query_buf,
    own_part,
    own_stat,
    y_send,
    y_send_stat,
    y_got,
    y_got_stat,
    z_send,
    z_send_stat,
    z_got,
    z_got_stat,
    suffix_out,
    suffix_max,
    suffix_total,
    local_sem,
    doc_send,
    doc_recv,
    query_send,
    query_recv,
    y_send_sem,
    y_stat_sem,
    y_recv,
    y_stat_recv,
    z_send_sem,
    z_stat_sem,
    z_recv,
    z_stat_recv,
):
    me = lax.axis_index("seq")
    core = lax.rem(me, 2)
    row = lax.rem(lax.div(me, 2), 2)
    line = lax.div(me, 4)
    lines = n // 4
    samples, cache = sample_keys.shape[0], sample_keys.shape[1]
    steps = step_keys.shape[1]
    rows = steps * GROUP
    core_rows = samples * rows
    chip_rows = 2 * core_rows
    prompts, block = document_keys.shape[:2]
    half_width = HALF * HEAD_SIZE
    padded = key_buf.shape[1]

    def device(at_line, at_row, at_core):
        return at_line * 4 + at_row * 2 + at_core

    def line_at(step):
        return lax.rem(line + step, lines)

    def remote(source, target, send, recv, other):
        return pltpu.make_async_remote_copy(
            src_ref=source,
            dst_ref=target,
            send_sem=send,
            recv_sem=recv,
            device_id={"seq": other},
            device_id_type=MESH,
        )

    def arrived(ref, sem):
        pltpu.make_async_copy(ref, ref, sem).wait()

    partner = device(line, row, 1 - core)
    across = device(line, 1 - row, core)

    barrier = pltpu.get_barrier_semaphore()

    def greet(other):
        pl.semaphore_signal(barrier, inc=1, device_id={"seq": other}, device_id_type=MESH)

    greet(partner)
    for c in range(2):
        greet(device(line, 1 - row, c))

    def greet_line(step, carry):
        for c in range(2):
            greet(device(line_at(step), row, c))
        return carry

    lax.fori_loop(1, lines, greet_line, 0)

    def half_of(ref, half):
        return ref.at[:, :, pl.ds(pl.multiple_of(half * half_width, half_width), half_width)]

    def own_rows(ref):
        return ref.at[:, pl.ds(pl.multiple_of(core * block, block), block), :]

    small = [
        pltpu.make_async_copy(queries, query_ref, local_sem.at[4]),
        pltpu.make_async_copy(step_keys, step_key_ref, local_sem.at[5]),
        pltpu.make_async_copy(step_values, step_value_ref, local_sem.at[6]),
        pltpu.make_async_copy(prompt_id, id_ref, local_sem.at[7]),
        pltpu.make_async_copy(lengths, len_ref, local_sem.at[8]),
    ]
    local = [
        pltpu.make_async_copy(half_of(document_keys, core), own_rows(doc_keys), local_sem.at[0]),
        pltpu.make_async_copy(half_of(document_values, core), own_rows(doc_values), local_sem.at[1]),
        pltpu.make_async_copy(sample_keys, key_buf.at[:, pl.ds(0, cache), :], local_sem.at[2]),
        pltpu.make_async_copy(sample_values, value_buf.at[:, pl.ds(0, cache), :], local_sem.at[3]),
    ]
    for copy in small + local:
        copy.start()

    small[0].wait()
    query_pair[...] = jnp.zeros(query_pair.shape, BF16)
    for s in range(samples):
        for g in range(KEY_VALUE_HEADS):
            first = g * GROUP
            part = jnp.concatenate(
                [
                    query_ref[s, :, (first + r) * HEAD_SIZE : (first + r + 1) * HEAD_SIZE].astype(F32)
                    for r in range(GROUP)
                ],
                axis=0,
            ).astype(BF16)
            query_msg[g // HALF, pl.ds((g % HALF) * core_rows + s * rows, rows), :] = part
            side = g % 2
            query_pair[
                g // 2, s, pl.ds(side * rows, rows), pl.ds(side * HEAD_SIZE, HEAD_SIZE)
            ] = part
    small[3].wait()
    tile_row = lax.broadcasted_iota(jnp.int32, (ID_ROWS, HEAD_SIZE), 0)
    tile_lane = lax.broadcasted_iota(jnp.int32, (ID_ROWS, HEAD_SIZE), 1)
    tile_sample = lax.rem(tile_lane, core_rows) // rows
    marks = jnp.zeros((ID_ROWS, HEAD_SIZE), F32)
    for s in range(samples):
        mine = (tile_row == s) | ((tile_row >= samples) & (tile_sample == s))
        marks = jnp.where(mine, id_ref[s].astype(F32), marks)
    for half in range(2):
        query_msg[half, pl.ds(HALF * core_rows, ID_ROWS), :] = marks.astype(BF16)

    pl.semaphore_wait(barrier, 2 * lines + 1)

    def send_query(half, other):
        remote(query_msg.at[half], query_buf.at[me], query_send, query_recv.at[me], other).start()

    for c in range(2):
        send_query(c, device(line, 1 - row, c))

    def send_line(step, carry):
        target = lax.rem(line + lines - step, lines)
        for c in range(2):
            send_query(c, device(target, row, c))
        return carry

    lax.fori_loop(1, lines, send_line, 0)
    send_query(1 - core, partner)
    swaps = [
        remote(half_of(source, 1 - core), own_rows(target), doc_send.at[k], doc_recv.at[k], partner)
        for k, (source, target) in enumerate(
            ((document_keys, doc_keys), (document_values, doc_values))
        )
    ]
    for copy in swaps:
        copy.start()

    query_buf[me] = query_msg[core]
    small[1].wait()
    small[2].wait()
    small[4].wait()
    for s in range(samples):
        for buf, step_ref in ((key_buf, step_key_ref), (value_buf, step_value_ref)):
            buf[s, pl.ds(cache, padded - cache), :] = jnp.zeros(
                (padded - cache, buf.shape[2]), buf.dtype
            )
            buf[s, pl.ds(cache, steps), :] = step_ref[s]
    local[2].wait()
    local[3].wait()

    slot = lax.broadcasted_iota(jnp.int32, (2 * rows, padded), 1)
    now = lax.rem(lax.broadcasted_iota(jnp.int32, (2 * rows, padded), 0), steps)
    fresh = (slot >= cache) & (slot - cache <= now)

    def suffix(pair, carry=0):
        wide = pl.ds(pl.multiple_of(pair * 2 * HEAD_SIZE, 2 * HEAD_SIZE), 2 * HEAD_SIZE)
        for s in range(samples):
            scores = lax.dot_general(
                query_pair[pair, s], key_buf[s, :, wide], NT, preferred_element_type=F32
            )
            scores = jnp.where((slot < len_ref[s]) | fresh, scores, -jnp.inf)
            peak = jnp.max(scores, axis=1, keepdims=True)
            expo = jnp.exp2((scores - peak) * FACTOR)
            total = jnp.sum(expo, axis=1, keepdims=True)
            result = lax.dot_general(
                expo.astype(BF16), value_buf[s, :, wide], NN, preferred_element_type=F32
            )
            for side in range(2):
                part = pl.ds(side * core_rows + s * rows, rows)
                cut = slice(side * rows, (side + 1) * rows)
                suffix_max[pair, part, :] = peak[cut]
                suffix_total[pair, part, :] = total[cut]
                suffix_out[pair, part, :] = result[
                    cut, side * HEAD_SIZE : (side + 1) * HEAD_SIZE
                ]
        return carry

    lax.fori_loop(0, HALF // 2, suffix, 0)

    local[0].wait()
    local[1].wait()
    for copy in swaps:
        copy.wait_recv()
    for h in range(HALF):
        for p in range(prompts):
            value_t[h, pl.ds(p * HEAD_SIZE, HEAD_SIZE), :] = doc_values[
                p, :, h * HEAD_SIZE : (h + 1) * HEAD_SIZE
            ].T

    lane = lax.broadcasted_iota(jnp.int32, (1, chip_rows), 1)

    def relay(step):
        for c in range(2):
            source = device(line_at(step), row, c)
            arrived(query_buf.at[source], query_recv.at[source])
            remote(
                query_buf.at[source],
                query_buf.at[source],
                query_send,
                query_recv.at[source],
                across,
            ).start()

    def attend(step):
        there = line_at(step)
        mine = [device(there, row, c) for c in range(2)]
        theirs = [device(there, 1 - row, c) for c in range(2)]

        @pl.when(step == 0)
        def _():
            arrived(query_buf.at[partner], query_recv.at[partner])

        for source in theirs:
            arrived(query_buf.at[source], query_recv.at[source])
        sources = mine + theirs
        tiles = [
            query_buf[source, pl.ds(HALF * core_rows, ID_ROWS), :].astype(F32)
            for source in sources
        ]
        masks = [
            jnp.concatenate(
                [
                    jnp.broadcast_to(
                        jnp.where(tile[s : s + 1] == p, 1.0, 0.0), (rows, HEAD_SIZE)
                    )
                    for tile in tiles
                    for s in range(samples)
                ],
                axis=0,
            ).astype(BF16)
            for p in range(prompts)
        ]
        marks = jnp.concatenate(
            [
                jnp.where(
                    lane < core_rows,
                    tiles[2 * k][samples : samples + 1],
                    tiles[2 * k + 1][samples : samples + 1],
                )
                for k in range(2)
            ],
            axis=1,
        )
        for pair in range(HALF // 2):
            stats = []
            for h in (2 * pair, 2 * pair + 1):
                query = jnp.concatenate(
                    [query_buf[source, pl.ds(h * core_rows, core_rows), :] for source in sources],
                    axis=0,
                )
                query = jnp.concatenate([query * mask for mask in masks], axis=1)
                cols = slice(h * HEAD_SIZE, (h + 1) * HEAD_SIZE)
                keys = jnp.concatenate([doc_keys[p, :, cols] for p in range(prompts)], axis=1)
                scores = lax.dot_general(keys, query, NT, preferred_element_type=F32)
                peak = jnp.max(scores, axis=0, keepdims=True)
                expo = jnp.exp2((scores - peak) * FACTOR)
                total = jnp.sum(expo, axis=0, keepdims=True)
                both = lax.dot_general(
                    value_t[h], expo.astype(BF16), NN, preferred_element_type=F32
                )
                result = both[:HEAD_SIZE]
                for p in range(1, prompts):
                    result = jnp.where(
                        marks == p, both[p * HEAD_SIZE : (p + 1) * HEAD_SIZE], result
                    )
                own_part[step, h] = result[:, :chip_rows]
                own_stat[step, h, 0:1, :] = peak[:, :chip_rows]
                own_stat[step, h, 1:2, :] = total[:, :chip_rows]
                y_send[step, h], scale = quantize(result[:, chip_rows:])
                stats += [peak[:, chip_rows:], total[:, chip_rows:], scale]
            y_send_stat[step, pair] = jnp.concatenate(
                stats + [jnp.zeros((2, chip_rows), F32)], axis=0
            )
            heads = pl.ds(2 * pair, 2)
            remote(
                y_send.at[step, heads],
                y_got.at[step, heads],
                y_send_sem,
                y_recv.at[step, pair],
                across,
            ).start()
            remote(
                y_send_stat.at[step, pair],
                y_got_stat.at[step, pair],
                y_stat_sem,
                y_stat_recv.at[step, pair],
                across,
            ).start()

    def give(source, target, send, recv, other):
        @pl.when(other != me)
        def _():
            remote(source, target, send, recv, other).start()

        @pl.when(other == me)
        def _():
            pltpu.make_async_copy(source, target, recv).start()

    def combine(step):
        there = line_at(step)
        stats = [[], []]
        for pair in range(HALF // 2):
            arrived(y_got.at[step, pl.ds(2 * pair, 2)], y_recv.at[step, pair])
            arrived(y_got_stat.at[step, pair], y_stat_recv.at[step, pair])
            merged = []
            got = y_got_stat[step, pair]
            for side in range(2):
                h = 2 * pair + side
                peak_a, total_a = own_stat[step, h, 0:1, :], own_stat[step, h, 1:2, :]
                peak_b, total_b, scale_b = (
                    got[3 * side : 3 * side + 1],
                    got[3 * side + 1 : 3 * side + 2],
                    got[3 * side + 2 : 3 * side + 3],
                )
                top = jnp.maximum(peak_a, peak_b)
                weight_a = jnp.exp2((peak_a - top) * FACTOR)
                weight_b = jnp.exp2((peak_b - top) * FACTOR)
                result = own_part[step, h] * weight_a + y_got[step, h].astype(jnp.int32).astype(
                    F32
                ) * (weight_b * (scale_b * (1.0 / LEVELS)))
                merged.append((result, top, total_a * weight_a + total_b * weight_b))
            for c in range(2):
                mixed = []
                for low, high in zip(*merged):
                    wide = jnp.broadcast_to(low, (max(8, low.shape[0]), chip_rows))
                    wide_high = jnp.broadcast_to(high, wide.shape)
                    if c == 0:
                        wide_high = pltpu.roll(wide_high, core_rows, 1)
                    else:
                        wide = pltpu.roll(wide, core_rows, 1)
                    mixed.append(
                        jnp.where(lane < core_rows, wide, wide_high)[: low.shape[0]]
                    )
                result, top, total = mixed
                at = (step * 2 + c) * 2 + pair
                z_send[at], scale = quantize(result)
                stats[c] += [top, total, scale]
                give(
                    z_send.at[at],
                    z_got.at[step, core, pair],
                    z_send_sem,
                    z_recv.at[step, core, pair],
                    device(there, row, c),
                )
        for c in range(2):
            z_send_stat[step * 2 + c] = jnp.concatenate(
                stats[c] + [jnp.zeros((2, chip_rows), F32)], axis=0
            )
            give(
                z_send_stat.at[step * 2 + c],
                z_got_stat.at[step, core],
                z_stat_sem,
                z_stat_recv.at[step, core],
                device(there, row, c),
            )

    def advance(step, carry):
        @pl.when(step + 1 < lines)
        def _():
            relay(step + 1)

        @pl.when((step >= HALF // 2) & (step < HALF))
        def _():
            suffix(step)

        attend(step)

        @pl.when(step >= 1)
        def _():
            combine(step - 1)

        return carry

    lax.fori_loop(0, lines, advance, 0)
    combine(lines - 1)
    lax.fori_loop(min(lines, HALF), HALF, suffix, 0)

    for half in range(2):
        for step in range(lines):
            arrived(z_got_stat.at[step, half], z_stat_recv.at[step, half])
        for pair in range(HALF // 2):
            for step in range(lines):
                arrived(z_got.at[step, half, pair], z_recv.at[step, half, pair])
            tops = [z_got_stat[step, half, 3 * pair : 3 * pair + 1, :] for step in range(lines)]
            top = functools.reduce(jnp.maximum, tops)
            above, below = 0.0, 0.0
            for step in range(lines):
                weight = jnp.exp2((tops[step] - top) * FACTOR)
                below = below + z_got_stat[step, half, 3 * pair + 1 : 3 * pair + 2, :] * weight
                scale = z_got_stat[step, half, 3 * pair + 2 : 3 * pair + 3, :]
                above = above + z_got[step, half, pair].astype(jnp.int32).astype(F32) * (
                    weight * (scale * (1.0 / LEVELS))
                )
            turned = jnp.concatenate([top, below, jnp.zeros((6, chip_rows), F32)], axis=0).T
            peak, total = turned[:, 0:1], turned[:, 1:2]
            at = half * (HALF // 2) + pair
            top = jnp.maximum(peak, suffix_max[at])
            weight = jnp.exp2((peak - top) * FACTOR)
            weight_own = jnp.exp2((suffix_max[at] - top) * FACTOR)
            result = (above.T * weight + suffix_out[at] * weight_own) / (
                total * weight + suffix_total[at] * weight_own
            )
            for side in range(2):
                for s in range(samples):
                    first = side * core_rows + s * rows
                    target = (s * KEY_VALUE_HEADS + 2 * at + side) * rows
                    out_ref[pl.ds(target, rows), :] = result[first : first + rows].astype(
                        out_ref.dtype
                    )

    sent = query_buf.at[pl.ds(0, n - 1)]
    pltpu.make_async_copy(sent, sent, query_send).wait()
    pltpu.make_async_copy(y_send, y_send, y_send_sem).wait()
    pltpu.make_async_copy(y_send_stat, y_send_stat, y_stat_sem).wait()
    sent = z_send.at[pl.ds(0, 4 * lines - 2)]
    pltpu.make_async_copy(sent, sent, z_send_sem).wait()
    sent = z_send_stat.at[pl.ds(0, 2 * lines - 1)]
    pltpu.make_async_copy(sent, sent, z_stat_sem).wait()
    for copy in swaps:
        copy.wait_send()


def body(
    queries,
    step_keys,
    step_values,
    sample_keys,
    sample_values,
    suffix_len,
    prompt_id,
    document_keys,
    document_values,
):
    n = lax.axis_size("seq")
    samples, steps = queries.shape[:2]
    cache = sample_keys.shape[1]
    width = KEY_VALUE_HEADS * HEAD_SIZE
    half_width = HALF * HEAD_SIZE
    prompts, block = document_keys.shape[:2]
    rows = steps * GROUP
    core_rows = samples * rows
    chip_rows = 2 * core_rows
    lines = n // 4
    padded = cache + 128
    pairs = HALF // 2
    vmem = pl.BlockSpec(memory_space=pltpu.VMEM)
    hbm = pl.BlockSpec(memory_space=pl.ANY)
    dma = pltpu.SemaphoreType.DMA
    result = pl.pallas_call(
        functools.partial(kernel, n),
        out_shape=pltpu.VMEM((samples * QUERY_HEADS * steps, HEAD_SIZE), BF16),
        in_specs=[hbm, hbm, hbm, hbm, hbm, hbm, hbm, hbm, hbm],
        out_specs=vmem,
        scratch_shapes=[
            pltpu.SMEM(suffix_len.shape, jnp.int32),
            pltpu.SMEM(prompt_id.shape, jnp.int32),
            pltpu.VMEM(queries.shape, BF16),
            pltpu.VMEM(step_keys.shape, BF16),
            pltpu.VMEM(step_values.shape, BF16),
            pltpu.VMEM((samples, padded, width), BF16),
            pltpu.VMEM((samples, padded, width), BF16),
            pltpu.VMEM((prompts, 2 * block, half_width), BF16),
            pltpu.VMEM((prompts, 2 * block, half_width), BF16),
            pltpu.VMEM((HALF, prompts * HEAD_SIZE, 2 * block), BF16),
            pltpu.VMEM((2, HALF * core_rows + ID_ROWS, HEAD_SIZE), BF16),
            pltpu.VMEM((2 * pairs, samples, 2 * rows, 2 * HEAD_SIZE), BF16),
            pltpu.VMEM((n, HALF * core_rows + ID_ROWS, HEAD_SIZE), BF16),
            pltpu.VMEM((lines, HALF, HEAD_SIZE, chip_rows), F32),
            pltpu.VMEM((lines, HALF, 8, chip_rows), F32),
            pltpu.VMEM((lines, HALF, HEAD_SIZE, chip_rows), I16),
            pltpu.VMEM((lines, pairs, 8, chip_rows), F32),
            pltpu.VMEM((lines, HALF, HEAD_SIZE, chip_rows), I16),
            pltpu.VMEM((lines, pairs, 8, chip_rows), F32),
            pltpu.VMEM((lines * 2 * pairs, HEAD_SIZE, chip_rows), I16),
            pltpu.VMEM((lines * 2, 8, chip_rows), F32),
            pltpu.VMEM((lines, 2, pairs, HEAD_SIZE, chip_rows), I16),
            pltpu.VMEM((lines, 2, 8, chip_rows), F32),
            pltpu.VMEM((2 * pairs, 2 * core_rows, HEAD_SIZE), F32),
            pltpu.VMEM((2 * pairs, 2 * core_rows, 1), F32),
            pltpu.VMEM((2 * pairs, 2 * core_rows, 1), F32),
            dma((9,)),
            dma((2,)),
            dma((2,)),
            dma,
            dma((n,)),
            dma,
            dma,
            dma((lines, pairs)),
            dma((lines, pairs)),
            dma,
            dma,
            dma((lines, 2, pairs)),
            dma((lines, 2)),
        ],
        compiler_params=pltpu.CompilerParams(
            collective_id=0, has_side_effects=True, vmem_limit_bytes=60 << 20
        ),
    )(
        suffix_len,
        prompt_id,
        queries,
        step_keys,
        step_values,
        sample_keys,
        sample_values,
        document_keys,
        document_values,
    )
    return result.reshape(samples, QUERY_HEADS, steps, HEAD_SIZE).transpose(0, 2, 1, 3).reshape(queries.shape)


def solution(mesh):
    return jax.shard_map(
        body,
        mesh=mesh,
        in_specs=(
            P(("groups", "seq"), None, None),
            P(("groups", "seq"), None, None),
            P(("groups", "seq"), None, None),
            P(("groups", "seq"), None, None),
            P(("groups", "seq"), None, None),
            P(("groups", "seq")),
            P(("groups", "seq")),
            P("groups", "seq", None),
            P("groups", "seq", None),
        ),
        out_specs=P(("groups", "seq"), None, None),
        check_vma=False,
    )
```

```python
import functools

import jax
import jax.numpy as jnp
from jax import lax
from jax.experimental import pallas as pl
from jax.experimental.pallas import tpu as pltpu
from jax.sharding import PartitionSpec as P

QUERY_HEADS = 64
KEY_VALUE_HEADS = 8
HEAD_SIZE = 128
HALF = KEY_VALUE_HEADS // 2
GROUP = QUERY_HEADS // KEY_VALUE_HEADS
LOG2E = 1.4426950408889634
FACTOR = (HEAD_SIZE ** (-0.5)) * LOG2E
ID_ROWS = 16
LEVELS = 32767.0
MESH = pl.DeviceIdType.MESH
NT = (((1,), (1,)), ((), ()))
NN = (((1,), (0,)), ((), ()))
F32, BF16, I16 = jnp.float32, jnp.bfloat16, jnp.int16


def quantize(values):
    scale = jnp.maximum(jnp.max(jnp.abs(values), axis=0, keepdims=True), 1e-30)
    return jnp.round(values * (LEVELS / scale)).astype(jnp.int32).astype(I16), scale


def kernel(
    n,
    lengths,
    prompt_id,
    queries,
    step_keys,
    step_values,
    sample_keys,
    sample_values,
    document_keys,
    document_values,
    out_ref,
    len_ref,
    id_ref,
    query_ref,
    step_key_ref,
    step_value_ref,
    key_buf,
    value_buf,
    doc_keys,
    doc_values,
    value_t,
    query_msg,
    query_pair,
    query_buf,
    own_part,
    own_stat,
    y_send,
    y_send_stat,
    y_got,
    y_got_stat,
    z_send,
    z_send_stat,
    z_got,
    z_got_stat,
    sum_part,
    sum_stat,
    suffix_out,
    suffix_max,
    suffix_total,
    local_sem,
    doc_send,
    doc_recv,
    query_send,
    forward_sem,
    query_recv,
    y_send_sem,
    y_stat_sem,
    y_recv,
    y_stat_recv,
    z_send_sem,
    z_stat_sem,
    z_recv,
    z_stat_recv,
):
    me = lax.axis_index("seq")
    core = lax.rem(me, 2)
    row = lax.rem(lax.div(me, 2), 2)
    line = lax.div(me, 4)
    lines = n // 4
    samples, cache = sample_keys.shape[0], sample_keys.shape[1]
    steps = step_keys.shape[1]
    rows = steps * GROUP
    core_rows = samples * rows
    chip_rows = 2 * core_rows
    prompts, block = document_keys.shape[:2]
    half_width = HALF * HEAD_SIZE
    padded = key_buf.shape[1]

    def device(at_line, at_row, at_core):
        return at_line * 4 + at_row * 2 + at_core

    couples = lines // 2
    couple, member = lax.div(line, 2), lax.rem(line, 2)
    mate = line + 1 - 2 * member

    def wraps(turn):
        return lax.div(couple + turn, couples)

    def couple_at(turn):
        return couple + turn - wraps(turn) * couples

    def turn_at(step):
        return lax.div(step, 2)

    def line_at(step):
        turn, second = turn_at(step), lax.rem(step, 2)
        first = wraps(turn) + (1 - jnp.minimum(turn, 1)) * member
        return couple_at(turn) * 2 + first + second - 2 * first * second

    def gateway(turn):
        return (turn >= 1) & (member == 1 - wraps(turn))

    inner = gateway(1)
    upper = wraps(1) == 1

    def remote(source, target, send, recv, other):
        return pltpu.make_async_remote_copy(
            src_ref=source,
            dst_ref=target,
            send_sem=send,
            recv_sem=recv,
            device_id={"seq": other},
            device_id_type=MESH,
        )

    def arrived(ref, sem):
        pltpu.make_async_copy(ref, ref, sem).wait()

    partner = device(line, row, 1 - core)
    across = device(line, 1 - row, core)

    barrier = pltpu.get_barrier_semaphore()

    def greet(other):
        pl.semaphore_signal(barrier, inc=1, device_id={"seq": other}, device_id_type=MESH)

    greet(partner)
    for c in range(2):
        greet(device(line, 1 - row, c))

    def greet_line(step, carry):
        for c in range(2):
            greet(device(lax.rem(line + step, lines), row, c))
        return carry

    lax.fori_loop(1, lines, greet_line, 0)

    def half_of(ref, half):
        return ref.at[:, :, pl.ds(pl.multiple_of(half * half_width, half_width), half_width)]

    def own_rows(ref):
        return ref.at[:, pl.ds(pl.multiple_of(core * block, block), block), :]

    small = [
        pltpu.make_async_copy(queries, query_ref, local_sem.at[4]),
        pltpu.make_async_copy(step_keys, step_key_ref, local_sem.at[5]),
        pltpu.make_async_copy(step_values, step_value_ref, local_sem.at[6]),
        pltpu.make_async_copy(prompt_id, id_ref, local_sem.at[7]),
        pltpu.make_async_copy(lengths, len_ref, local_sem.at[8]),
    ]
    local = [
        pltpu.make_async_copy(half_of(document_keys, core), own_rows(doc_keys), local_sem.at[0]),
        pltpu.make_async_copy(half_of(document_values, core), own_rows(doc_values), local_sem.at[1]),
        pltpu.make_async_copy(sample_keys, key_buf.at[:, pl.ds(0, cache), :], local_sem.at[2]),
        pltpu.make_async_copy(sample_values, value_buf.at[:, pl.ds(0, cache), :], local_sem.at[3]),
    ]
    for copy in small + local:
        copy.start()

    small[0].wait()
    query_pair[...] = jnp.zeros(query_pair.shape, BF16)
    for s in range(samples):
        for g in range(KEY_VALUE_HEADS):
            first = g * GROUP
            part = jnp.concatenate(
                [
                    query_ref[s, :, (first + r) * HEAD_SIZE : (first + r + 1) * HEAD_SIZE].astype(F32)
                    for r in range(GROUP)
                ],
                axis=0,
            ).astype(BF16)
            query_msg[g // HALF, pl.ds((g % HALF) * core_rows + s * rows, rows), :] = part
            side = g % 2
            query_pair[
                g // 2, s, pl.ds(side * rows, rows), pl.ds(side * HEAD_SIZE, HEAD_SIZE)
            ] = part
    small[3].wait()
    tile_row = lax.broadcasted_iota(jnp.int32, (ID_ROWS, HEAD_SIZE), 0)
    tile_lane = lax.broadcasted_iota(jnp.int32, (ID_ROWS, HEAD_SIZE), 1)
    tile_sample = lax.rem(tile_lane, core_rows) // rows
    marks = jnp.zeros((ID_ROWS, HEAD_SIZE), F32)
    for s in range(samples):
        mine = (tile_row == s) | ((tile_row >= samples) & (tile_sample == s))
        marks = jnp.where(mine, id_ref[s].astype(F32), marks)
    for half in range(2):
        query_msg[half, pl.ds(HALF * core_rows, ID_ROWS), :] = marks.astype(BF16)

    pl.semaphore_wait(barrier, 2 * lines + 1)

    def send_query(half, other):
        remote(query_msg.at[half], query_buf.at[me], query_send, query_recv.at[me], other).start()

    for c in range(2):
        send_query(c, device(line, 1 - row, c))

    for c in range(2):
        send_query(c, device(mate, row, c))

    def send_far(turn, carry):
        for c in range(2):
            send_query(c, device(couple_at(turn) * 2 + wraps(turn), row, c))
        return carry

    lax.fori_loop(1, couples, send_far, 0)
    send_query(1 - core, partner)
    swaps = [
        remote(half_of(source, 1 - core), own_rows(target), doc_send.at[k], doc_recv.at[k], partner)
        for k, (source, target) in enumerate(
            ((document_keys, doc_keys), (document_values, doc_values))
        )
    ]
    for copy in swaps:
        copy.start()

    query_buf[me] = query_msg[core]
    small[1].wait()
    small[2].wait()
    small[4].wait()
    for s in range(samples):
        for buf, step_ref in ((key_buf, step_key_ref), (value_buf, step_value_ref)):
            buf[s, pl.ds(cache, padded - cache), :] = jnp.zeros(
                (padded - cache, buf.shape[2]), buf.dtype
            )
            buf[s, pl.ds(cache, steps), :] = step_ref[s]
    local[2].wait()
    local[3].wait()

    slot = lax.broadcasted_iota(jnp.int32, (2 * rows, padded), 1)
    now = lax.rem(lax.broadcasted_iota(jnp.int32, (2 * rows, padded), 0), steps)
    fresh = (slot >= cache) & (slot - cache <= now)

    def suffix(pair, carry=0):
        wide = pl.ds(pl.multiple_of(pair * 2 * HEAD_SIZE, 2 * HEAD_SIZE), 2 * HEAD_SIZE)
        for s in range(samples):
            scores = lax.dot_general(
                query_pair[pair, s], key_buf[s, :, wide], NT, preferred_element_type=F32
            )
            scores = jnp.where((slot < len_ref[s]) | fresh, scores, -jnp.inf)
            peak = jnp.max(scores, axis=1, keepdims=True)
            expo = jnp.exp2((scores - peak) * FACTOR)
            total = jnp.sum(expo, axis=1, keepdims=True)
            result = lax.dot_general(
                expo.astype(BF16), value_buf[s, :, wide], NN, preferred_element_type=F32
            )
            for side in range(2):
                part = pl.ds(side * core_rows + s * rows, rows)
                cut = slice(side * rows, (side + 1) * rows)
                suffix_max[pair, part, :] = peak[cut]
                suffix_total[pair, part, :] = total[cut]
                suffix_out[pair, part, :] = result[
                    cut, side * HEAD_SIZE : (side + 1) * HEAD_SIZE
                ]
        return carry

    lax.fori_loop(0, HALF // 2, suffix, 0)

    local[0].wait()
    local[1].wait()
    for copy in swaps:
        copy.wait_recv()
    for h in range(HALF):
        for p in range(prompts):
            value_t[h, pl.ds(p * HEAD_SIZE, HEAD_SIZE), :] = doc_values[
                p, :, h * HEAD_SIZE : (h + 1) * HEAD_SIZE
            ].T

    lane = lax.broadcasted_iota(jnp.int32, (1, chip_rows), 1)

    def relay(step):
        for c in range(2):
            source = device(line_at(step), row, c)
            arrived(query_buf.at[source], query_recv.at[source])
            turn = turn_at(step)

            @pl.when(gateway(turn))
            def _():
                remote(
                    query_buf.at[source],
                    query_buf.at[source],
                    forward_sem.at[turn],
                    query_recv.at[source],
                    device(mate, row, core),
                ).start()

            remote(
                query_buf.at[source],
                query_buf.at[source],
                query_send,
                query_recv.at[source],
                across,
            ).start()

    def attend(step):
        there = line_at(step)
        mine = [device(there, row, c) for c in range(2)]
        theirs = [device(there, 1 - row, c) for c in range(2)]

        @pl.when(step == 0)
        def _():
            arrived(query_buf.at[partner], query_recv.at[partner])

        for source in theirs:
            arrived(query_buf.at[source], query_recv.at[source])
        sources = mine + theirs
        tiles = [
            query_buf[source, pl.ds(HALF * core_rows, ID_ROWS), :].astype(F32)
            for source in sources
        ]
        masks = [
            jnp.concatenate(
                [
                    jnp.broadcast_to(
                        jnp.where(tile[s : s + 1] == p, 1.0, 0.0), (rows, HEAD_SIZE)
                    )
                    for tile in tiles
                    for s in range(samples)
                ],
                axis=0,
            ).astype(BF16)
            for p in range(prompts)
        ]
        marks = jnp.concatenate(
            [
                jnp.where(
                    lane < core_rows,
                    tiles[2 * k][samples : samples + 1],
                    tiles[2 * k + 1][samples : samples + 1],
                )
                for k in range(2)
            ],
            axis=1,
        )
        for pair in range(HALF // 2):
            stats = []
            for h in (2 * pair, 2 * pair + 1):
                query = jnp.concatenate(
                    [query_buf[source, pl.ds(h * core_rows, core_rows), :] for source in sources],
                    axis=0,
                )
                query = jnp.concatenate([query * mask for mask in masks], axis=1)
                cols = slice(h * HEAD_SIZE, (h + 1) * HEAD_SIZE)
                keys = jnp.concatenate([doc_keys[p, :, cols] for p in range(prompts)], axis=1)
                scores = lax.dot_general(keys, query, NT, preferred_element_type=F32)
                peak = jnp.max(scores, axis=0, keepdims=True)
                expo = jnp.exp2((scores - peak) * FACTOR)
                total = jnp.sum(expo, axis=0, keepdims=True)
                both = lax.dot_general(
                    value_t[h], expo.astype(BF16), NN, preferred_element_type=F32
                )
                result = both[:HEAD_SIZE]
                for p in range(1, prompts):
                    result = jnp.where(
                        marks == p, both[p * HEAD_SIZE : (p + 1) * HEAD_SIZE], result
                    )
                own_part[step, h] = result[:, :chip_rows]
                own_stat[step, h, 0:1, :] = peak[:, :chip_rows]
                own_stat[step, h, 1:2, :] = total[:, :chip_rows]
                y_send[step, h], scale = quantize(result[:, chip_rows:])
                stats += [peak[:, chip_rows:], total[:, chip_rows:], scale]
            y_send_stat[step, pair] = jnp.concatenate(
                stats + [jnp.zeros((2, chip_rows), F32)], axis=0
            )
            heads = pl.ds(2 * pair, 2)
            remote(
                y_send.at[step, heads],
                y_got.at[step, heads],
                y_send_sem,
                y_recv.at[step, pair],
                across,
            ).start()
            remote(
                y_send_stat.at[step, pair],
                y_got_stat.at[step, pair],
                y_stat_sem,
                y_stat_recv.at[step, pair],
                across,
            ).start()

    def give(source, target, send, recv, other):
        @pl.when(other != me)
        def _():
            remote(source, target, send, recv, other).start()

        @pl.when(other == me)
        def _():
            pltpu.make_async_copy(source, target, recv).start()

    def combine(step):
        there = line_at(step)
        place = 2 * turn_at(step) + member
        for pair in range(HALF // 2):
            arrived(y_got.at[step, pl.ds(2 * pair, 2)], y_recv.at[step, pair])
            arrived(y_got_stat.at[step, pair], y_stat_recv.at[step, pair])
            merged = []
            got = y_got_stat[step, pair]
            for side in range(2):
                h = 2 * pair + side
                peak_a, total_a = own_stat[step, h, 0:1, :], own_stat[step, h, 1:2, :]
                peak_b, total_b, scale_b = (
                    got[3 * side : 3 * side + 1],
                    got[3 * side + 1 : 3 * side + 2],
                    got[3 * side + 2 : 3 * side + 3],
                )
                top = jnp.maximum(peak_a, peak_b)
                weight_a = jnp.exp2((peak_a - top) * FACTOR)
                weight_b = jnp.exp2((peak_b - top) * FACTOR)
                result = own_part[step, h] * weight_a + y_got[step, h].astype(jnp.int32).astype(
                    F32
                ) * (weight_b * (scale_b * (1.0 / LEVELS)))
                merged.append((result, top, total_a * weight_a + total_b * weight_b))
            for c in range(2):
                mixed = []
                for low, high in zip(*merged):
                    wide = jnp.broadcast_to(low, (max(8, low.shape[0]), chip_rows))
                    wide_high = jnp.broadcast_to(high, wide.shape)
                    if c == 0:
                        wide_high = pltpu.roll(wide_high, core_rows, 1)
                    else:
                        wide = pltpu.roll(wide, core_rows, 1)
                    mixed.append(
                        jnp.where(lane < core_rows, wide, wide_high)[: low.shape[0]]
                    )
                result, top, total = mixed
                at = (step * 2 + c) * 2 + pair
                z_send[at], scale = quantize(result)
                z_send_stat[at, 0:1, :] = top
                z_send_stat[at, 1:2, :] = total
                z_send_stat[at, 2:3, :] = scale
                give(
                    z_send.at[at],
                    z_got.at[place, core, pair],
                    z_send_sem,
                    z_recv.at[place, core, pair],
                    device(there, row, c),
                )
                give(
                    z_send_stat.at[at],
                    z_got_stat.at[place, core, pair],
                    z_stat_sem,
                    z_stat_recv.at[place, core, pair],
                    device(there, row, c),
                )

    def attend_at(trip):
        outer = jnp.where(upper & (trip >= 2), trip + 1 - 2 * lax.rem(trip, 2), trip + 0)
        return jnp.where(inner, jnp.where(trip <= lines - 3, trip + 2, trip + 2 - lines), outer)

    def relay_at(index):
        outer = index + 1
        return jnp.where(inner, jnp.where(index <= lines - 3, index + 2, 1), outer)

    def advance(trip, carry):
        @pl.when((trip == 0) == inner)
        def _():
            @pl.when(trip <= 1)
            def _():
                relay(relay_at(1))

        @pl.when((trip >= 1) & (trip <= HALF // 2))
        def _():
            suffix(trip + HALF // 2 - 1)

        index = trip + 1 - jnp.where(inner, 1, 0)

        @pl.when((index >= 2) & (index <= lines - 2))
        def _():
            relay(relay_at(index))

        attend(attend_at(trip))

        @pl.when(trip >= 1)
        def _():
            combine(attend_at(trip - 1))

        return carry

    relay(relay_at(0))
    lax.fori_loop(0, lines, advance, 0)
    combine(attend_at(lines - 1))

    last = jnp.where(inner, 2 + member, 1 - member)

    def gather(place, at, half, pair):
        arrived(z_got_stat.at[place, half, pair], z_stat_recv.at[place, half, pair])
        arrived(z_got.at[place, half, pair], z_recv.at[place, half, pair])
        peak = z_got_stat[place, half, pair, 0:1, :]
        total = z_got_stat[place, half, pair, 1:2, :]
        scale = z_got_stat[place, half, pair, 2:3, :]
        before = sum_stat[at, 0:1, :]
        top = jnp.maximum(before, peak)
        old = jnp.exp2((before - top) * FACTOR)
        new = jnp.exp2((peak - top) * FACTOR)
        above = sum_part[at] * old + z_got[place, half, pair].astype(jnp.int32).astype(F32) * (
            new * (scale * (1.0 / LEVELS))
        )
        return above, top, sum_stat[at, 1:2, :] * old + total * new

    def tiles(place, use):
        for pair in range(HALF // 2):
            for half in range(2):
                at = half * (HALF // 2) + pair
                use(at, *gather(place, at, half, pair))

    def keep(at, above, top, total):
        sum_part[at] = above
        sum_stat[at, 0:1, :] = top
        sum_stat[at, 1:2, :] = total

    def finish(at, above, top, total):
        turned = jnp.concatenate([top, total, jnp.zeros((6, chip_rows), F32)], axis=0).T
        peak, total = turned[:, 0:1], turned[:, 1:2]
        top = jnp.maximum(peak, suffix_max[at])
        weight = jnp.exp2((peak - top) * FACTOR)
        weight_own = jnp.exp2((suffix_max[at] - top) * FACTOR)
        result = (above.T * weight + suffix_out[at] * weight_own) / (
            total * weight + suffix_total[at] * weight_own
        )
        for side in range(2):
            for s in range(samples):
                first = side * core_rows + s * rows
                target = (s * KEY_VALUE_HEADS + 2 * at + side) * rows
                out_ref[pl.ds(target, rows), :] = result[first : first + rows].astype(
                    out_ref.dtype
                )

    for at in range(2 * (HALF // 2)):
        keep(
            at,
            jnp.zeros((HEAD_SIZE, chip_rows), F32),
            jnp.full((1, chip_rows), -1e30, F32),
            jnp.zeros((1, chip_rows), F32),
        )

    def add(step, carry):
        tiles(lax.rem(last + 1 + step, lines), keep)
        return carry

    lax.fori_loop(0, lines - 1, add, 0)
    tiles(last, finish)

    sent = query_buf.at[pl.ds(0, 6 * couples + 1)]
    pltpu.make_async_copy(sent, sent, query_send).wait()
    sent = query_buf.at[pl.ds(0, 4)]
    for turn in range(1, couples):

        @pl.when(gateway(turn))
        def _():
            pltpu.make_async_copy(sent, sent, forward_sem.at[turn]).wait()

    pltpu.make_async_copy(y_send, y_send, y_send_sem).wait()
    pltpu.make_async_copy(y_send_stat, y_send_stat, y_stat_sem).wait()
    sent = z_send.at[pl.ds(0, 4 * lines - 2)]
    pltpu.make_async_copy(sent, sent, z_send_sem).wait()
    sent = z_send_stat.at[pl.ds(0, 4 * lines - 2)]
    pltpu.make_async_copy(sent, sent, z_stat_sem).wait()
    for copy in swaps:
        copy.wait_send()


def body(
    queries,
    step_keys,
    step_values,
    sample_keys,
    sample_values,
    suffix_len,
    prompt_id,
    document_keys,
    document_values,
):
    n = lax.axis_size("seq")
    samples, steps = queries.shape[:2]
    cache = sample_keys.shape[1]
    width = KEY_VALUE_HEADS * HEAD_SIZE
    half_width = HALF * HEAD_SIZE
    prompts, block = document_keys.shape[:2]
    rows = steps * GROUP
    core_rows = samples * rows
    chip_rows = 2 * core_rows
    lines = n // 4
    padded = cache + 128
    pairs = HALF // 2
    vmem = pl.BlockSpec(memory_space=pltpu.VMEM)
    hbm = pl.BlockSpec(memory_space=pl.ANY)
    dma = pltpu.SemaphoreType.DMA
    result = pl.pallas_call(
        functools.partial(kernel, n),
        out_shape=pltpu.VMEM((samples * QUERY_HEADS * steps, HEAD_SIZE), BF16),
        in_specs=[hbm, hbm, hbm, hbm, hbm, hbm, hbm, hbm, hbm],
        out_specs=vmem,
        scratch_shapes=[
            pltpu.SMEM(suffix_len.shape, jnp.int32),
            pltpu.SMEM(prompt_id.shape, jnp.int32),
            pltpu.VMEM(queries.shape, BF16),
            pltpu.VMEM(step_keys.shape, BF16),
            pltpu.VMEM(step_values.shape, BF16),
            pltpu.VMEM((samples, padded, width), BF16),
            pltpu.VMEM((samples, padded, width), BF16),
            pltpu.VMEM((prompts, 2 * block, half_width), BF16),
            pltpu.VMEM((prompts, 2 * block, half_width), BF16),
            pltpu.VMEM((HALF, prompts * HEAD_SIZE, 2 * block), BF16),
            pltpu.VMEM((2, HALF * core_rows + ID_ROWS, HEAD_SIZE), BF16),
            pltpu.VMEM((2 * pairs, samples, 2 * rows, 2 * HEAD_SIZE), BF16),
            pltpu.VMEM((n, HALF * core_rows + ID_ROWS, HEAD_SIZE), BF16),
            pltpu.VMEM((lines, HALF, HEAD_SIZE, chip_rows), F32),
            pltpu.VMEM((lines, HALF, 8, chip_rows), F32),
            pltpu.VMEM((lines, HALF, HEAD_SIZE, chip_rows), I16),
            pltpu.VMEM((lines, pairs, 8, chip_rows), F32),
            pltpu.VMEM((lines, HALF, HEAD_SIZE, chip_rows), I16),
            pltpu.VMEM((lines, pairs, 8, chip_rows), F32),
            pltpu.VMEM((lines * 2 * pairs, HEAD_SIZE, chip_rows), I16),
            pltpu.VMEM((lines * 2 * pairs, 4, chip_rows), F32),
            pltpu.VMEM((lines, 2, pairs, HEAD_SIZE, chip_rows), I16),
            pltpu.VMEM((lines, 2, pairs, 4, chip_rows), F32),
            pltpu.VMEM((2 * pairs, HEAD_SIZE, chip_rows), F32),
            pltpu.VMEM((2 * pairs, 8, chip_rows), F32),
            pltpu.VMEM((2 * pairs, 2 * core_rows, HEAD_SIZE), F32),
            pltpu.VMEM((2 * pairs, 2 * core_rows, 1), F32),
            pltpu.VMEM((2 * pairs, 2 * core_rows, 1), F32),
            dma((9,)),
            dma((2,)),
            dma((2,)),
            dma,
            dma((lines // 2,)),
            dma((n,)),
            dma,
            dma,
            dma((lines, pairs)),
            dma((lines, pairs)),
            dma,
            dma,
            dma((lines, 2, pairs)),
            dma((lines, 2, pairs)),
        ],
        compiler_params=pltpu.CompilerParams(
            collective_id=0, has_side_effects=True, vmem_limit_bytes=60 << 20
        ),
    )(
        suffix_len,
        prompt_id,
        queries,
        step_keys,
        step_values,
        sample_keys,
        sample_values,
        document_keys,
        document_values,
    )
    return result.reshape(samples, QUERY_HEADS, steps, HEAD_SIZE).transpose(0, 2, 1, 3).reshape(queries.shape)


def solution(mesh):
    return jax.shard_map(
        body,
        mesh=mesh,
        in_specs=(
            P(("groups", "seq"), None, None),
            P(("groups", "seq"), None, None),
            P(("groups", "seq"), None, None),
            P(("groups", "seq"), None, None),
            P(("groups", "seq"), None, None),
            P(("groups", "seq")),
            P(("groups", "seq")),
            P("groups", "seq", None),
            P("groups", "seq", None),
        ),
        out_specs=P(("groups", "seq"), None, None),
        check_vma=False,
    )
```

```python
import functools

import jax
import jax.numpy as jnp
from jax import lax
from jax.experimental import pallas as pl
from jax.experimental.pallas import tpu as pltpu
from jax.sharding import PartitionSpec as P

QUERY_HEADS = 64
KEY_VALUE_HEADS = 8
HEAD_SIZE = 128
HALF = KEY_VALUE_HEADS // 2
GROUP = QUERY_HEADS // KEY_VALUE_HEADS
LOG2E = 1.4426950408889634
FACTOR = (HEAD_SIZE ** (-0.5)) * LOG2E
LEVELS = 32767.0
MESH = pl.DeviceIdType.MESH
NT = (((1,), (1,)), ((), ()))
NN = (((1,), (0,)), ((), ()))
F32, BF16, I16 = jnp.float32, jnp.bfloat16, jnp.int16


def quantize(values):
    scale = jnp.maximum(jnp.max(jnp.abs(values), axis=0, keepdims=True), 1e-30)
    return jnp.round(values * (LEVELS / scale)).astype(jnp.int32).astype(I16), scale


def kernel(
    n,
    lengths,
    prompt_id,
    queries,
    step_keys,
    step_values,
    sample_keys,
    sample_values,
    document_keys,
    document_values,
    out_ref,
    len_ref,
    id_ref,
    query_ref,
    step_key_ref,
    step_value_ref,
    key_buf,
    value_buf,
    doc_keys,
    doc_values,
    value_t,
    query_msg,
    query_pair,
    query_buf,
    mark_msg,
    mark_buf,
    own_part,
    own_stat,
    y_send,
    y_send_stat,
    y_got,
    y_got_stat,
    z_send,
    z_send_stat,
    z_got,
    z_got_stat,
    sum_part,
    sum_stat,
    suffix_out,
    suffix_max,
    suffix_total,
    local_sem,
    doc_send,
    doc_recv,
    query_send,
    forward_sem,
    query_recv,
    mark_send,
    mark_recv,
    y_send_sem,
    y_stat_sem,
    y_recv,
    y_stat_recv,
    z_send_sem,
    z_stat_sem,
    z_recv,
    z_stat_recv,
):
    me = lax.axis_index("seq")
    core = lax.rem(me, 2)
    row = lax.rem(lax.div(me, 2), 2)
    line = lax.div(me, 4)
    lines = n // 4
    samples, cache = sample_keys.shape[0], sample_keys.shape[1]
    steps = step_keys.shape[1]
    rows = steps * GROUP
    core_rows = samples * rows
    chip_rows = 2 * core_rows
    prompts, block = document_keys.shape[:2]
    half_width = HALF * HEAD_SIZE
    padded = key_buf.shape[1]

    def device(at_line, at_row, at_core):
        return at_line * 4 + at_row * 2 + at_core

    couples = lines // 2
    couple, member = lax.div(line, 2), lax.rem(line, 2)
    mate = line + 1 - 2 * member

    def wraps(turn):
        return lax.div(couple + turn, couples)

    def couple_at(turn):
        return couple + turn - wraps(turn) * couples

    def turn_at(step):
        return lax.div(step, 2)

    def line_at(step):
        turn, second = turn_at(step), lax.rem(step, 2)
        first = wraps(turn) + (1 - jnp.minimum(turn, 1)) * member
        return couple_at(turn) * 2 + first + second - 2 * first * second

    def gateway(turn):
        return (turn >= 1) & (member == 1 - wraps(turn))

    inner = gateway(1)
    upper = wraps(1) == 1

    def remote(source, target, send, recv, other):
        return pltpu.make_async_remote_copy(
            src_ref=source,
            dst_ref=target,
            send_sem=send,
            recv_sem=recv,
            device_id={"seq": other},
            device_id_type=MESH,
        )

    def arrived(ref, sem):
        pltpu.make_async_copy(ref, ref, sem).wait()

    def query_arrived(source):
        arrived(query_buf.at[source], query_recv.at[source])
        arrived(mark_buf.at[source], mark_recv.at[source])

    partner = device(line, row, 1 - core)
    across = device(line, 1 - row, core)

    barrier = pltpu.get_barrier_semaphore()

    def greet(other):
        pl.semaphore_signal(barrier, inc=1, device_id={"seq": other}, device_id_type=MESH)

    greet(partner)
    for c in range(2):
        greet(device(line, 1 - row, c))

    for c in range(2):
        greet(device(mate, row, c))

    def greet_far(turn, carry):
        @pl.when(gateway(turn))
        def _():
            for at in range(2):
                for c in range(2):
                    greet(device(couple_at(turn) * 2 + at, row, c))

        return carry

    lax.fori_loop(1, couples, greet_far, 0)

    def half_of(ref, half):
        return ref.at[:, :, pl.ds(pl.multiple_of(half * half_width, half_width), half_width)]

    def own_rows(ref):
        return ref.at[:, pl.ds(pl.multiple_of(core * block, block), block), :]

    small = [
        pltpu.make_async_copy(queries, query_ref, local_sem.at[4]),
        pltpu.make_async_copy(step_keys, step_key_ref, local_sem.at[5]),
        pltpu.make_async_copy(step_values, step_value_ref, local_sem.at[6]),
        pltpu.make_async_copy(prompt_id, id_ref, local_sem.at[7]),
        pltpu.make_async_copy(lengths, len_ref, local_sem.at[8]),
    ]
    local = [
        pltpu.make_async_copy(half_of(document_keys, core), own_rows(doc_keys), local_sem.at[0]),
        pltpu.make_async_copy(half_of(document_values, core), own_rows(doc_values), local_sem.at[1]),
        pltpu.make_async_copy(sample_keys, key_buf.at[:, pl.ds(0, cache), :], local_sem.at[2]),
        pltpu.make_async_copy(sample_values, value_buf.at[:, pl.ds(0, cache), :], local_sem.at[3]),
    ]
    for copy in small + local:
        copy.start()

    small[0].wait()
    query_pair[...] = jnp.zeros(query_pair.shape, BF16)
    for s in range(samples):
        for g in range(KEY_VALUE_HEADS):
            first = g * GROUP
            part = jnp.concatenate(
                [
                    query_ref[s, :, (first + r) * HEAD_SIZE : (first + r + 1) * HEAD_SIZE].astype(F32)
                    for r in range(GROUP)
                ],
                axis=0,
            ).astype(BF16)
            query_msg[g // HALF, pl.ds((g % HALF) * core_rows + s * rows, rows), :] = part
            side = g % 2
            query_pair[
                g // 2, s, pl.ds(side * rows, rows), pl.ds(side * HEAD_SIZE, HEAD_SIZE)
            ] = part
    small[3].wait()
    mark_lane = lax.rem(lax.broadcasted_iota(jnp.int32, (1, HEAD_SIZE), 1), core_rows) // rows
    marks = jnp.zeros((1, HEAD_SIZE), F32)
    for s in range(samples):
        marks = jnp.where(mark_lane == s, id_ref[s].astype(F32), marks)
    mark_msg[...] = marks

    pl.semaphore_wait(barrier, 2 * couples + 3)

    def send_query(half, other):
        remote(query_msg.at[half], query_buf.at[me], query_send, query_recv.at[me], other).start()
        remote(mark_msg, mark_buf.at[me], mark_send, mark_recv.at[me], other).start()

    for c in range(2):
        send_query(c, device(line, 1 - row, c))

    for c in range(2):
        send_query(c, device(mate, row, c))

    def send_far(turn, carry):
        for c in range(2):
            send_query(c, device(couple_at(turn) * 2 + wraps(turn), row, c))
        return carry

    lax.fori_loop(1, couples, send_far, 0)
    send_query(1 - core, partner)
    swaps = [
        remote(half_of(source, 1 - core), own_rows(target), doc_send.at[k], doc_recv.at[k], partner)
        for k, (source, target) in enumerate(
            ((document_keys, doc_keys), (document_values, doc_values))
        )
    ]
    for copy in swaps:
        copy.start()

    query_buf[me] = query_msg[core]
    mark_buf[me] = marks
    small[1].wait()
    small[2].wait()
    small[4].wait()
    for s in range(samples):
        for buf, step_ref in ((key_buf, step_key_ref), (value_buf, step_value_ref)):
            buf[s, pl.ds(cache, padded - cache), :] = jnp.zeros(
                (padded - cache, buf.shape[2]), buf.dtype
            )
            buf[s, pl.ds(cache, steps), :] = step_ref[s]
    local[2].wait()
    local[3].wait()

    slot = lax.broadcasted_iota(jnp.int32, (2 * rows, padded), 1)
    now = lax.rem(lax.broadcasted_iota(jnp.int32, (2 * rows, padded), 0), steps)
    fresh = (slot >= cache) & (slot - cache <= now)

    def suffix(pair, carry=0):
        wide = pl.ds(pl.multiple_of(pair * 2 * HEAD_SIZE, 2 * HEAD_SIZE), 2 * HEAD_SIZE)
        for s in range(samples):
            scores = lax.dot_general(
                query_pair[pair, s], key_buf[s, :, wide], NT, preferred_element_type=F32
            )
            scores = jnp.where((slot < len_ref[s]) | fresh, scores, -jnp.inf)
            peak = jnp.max(scores, axis=1, keepdims=True)
            expo = jnp.exp2((scores - peak) * FACTOR)
            total = jnp.sum(expo, axis=1, keepdims=True)
            result = lax.dot_general(
                expo.astype(BF16), value_buf[s, :, wide], NN, preferred_element_type=F32
            )
            for side in range(2):
                part = pl.ds(side * core_rows + s * rows, rows)
                cut = slice(side * rows, (side + 1) * rows)
                suffix_max[pair, part, :] = peak[cut]
                suffix_total[pair, part, :] = total[cut]
                suffix_out[pair, part, :] = result[
                    cut, side * HEAD_SIZE : (side + 1) * HEAD_SIZE
                ]
        return carry

    lax.fori_loop(0, HALF // 2, suffix, 0)

    local[0].wait()
    local[1].wait()
    for copy in swaps:
        copy.wait_recv()
    for h in range(HALF):
        for p in range(prompts):
            value_t[h, pl.ds(p * HEAD_SIZE, HEAD_SIZE), :] = doc_values[
                p, :, h * HEAD_SIZE : (h + 1) * HEAD_SIZE
            ].T

    lane = lax.broadcasted_iota(jnp.int32, (1, chip_rows), 1)

    def relay(step):
        for c in range(2):
            source = device(line_at(step), row, c)
            query_arrived(source)
            turn = turn_at(step)

            @pl.when(gateway(turn))
            def _():
                remote(
                    query_buf.at[source],
                    query_buf.at[source],
                    forward_sem.at[0, turn],
                    query_recv.at[source],
                    device(mate, row, core),
                ).start()
                remote(
                    mark_buf.at[source],
                    mark_buf.at[source],
                    forward_sem.at[1, turn],
                    mark_recv.at[source],
                    device(mate, row, core),
                ).start()

            remote(
                query_buf.at[source],
                query_buf.at[source],
                query_send,
                query_recv.at[source],
                across,
            ).start()
            remote(
                mark_buf.at[source],
                mark_buf.at[source],
                mark_send,
                mark_recv.at[source],
                across,
            ).start()

    def attend(step):
        there = line_at(step)
        mine = [device(there, row, c) for c in range(2)]
        theirs = [device(there, 1 - row, c) for c in range(2)]

        @pl.when(step == 0)
        def _():
            query_arrived(partner)

        for source in theirs:
            query_arrived(source)
        sources = mine + theirs
        marked = [mark_buf[source] for source in sources]
        masks = [
            jnp.concatenate(
                [
                    jnp.broadcast_to(
                        jnp.where(mark[:, s * rows : s * rows + 1] == p, 1.0, 0.0),
                        (rows, HEAD_SIZE),
                    )
                    for mark in marked
                    for s in range(samples)
                ],
                axis=0,
            ).astype(BF16)
            for p in range(prompts)
        ]
        marks = jnp.concatenate(
            [
                jnp.where(lane < core_rows, marked[2 * k], marked[2 * k + 1])
                for k in range(2)
            ],
            axis=1,
        )
        for pair in range(HALF // 2):
            stats = []
            for h in (2 * pair, 2 * pair + 1):
                query = jnp.concatenate(
                    [query_buf[source, pl.ds(h * core_rows, core_rows), :] for source in sources],
                    axis=0,
                )
                query = jnp.concatenate([query * mask for mask in masks], axis=1)
                cols = slice(h * HEAD_SIZE, (h + 1) * HEAD_SIZE)
                keys = jnp.concatenate([doc_keys[p, :, cols] for p in range(prompts)], axis=1)
                scores = lax.dot_general(keys, query, NT, preferred_element_type=F32)
                peak = jnp.max(scores, axis=0, keepdims=True)
                expo = jnp.exp2((scores - peak) * FACTOR)
                total = jnp.sum(expo, axis=0, keepdims=True)
                both = lax.dot_general(
                    value_t[h], expo.astype(BF16), NN, preferred_element_type=F32
                )
                result = both[:HEAD_SIZE]
                for p in range(1, prompts):
                    result = jnp.where(
                        marks == p, both[p * HEAD_SIZE : (p + 1) * HEAD_SIZE], result
                    )
                own_part[step, h] = result[:, :chip_rows]
                own_stat[step, h, 0:1, :] = peak[:, :chip_rows]
                own_stat[step, h, 1:2, :] = total[:, :chip_rows]
                y_send[step, h], scale = quantize(result[:, chip_rows:])
                stats += [peak[:, chip_rows:], total[:, chip_rows:], scale]
            for k, stat in enumerate(stats):
                y_send_stat[step, pair, k % 3, k // 3 : k // 3 + 1, :] = stat
            heads = pl.ds(2 * pair, 2)
            remote(
                y_send.at[step, heads],
                y_got.at[step, heads],
                y_send_sem,
                y_recv.at[step, pair],
                across,
            ).start()
            remote(
                y_send_stat.at[step, pair],
                y_got_stat.at[step, pair],
                y_stat_sem,
                y_stat_recv.at[step, pair],
                across,
            ).start()

    def give(source, target, send, recv, other):
        @pl.when(other != me)
        def _():
            remote(source, target, send, recv, other).start()

        @pl.when(other == me)
        def _():
            pltpu.make_async_copy(source, target, recv).start()

    def combine(step):
        there = line_at(step)
        place = 2 * turn_at(step) + member
        for pair in range(HALF // 2):
            arrived(y_got.at[step, pl.ds(2 * pair, 2)], y_recv.at[step, pair])
            arrived(y_got_stat.at[step, pair], y_stat_recv.at[step, pair])
            merged = []
            for side in range(2):
                h = 2 * pair + side
                peak_a, total_a = own_stat[step, h, 0:1, :], own_stat[step, h, 1:2, :]
                peak_b, total_b, scale_b = (
                    y_got_stat[step, pair, k, side : side + 1, :] for k in range(3)
                )
                top = jnp.maximum(peak_a, peak_b)
                weight_a = jnp.exp2((peak_a - top) * FACTOR)
                weight_b = jnp.exp2((peak_b - top) * FACTOR)
                result = own_part[step, h] * weight_a + y_got[step, h].astype(jnp.int32).astype(
                    F32
                ) * (weight_b * (scale_b * (1.0 / LEVELS)))
                merged.append((result, top, total_a * weight_a + total_b * weight_b))
            for c in range(2):
                mixed = []
                for low, high in zip(*merged):
                    wide = jnp.broadcast_to(low, (max(8, low.shape[0]), chip_rows))
                    wide_high = jnp.broadcast_to(high, wide.shape)
                    if c == 0:
                        wide_high = pltpu.roll(wide_high, core_rows, 1)
                    else:
                        wide = pltpu.roll(wide, core_rows, 1)
                    mixed.append(
                        jnp.where(lane < core_rows, wide, wide_high)[: low.shape[0]]
                    )
                result, top, total = mixed
                at = (step * 2 + c) * 2 + pair
                z_send[at], scale = quantize(result)
                z_send_stat[at, 0:1, :] = top
                z_send_stat[at, 1:2, :] = total
                z_send_stat[at, 2:3, :] = scale
                give(
                    z_send.at[at],
                    z_got.at[place, core, pair],
                    z_send_sem,
                    z_recv.at[place, core, pair],
                    device(there, row, c),
                )
                give(
                    z_send_stat.at[at],
                    z_got_stat.at[place, core, pair],
                    z_stat_sem,
                    z_stat_recv.at[place, core, pair],
                    device(there, row, c),
                )

    def attend_at(trip):
        outer = jnp.where(upper & (jnp.where(trip == 0, 0, trip + 1) >= 2) & (trip < lines - 1), trip + 2 - 2 * lax.rem(trip + 1, 2), jnp.where(trip == 0, 0, jnp.where(trip == lines - 1, 1, trip + 1)))
        return jnp.where(inner, jnp.where(trip <= lines - 3, trip + 2, trip + 2 - lines), outer)

    def relay_at(index):
        outer = index + 1
        return jnp.where(inner, jnp.where(index <= lines - 3, index + 2, 1), outer)

    def advance(trip, carry):
        turned = ((trip == 0) == inner) & (trip <= 1)

        @pl.when(turned)
        def _():
            suffix(HALF // 2)

        @pl.when(turned & inner)
        def _():
            suffix(HALF // 2 + 1)

        @pl.when(turned)
        def _():
            relay(relay_at(1))

        @pl.when(turned & jnp.logical_not(inner))
        def _():
            suffix(HALF // 2 + 1)

        index = trip + 1 - jnp.where(inner, 1, 0)

        @pl.when((index >= 2) & (index <= lines - 2))
        def _():
            relay(relay_at(index))

        attend(attend_at(trip))

        @pl.when(trip >= 1)
        def _():
            combine(attend_at(trip - 1))

        return carry

    relay(relay_at(0))
    lax.fori_loop(0, lines, advance, 0)
    combine(attend_at(lines - 1))

    last = jnp.where(inner, 2 + member, 1 - member)

    def gather(place, at, half, pair):
        arrived(z_got_stat.at[place, half, pair], z_stat_recv.at[place, half, pair])
        arrived(z_got.at[place, half, pair], z_recv.at[place, half, pair])
        peak = z_got_stat[place, half, pair, 0:1, :]
        total = z_got_stat[place, half, pair, 1:2, :]
        scale = z_got_stat[place, half, pair, 2:3, :]
        before = sum_stat[at, 0:1, :]
        top = jnp.maximum(before, peak)
        old = jnp.exp2((before - top) * FACTOR)
        new = jnp.exp2((peak - top) * FACTOR)
        above = sum_part[at] * old + z_got[place, half, pair].astype(jnp.int32).astype(F32) * (
            new * (scale * (1.0 / LEVELS))
        )
        return above, top, sum_stat[at, 1:2, :] * old + total * new

    def tiles(place, use):
        for pair in range(HALF // 2):
            for half in range(2):
                at = half * (HALF // 2) + pair
                use(at, *gather(place, at, half, pair))

    def keep(at, above, top, total):
        sum_part[at] = above
        sum_stat[at, 0:1, :] = top
        sum_stat[at, 1:2, :] = total

    def finish(at, above, top, total):
        turned = jnp.concatenate([top, total, jnp.zeros((6, chip_rows), F32)], axis=0).T
        peak, total = turned[:, 0:1], turned[:, 1:2]
        top = jnp.maximum(peak, suffix_max[at])
        weight = jnp.exp2((peak - top) * FACTOR)
        weight_own = jnp.exp2((suffix_max[at] - top) * FACTOR)
        result = (above.T * weight + suffix_out[at] * weight_own) / (
            total * weight + suffix_total[at] * weight_own
        )
        for side in range(2):
            for s in range(samples):
                first = side * core_rows + s * rows
                target = (s * KEY_VALUE_HEADS + 2 * at + side) * rows
                out_ref[pl.ds(target, rows), :] = result[first : first + rows].astype(
                    out_ref.dtype
                )

    for at in range(2 * (HALF // 2)):
        keep(
            at,
            jnp.zeros((HEAD_SIZE, chip_rows), F32),
            jnp.full((1, chip_rows), -1e30, F32),
            jnp.zeros((1, chip_rows), F32),
        )

    def add(step, carry):
        tiles(lax.rem(last + 1 + step, lines), keep)
        return carry

    lax.fori_loop(0, lines - 1, add, 0)
    tiles(last, finish)

    for kind, (buf, sem) in enumerate(((query_buf, query_send), (mark_buf, mark_send))):
        arrived(buf.at[pl.ds(0, 6 * couples + 1)], sem)
        for turn in range(1, couples):

            @pl.when(gateway(turn))
            def _():
                arrived(buf.at[pl.ds(0, 4)], forward_sem.at[kind, turn])

    pltpu.make_async_copy(y_send, y_send, y_send_sem).wait()
    pltpu.make_async_copy(y_send_stat, y_send_stat, y_stat_sem).wait()
    sent = z_send.at[pl.ds(0, 4 * lines - 2)]
    pltpu.make_async_copy(sent, sent, z_send_sem).wait()
    sent = z_send_stat.at[pl.ds(0, 4 * lines - 2)]
    pltpu.make_async_copy(sent, sent, z_stat_sem).wait()
    for copy in swaps:
        copy.wait_send()


def body(
    queries,
    step_keys,
    step_values,
    sample_keys,
    sample_values,
    suffix_len,
    prompt_id,
    document_keys,
    document_values,
):
    n = lax.axis_size("seq")
    samples, steps = queries.shape[:2]
    cache = sample_keys.shape[1]
    width = KEY_VALUE_HEADS * HEAD_SIZE
    half_width = HALF * HEAD_SIZE
    prompts, block = document_keys.shape[:2]
    rows = steps * GROUP
    core_rows = samples * rows
    chip_rows = 2 * core_rows
    lines = n // 4
    padded = cache + 128
    pairs = HALF // 2
    vmem = pl.BlockSpec(memory_space=pltpu.VMEM)
    hbm = pl.BlockSpec(memory_space=pl.ANY)
    dma = pltpu.SemaphoreType.DMA
    result = pl.pallas_call(
        functools.partial(kernel, n),
        out_shape=pltpu.VMEM((samples * QUERY_HEADS * steps, HEAD_SIZE), BF16),
        in_specs=[hbm, hbm, hbm, hbm, hbm, hbm, hbm, hbm, hbm],
        out_specs=vmem,
        scratch_shapes=[
            pltpu.SMEM(suffix_len.shape, jnp.int32),
            pltpu.SMEM(prompt_id.shape, jnp.int32),
            pltpu.VMEM(queries.shape, BF16),
            pltpu.VMEM(step_keys.shape, BF16),
            pltpu.VMEM(step_values.shape, BF16),
            pltpu.VMEM((samples, padded, width), BF16),
            pltpu.VMEM((samples, padded, width), BF16),
            pltpu.VMEM((prompts, 2 * block, half_width), BF16),
            pltpu.VMEM((prompts, 2 * block, half_width), BF16),
            pltpu.VMEM((HALF, prompts * HEAD_SIZE, 2 * block), BF16),
            pltpu.VMEM((2, HALF * core_rows, HEAD_SIZE), BF16),
            pltpu.VMEM((2 * pairs, samples, 2 * rows, 2 * HEAD_SIZE), BF16),
            pltpu.VMEM((n, HALF * core_rows, HEAD_SIZE), BF16),
            pltpu.VMEM((1, HEAD_SIZE), F32),
            pltpu.VMEM((n, 1, HEAD_SIZE), F32),
            pltpu.VMEM((lines, HALF, HEAD_SIZE, chip_rows), F32),
            pltpu.VMEM((lines, HALF, 8, chip_rows), F32),
            pltpu.VMEM((lines, HALF, HEAD_SIZE, chip_rows), I16),
            pltpu.VMEM((lines, pairs, 3, 2, chip_rows), F32),
            pltpu.VMEM((lines, HALF, HEAD_SIZE, chip_rows), I16),
            pltpu.VMEM((lines, pairs, 3, 2, chip_rows), F32),
            pltpu.VMEM((lines * 2 * pairs, HEAD_SIZE, chip_rows), I16),
            pltpu.VMEM((lines * 2 * pairs, 4, chip_rows), F32),
            pltpu.VMEM((lines, 2, pairs, HEAD_SIZE, chip_rows), I16),
            pltpu.VMEM((lines, 2, pairs, 4, chip_rows), F32),
            pltpu.VMEM((2 * pairs, HEAD_SIZE, chip_rows), F32),
            pltpu.VMEM((2 * pairs, 8, chip_rows), F32),
            pltpu.VMEM((2 * pairs, 2 * core_rows, HEAD_SIZE), F32),
            pltpu.VMEM((2 * pairs, 2 * core_rows, 1), F32),
            pltpu.VMEM((2 * pairs, 2 * core_rows, 1), F32),
            dma((9,)),
            dma((2,)),
            dma((2,)),
            dma,
            dma((2, lines // 2)),
            dma((n,)),
            dma,
            dma((n,)),
            dma,
            dma,
            dma((lines, pairs)),
            dma((lines, pairs)),
            dma,
            dma,
            dma((lines, 2, pairs)),
            dma((lines, 2, pairs)),
        ],
        compiler_params=pltpu.CompilerParams(
            collective_id=0, has_side_effects=True, vmem_limit_bytes=60 << 20
        ),
    )(
        suffix_len,
        prompt_id,
        queries,
        step_keys,
        step_values,
        sample_keys,
        sample_values,
        document_keys,
        document_values,
    )
    return result.reshape(samples, QUERY_HEADS, steps, HEAD_SIZE).transpose(0, 2, 1, 3).reshape(queries.shape)


def solution(mesh):
    return jax.shard_map(
        body,
        mesh=mesh,
        in_specs=(
            P(("groups", "seq"), None, None),
            P(("groups", "seq"), None, None),
            P(("groups", "seq"), None, None),
            P(("groups", "seq"), None, None),
            P(("groups", "seq"), None, None),
            P(("groups", "seq")),
            P(("groups", "seq")),
            P("groups", "seq", None),
            P("groups", "seq", None),
        ),
        out_specs=P(("groups", "seq"), None, None),
        check_vma=False,
    )
```

```python
import functools

import jax
import jax.numpy as jnp
from jax import lax
from jax.experimental import pallas as pl
from jax.experimental.pallas import tpu as pltpu
from jax.sharding import PartitionSpec as P

QUERY_HEADS = 64
KEY_VALUE_HEADS = 8
HEAD_SIZE = 128
HALF = KEY_VALUE_HEADS // 2
GROUP = QUERY_HEADS // KEY_VALUE_HEADS
LOG2E = 1.4426950408889634
FACTOR = (HEAD_SIZE ** (-0.5)) * LOG2E
LEVELS = 32767.0
MESH = pl.DeviceIdType.MESH
NT = (((1,), (1,)), ((), ()))
NN = (((1,), (0,)), ((), ()))
F32, BF16, I16 = jnp.float32, jnp.bfloat16, jnp.int16


def quantize(values):
    scale = jnp.maximum(jnp.max(jnp.abs(values), axis=0, keepdims=True), 1e-30)
    return jnp.round(values * (LEVELS / scale)).astype(jnp.int32).astype(I16), scale


def kernel(
    n,
    lengths,
    prompt_id,
    queries,
    step_keys,
    step_values,
    sample_keys,
    sample_values,
    document_keys,
    document_values,
    out_ref,
    len_ref,
    id_ref,
    query_ref,
    step_key_ref,
    step_value_ref,
    key_buf,
    value_buf,
    doc_keys,
    doc_values,
    value_t,
    query_msg,
    query_pair,
    query_buf,
    mark_msg,
    mark_buf,
    own_part,
    own_stat,
    y_send,
    y_send_stat,
    y_got,
    y_got_stat,
    z_send,
    z_send_stat,
    z_got,
    z_got_stat,
    sum_part,
    sum_stat,
    suffix_out,
    suffix_max,
    suffix_total,
    local_sem,
    doc_send,
    doc_recv,
    query_send,
    forward_sem,
    hop_sem,
    query_recv,
    mark_send,
    mark_recv,
    y_send_sem,
    y_stat_sem,
    y_recv,
    y_stat_recv,
    z_send_sem,
    z_stat_sem,
    z_recv,
    z_stat_recv,
):
    me = lax.axis_index("seq")
    core = lax.rem(me, 2)
    row = lax.rem(lax.div(me, 2), 2)
    line = lax.div(me, 4)
    lines = n // 4
    samples, cache = sample_keys.shape[0], sample_keys.shape[1]
    steps = step_keys.shape[1]
    rows = steps * GROUP
    core_rows = samples * rows
    chip_rows = 2 * core_rows
    prompts, block = document_keys.shape[:2]
    half_width = HALF * HEAD_SIZE
    padded = key_buf.shape[1]

    def device(at_line, at_row, at_core):
        return at_line * 4 + at_row * 2 + at_core

    couples = lines // 2
    couple, member = lax.div(line, 2), lax.rem(line, 2)
    mate = line + 1 - 2 * member

    def wraps(turn):
        return lax.div(couple + turn, couples)

    def couple_at(turn):
        return couple + turn - wraps(turn) * couples

    def turn_at(step):
        return lax.div(step, 2)

    def line_at(step):
        turn, second = turn_at(step), lax.rem(step, 2)
        first = wraps(turn) + (1 - jnp.minimum(turn, 1)) * member
        return couple_at(turn) * 2 + first + second - 2 * first * second

    def gateway(turn):
        return (turn >= 1) & (member == 1 - wraps(turn))

    inner = gateway(1)
    upper = wraps(1) == 1

    def remote(source, target, send, recv, other):
        return pltpu.make_async_remote_copy(
            src_ref=source,
            dst_ref=target,
            send_sem=send,
            recv_sem=recv,
            device_id={"seq": other},
            device_id_type=MESH,
        )

    def arrived(ref, sem):
        pltpu.make_async_copy(ref, ref, sem).wait()

    def query_arrived(source, pair):
        if pair == 0:
            arrived(mark_buf.at[source], mark_recv.at[source])
        arrived(query_buf.at[source, pair], query_recv.at[source, pair])

    partner = device(line, row, 1 - core)
    across = device(line, 1 - row, core)

    barrier = pltpu.get_barrier_semaphore()

    def greet(other):
        pl.semaphore_signal(barrier, inc=1, device_id={"seq": other}, device_id_type=MESH)

    greet(partner)
    for c in range(2):
        greet(device(line, 1 - row, c))

    for c in range(2):
        greet(device(mate, row, c))

    def greet_far(turn, carry):
        @pl.when(gateway(turn))
        def _():
            for at in range(2):
                for c in range(2):
                    greet(device(couple_at(turn) * 2 + at, row, c))

        return carry

    lax.fori_loop(1, couples, greet_far, 0)

    def half_of(ref, half):
        return ref.at[:, :, pl.ds(pl.multiple_of(half * half_width, half_width), half_width)]

    def own_rows(ref):
        return ref.at[:, pl.ds(pl.multiple_of(core * block, block), block), :]

    small = [
        pltpu.make_async_copy(queries, query_ref, local_sem.at[4]),
        pltpu.make_async_copy(step_keys, step_key_ref, local_sem.at[5]),
        pltpu.make_async_copy(step_values, step_value_ref, local_sem.at[6]),
        pltpu.make_async_copy(prompt_id, id_ref, local_sem.at[7]),
        pltpu.make_async_copy(lengths, len_ref, local_sem.at[8]),
    ]
    local = [
        pltpu.make_async_copy(half_of(document_keys, core), own_rows(doc_keys), local_sem.at[0]),
        pltpu.make_async_copy(half_of(document_values, core), own_rows(doc_values), local_sem.at[1]),
        pltpu.make_async_copy(sample_keys, key_buf.at[:, pl.ds(0, cache), :], local_sem.at[2]),
        pltpu.make_async_copy(sample_values, value_buf.at[:, pl.ds(0, cache), :], local_sem.at[3]),
    ]
    for copy in small + local:
        copy.start()

    small[0].wait()
    query_pair[...] = jnp.zeros(query_pair.shape, BF16)
    for s in range(samples):
        for g in range(KEY_VALUE_HEADS):
            first = g * GROUP
            part = jnp.concatenate(
                [
                    query_ref[s, :, (first + r) * HEAD_SIZE : (first + r + 1) * HEAD_SIZE].astype(F32)
                    for r in range(GROUP)
                ],
                axis=0,
            ).astype(BF16)
            query_msg[
                g // HALF, (g % HALF) // 2, pl.ds((g % 2) * core_rows + s * rows, rows), :
            ] = part
            side = g % 2
            query_pair[
                g // 2, s, pl.ds(side * rows, rows), pl.ds(side * HEAD_SIZE, HEAD_SIZE)
            ] = part
    small[3].wait()
    mark_lane = lax.rem(lax.broadcasted_iota(jnp.int32, (1, HEAD_SIZE), 1), core_rows) // rows
    marks = jnp.zeros((1, HEAD_SIZE), F32)
    for s in range(samples):
        marks = jnp.where(mark_lane == s, id_ref[s].astype(F32), marks)
    mark_msg[...] = marks

    pl.semaphore_wait(barrier, 2 * couples + 3)

    def send_query(half, pair, other):
        if pair == 0:
            remote(mark_msg, mark_buf.at[me], mark_send, mark_recv.at[me], other).start()
        remote(
            query_msg.at[half, pair],
            query_buf.at[me, pair],
            query_send,
            query_recv.at[me, pair],
            other,
        ).start()

    def send_chip(at_line, at_row):
        for pair in range(HALF // 2):
            for c in range(2):
                send_query(c, pair, device(at_line, at_row, c))

    send_chip(line, 1 - row)
    send_chip(mate, row)

    def send_far(turn, carry):
        send_chip(couple_at(turn) * 2 + wraps(turn), row)
        return carry

    lax.fori_loop(1, couples, send_far, 0)
    for pair in range(HALF // 2):
        send_query(1 - core, pair, partner)
    swaps = [
        remote(half_of(source, 1 - core), own_rows(target), doc_send.at[k], doc_recv.at[k], partner)
        for k, (source, target) in enumerate(
            ((document_keys, doc_keys), (document_values, doc_values))
        )
    ]
    for copy in swaps:
        copy.start()

    query_buf[me] = query_msg[core]
    mark_buf[me] = marks
    small[1].wait()
    small[2].wait()
    small[4].wait()
    for s in range(samples):
        for buf, step_ref in ((key_buf, step_key_ref), (value_buf, step_value_ref)):
            buf[s, pl.ds(cache, padded - cache), :] = jnp.zeros(
                (padded - cache, buf.shape[2]), buf.dtype
            )
            buf[s, pl.ds(cache, steps), :] = step_ref[s]
    local[2].wait()
    local[3].wait()

    slot = lax.broadcasted_iota(jnp.int32, (2 * rows, padded), 1)
    now = lax.rem(lax.broadcasted_iota(jnp.int32, (2 * rows, padded), 0), steps)
    fresh = (slot >= cache) & (slot - cache <= now)

    def suffix(pair, carry=0):
        wide = pl.ds(pl.multiple_of(pair * 2 * HEAD_SIZE, 2 * HEAD_SIZE), 2 * HEAD_SIZE)
        for s in range(samples):
            scores = lax.dot_general(
                query_pair[pair, s], key_buf[s, :, wide], NT, preferred_element_type=F32
            )
            scores = jnp.where((slot < len_ref[s]) | fresh, scores, -jnp.inf)
            peak = jnp.max(scores, axis=1, keepdims=True)
            expo = jnp.exp2((scores - peak) * FACTOR)
            total = jnp.sum(expo, axis=1, keepdims=True)
            result = lax.dot_general(
                expo.astype(BF16), value_buf[s, :, wide], NN, preferred_element_type=F32
            )
            for side in range(2):
                part = pl.ds(side * core_rows + s * rows, rows)
                cut = slice(side * rows, (side + 1) * rows)
                suffix_max[pair, part, :] = peak[cut]
                suffix_total[pair, part, :] = total[cut]
                suffix_out[pair, part, :] = result[
                    cut, side * HEAD_SIZE : (side + 1) * HEAD_SIZE
                ]
        return carry

    lax.fori_loop(0, HALF // 2, suffix, 0)

    local[0].wait()
    local[1].wait()
    for copy in swaps:
        copy.wait_recv()
    for h in range(HALF):
        for p in range(prompts):
            value_t[h, pl.ds(p * HEAD_SIZE, HEAD_SIZE), :] = doc_values[
                p, :, h * HEAD_SIZE : (h + 1) * HEAD_SIZE
            ].T

    lane = lax.broadcasted_iota(jnp.int32, (1, chip_rows), 1)

    def pass_on(source, pair, query_sem, mark_sem, other):
        if pair == 0:
            remote(
                mark_buf.at[source], mark_buf.at[source], mark_sem, mark_recv.at[source], other
            ).start()
        remote(
            query_buf.at[source, pair],
            query_buf.at[source, pair],
            query_sem,
            query_recv.at[source, pair],
            other,
        ).start()

    def is_far(step):
        return (step >= 2) & (lax.rem(step, 2) == 1)

    def relay(step):
        turn = turn_at(step)
        sources = [device(line_at(step), row, c) for c in range(2)]
        for pair in range(HALF // 2):
            for source in sources:
                query_arrived(source, pair)

                @pl.when(gateway(turn))
                def _():
                    pass_on(
                        source,
                        pair,
                        forward_sem.at[0, turn],
                        forward_sem.at[1, turn],
                        device(mate, row, core),
                    )

                @pl.when(jnp.logical_not(is_far(step)))
                def _():
                    pass_on(source, pair, query_send, mark_send, across)

    def hop_out():
        for pair in range(HALF // 2):
            for c in range(2):
                source = device(line, 1 - row, c)
                query_arrived(source, pair)
                for turn in range(1, couples):

                    @pl.when(jnp.logical_not(gateway(turn)))
                    def _():
                        pass_on(
                            source,
                            pair,
                            hop_sem.at[0, turn],
                            hop_sem.at[1, turn],
                            device(couple_at(turn) * 2 + wraps(turn), row, core),
                        )

    def hop_on(step):
        turn = turn_at(step)
        for pair in range(HALF // 2):
            for c in range(2):
                source = device(line_at(step), 1 - row, c)
                query_arrived(source, pair)
                pass_on(
                    source,
                    pair,
                    forward_sem.at[0, turn],
                    forward_sem.at[1, turn],
                    device(mate, row, core),
                )

    def attend(step):
        there = line_at(step)
        mine = [device(there, row, c) for c in range(2)]
        theirs = [device(there, 1 - row, c) for c in range(2)]

        sources = mine + theirs
        hopped = is_far(step) & gateway(turn_at(step))

        @pl.when(hopped)
        def _():
            hop_on(step)

        for pair in range(HALF // 2):

            @pl.when(step == 0)
            def _():
                query_arrived(partner, pair)

            @pl.when((step != 0) & jnp.logical_not(hopped))
            def _():
                for source in theirs:
                    query_arrived(source, pair)

            if pair == 0:
                marked = [mark_buf[source] for source in sources]
                masks = [
                    jnp.concatenate(
                        [
                            jnp.broadcast_to(
                                jnp.where(mark[:, s * rows : s * rows + 1] == p, 1.0, 0.0),
                                (rows, HEAD_SIZE),
                            )
                            for mark in marked
                            for s in range(samples)
                        ],
                        axis=0,
                    ).astype(BF16)
                    for p in range(prompts)
                ]
                marks = jnp.concatenate(
                    [
                        jnp.where(lane < core_rows, marked[2 * k], marked[2 * k + 1])
                        for k in range(2)
                    ],
                    axis=1,
                )
            stats = []
            for h in (2 * pair, 2 * pair + 1):
                query = jnp.concatenate(
                    [
                        query_buf[source, pair, pl.ds((h % 2) * core_rows, core_rows), :]
                        for source in sources
                    ],
                    axis=0,
                )
                query = jnp.concatenate([query * mask for mask in masks], axis=1)
                cols = slice(h * HEAD_SIZE, (h + 1) * HEAD_SIZE)
                keys = jnp.concatenate([doc_keys[p, :, cols] for p in range(prompts)], axis=1)
                scores = lax.dot_general(keys, query, NT, preferred_element_type=F32)
                peak = jnp.max(scores, axis=0, keepdims=True)
                expo = jnp.exp2((scores - peak) * FACTOR)
                total = jnp.sum(expo, axis=0, keepdims=True)
                both = lax.dot_general(
                    value_t[h], expo.astype(BF16), NN, preferred_element_type=F32
                )
                result = both[:HEAD_SIZE]
                for p in range(1, prompts):
                    result = jnp.where(
                        marks == p, both[p * HEAD_SIZE : (p + 1) * HEAD_SIZE], result
                    )
                own_part[step, h] = result[:, :chip_rows]
                own_stat[step, h, 0:1, :] = peak[:, :chip_rows]
                own_stat[step, h, 1:2, :] = total[:, :chip_rows]
                y_send[step, h], scale = quantize(result[:, chip_rows:])
                stats += [peak[:, chip_rows:], total[:, chip_rows:], scale]
            for k, stat in enumerate(stats):
                y_send_stat[step, pair, k % 3, k // 3 : k // 3 + 1, :] = stat
            heads = pl.ds(2 * pair, 2)
            remote(
                y_send.at[step, heads],
                y_got.at[step, heads],
                y_send_sem,
                y_recv.at[step, pair],
                across,
            ).start()
            remote(
                y_send_stat.at[step, pair],
                y_got_stat.at[step, pair],
                y_stat_sem,
                y_stat_recv.at[step, pair],
                across,
            ).start()

    def give(source, target, send, recv, other):
        @pl.when(other != me)
        def _():
            remote(source, target, send, recv, other).start()

        @pl.when(other == me)
        def _():
            pltpu.make_async_copy(source, target, recv).start()

    def combine(step):
        there = line_at(step)
        place = 2 * turn_at(step) + member
        for pair in range(HALF // 2):
            arrived(y_got.at[step, pl.ds(2 * pair, 2)], y_recv.at[step, pair])
            arrived(y_got_stat.at[step, pair], y_stat_recv.at[step, pair])
            merged = []
            for side in range(2):
                h = 2 * pair + side
                peak_a, total_a = own_stat[step, h, 0:1, :], own_stat[step, h, 1:2, :]
                peak_b, total_b, scale_b = (
                    y_got_stat[step, pair, k, side : side + 1, :] for k in range(3)
                )
                top = jnp.maximum(peak_a, peak_b)
                weight_a = jnp.exp2((peak_a - top) * FACTOR)
                weight_b = jnp.exp2((peak_b - top) * FACTOR)
                result = own_part[step, h] * weight_a + y_got[step, h].astype(jnp.int32).astype(
                    F32
                ) * (weight_b * (scale_b * (1.0 / LEVELS)))
                merged.append((result, top, total_a * weight_a + total_b * weight_b))
            for c in range(2):
                mixed = []
                for low, high in zip(*merged):
                    wide = jnp.broadcast_to(low, (max(8, low.shape[0]), chip_rows))
                    wide_high = jnp.broadcast_to(high, wide.shape)
                    if c == 0:
                        wide_high = pltpu.roll(wide_high, core_rows, 1)
                    else:
                        wide = pltpu.roll(wide, core_rows, 1)
                    mixed.append(
                        jnp.where(lane < core_rows, wide, wide_high)[: low.shape[0]]
                    )
                result, top, total = mixed
                at = (step * 2 + c) * 2 + pair
                z_send[at], scale = quantize(result)
                z_send_stat[at, 0:1, :] = top
                z_send_stat[at, 1:2, :] = total
                z_send_stat[at, 2:3, :] = scale
                give(
                    z_send.at[at],
                    z_got.at[place, core, pair],
                    z_send_sem,
                    z_recv.at[place, core, pair],
                    device(there, row, c),
                )
                give(
                    z_send_stat.at[at],
                    z_got_stat.at[place, core, pair],
                    z_stat_sem,
                    z_stat_recv.at[place, core, pair],
                    device(there, row, c),
                )

    far = list(range(2, lines))
    swapped = [step + 1 - 2 * (step % 2) for step in far]

    def pick(order, trip):
        chosen = order[-1]
        for k in range(lines - 1):
            chosen = jnp.where(trip == k, order[k], chosen)
        return chosen

    def attend_at(trip):
        low = jnp.where(inner, pick(far + [0, 1], trip), pick([0] + far + [1], trip))
        high = jnp.where(inner, pick(far + [0, 1], trip), pick([0] + swapped + [1], trip))
        return jnp.where(upper, high, low)

    def relay_at(index):
        outer = index + 1
        return jnp.where(inner, jnp.where(index <= lines - 3, index + 2, 1), outer)

    def advance(trip, carry):
        turned = ((trip == 0) == inner) & (trip <= 1)

        @pl.when(turned)
        def _():
            suffix(HALF // 2)

        @pl.when(turned & inner)
        def _():
            suffix(HALF // 2 + 1)

        @pl.when(turned)
        def _():
            relay(relay_at(1))

        @pl.when(turned & jnp.logical_not(inner))
        def _():
            suffix(HALF // 2 + 1)

        index = trip + 1 - jnp.where(inner, 1, 0)

        @pl.when((index >= 2) & (index <= lines - 2))
        def _():
            relay(relay_at(index))

        attend(attend_at(trip))

        @pl.when(trip >= 1)
        def _():
            combine(attend_at(trip - 1))

        return carry

    relay(relay_at(0))
    hop_out()
    lax.fori_loop(0, lines, advance, 0)
    combine(attend_at(lines - 1))

    last = jnp.where(inner, 2 + member, 1 - member)

    def gather(place, at, half, pair):
        arrived(z_got_stat.at[place, half, pair], z_stat_recv.at[place, half, pair])
        arrived(z_got.at[place, half, pair], z_recv.at[place, half, pair])
        peak = z_got_stat[place, half, pair, 0:1, :]
        total = z_got_stat[place, half, pair, 1:2, :]
        scale = z_got_stat[place, half, pair, 2:3, :]
        before = sum_stat[at, 0:1, :]
        top = jnp.maximum(before, peak)
        old = jnp.exp2((before - top) * FACTOR)
        new = jnp.exp2((peak - top) * FACTOR)
        above = sum_part[at] * old + z_got[place, half, pair].astype(jnp.int32).astype(F32) * (
            new * (scale * (1.0 / LEVELS))
        )
        return above, top, sum_stat[at, 1:2, :] * old + total * new

    def tiles(place, use):
        for pair in range(HALF // 2):
            for half in range(2):
                at = half * (HALF // 2) + pair
                use(at, *gather(place, at, half, pair))

    def keep(at, above, top, total):
        sum_part[at] = above
        sum_stat[at, 0:1, :] = top
        sum_stat[at, 1:2, :] = total

    def finish(at, above, top, total):
        turned = jnp.concatenate([top, total, jnp.zeros((6, chip_rows), F32)], axis=0).T
        peak, total = turned[:, 0:1], turned[:, 1:2]
        top = jnp.maximum(peak, suffix_max[at])
        weight = jnp.exp2((peak - top) * FACTOR)
        weight_own = jnp.exp2((suffix_max[at] - top) * FACTOR)
        result = (above.T * weight + suffix_out[at] * weight_own) / (
            total * weight + suffix_total[at] * weight_own
        )
        for side in range(2):
            for s in range(samples):
                first = side * core_rows + s * rows
                target = (s * KEY_VALUE_HEADS + 2 * at + side) * rows
                out_ref[pl.ds(target, rows), :] = result[first : first + rows].astype(
                    out_ref.dtype
                )

    for at in range(2 * (HALF // 2)):
        keep(
            at,
            jnp.zeros((HEAD_SIZE, chip_rows), F32),
            jnp.full((1, chip_rows), -1e30, F32),
            jnp.zeros((1, chip_rows), F32),
        )

    def add(step, carry):
        tiles(lax.rem(last + 1 + step, lines), keep)
        return carry

    lax.fori_loop(0, lines - 1, add, 0)
    tiles(last, finish)

    for kind, (buf, sem) in enumerate(((query_buf, query_send), (mark_buf, mark_send))):
        arrived(buf.at[pl.ds(0, 4 * couples + 3)], sem)
        for turn in range(1, couples):

            @pl.when(gateway(turn))
            def _():
                arrived(buf.at[pl.ds(0, 6)], forward_sem.at[kind, turn])

            @pl.when(jnp.logical_not(gateway(turn)))
            def _():
                arrived(buf.at[pl.ds(0, 2)], hop_sem.at[kind, turn])

    pltpu.make_async_copy(y_send, y_send, y_send_sem).wait()
    pltpu.make_async_copy(y_send_stat, y_send_stat, y_stat_sem).wait()
    sent = z_send.at[pl.ds(0, 4 * lines - 2)]
    pltpu.make_async_copy(sent, sent, z_send_sem).wait()
    sent = z_send_stat.at[pl.ds(0, 4 * lines - 2)]
    pltpu.make_async_copy(sent, sent, z_stat_sem).wait()
    for copy in swaps:
        copy.wait_send()


def body(
    queries,
    step_keys,
    step_values,
    sample_keys,
    sample_values,
    suffix_len,
    prompt_id,
    document_keys,
    document_values,
):
    n = lax.axis_size("seq")
    samples, steps = queries.shape[:2]
    cache = sample_keys.shape[1]
    width = KEY_VALUE_HEADS * HEAD_SIZE
    half_width = HALF * HEAD_SIZE
    prompts, block = document_keys.shape[:2]
    rows = steps * GROUP
    core_rows = samples * rows
    chip_rows = 2 * core_rows
    lines = n // 4
    padded = cache + 128
    pairs = HALF // 2
    vmem = pl.BlockSpec(memory_space=pltpu.VMEM)
    hbm = pl.BlockSpec(memory_space=pl.ANY)
    dma = pltpu.SemaphoreType.DMA
    result = pl.pallas_call(
        functools.partial(kernel, n),
        out_shape=pltpu.VMEM((samples * QUERY_HEADS * steps, HEAD_SIZE), BF16),
        in_specs=[hbm, hbm, hbm, hbm, hbm, hbm, hbm, hbm, hbm],
        out_specs=vmem,
        scratch_shapes=[
            pltpu.SMEM(suffix_len.shape, jnp.int32),
            pltpu.SMEM(prompt_id.shape, jnp.int32),
            pltpu.VMEM(queries.shape, BF16),
            pltpu.VMEM(step_keys.shape, BF16),
            pltpu.VMEM(step_values.shape, BF16),
            pltpu.VMEM((samples, padded, width), BF16),
            pltpu.VMEM((samples, padded, width), BF16),
            pltpu.VMEM((prompts, 2 * block, half_width), BF16),
            pltpu.VMEM((prompts, 2 * block, half_width), BF16),
            pltpu.VMEM((HALF, prompts * HEAD_SIZE, 2 * block), BF16),
            pltpu.VMEM((2, pairs, 2 * core_rows, HEAD_SIZE), BF16),
            pltpu.VMEM((2 * pairs, samples, 2 * rows, 2 * HEAD_SIZE), BF16),
            pltpu.VMEM((n, pairs, 2 * core_rows, HEAD_SIZE), BF16),
            pltpu.VMEM((1, HEAD_SIZE), F32),
            pltpu.VMEM((n, 1, HEAD_SIZE), F32),
            pltpu.VMEM((lines, HALF, HEAD_SIZE, chip_rows), F32),
            pltpu.VMEM((lines, HALF, 8, chip_rows), F32),
            pltpu.VMEM((lines, HALF, HEAD_SIZE, chip_rows), I16),
            pltpu.VMEM((lines, pairs, 3, 2, chip_rows), F32),
            pltpu.VMEM((lines, HALF, HEAD_SIZE, chip_rows), I16),
            pltpu.VMEM((lines, pairs, 3, 2, chip_rows), F32),
            pltpu.VMEM((lines * 2 * pairs, HEAD_SIZE, chip_rows), I16),
            pltpu.VMEM((lines * 2 * pairs, 4, chip_rows), F32),
            pltpu.VMEM((lines, 2, pairs, HEAD_SIZE, chip_rows), I16),
            pltpu.VMEM((lines, 2, pairs, 4, chip_rows), F32),
            pltpu.VMEM((2 * pairs, HEAD_SIZE, chip_rows), F32),
            pltpu.VMEM((2 * pairs, 8, chip_rows), F32),
            pltpu.VMEM((2 * pairs, 2 * core_rows, HEAD_SIZE), F32),
            pltpu.VMEM((2 * pairs, 2 * core_rows, 1), F32),
            pltpu.VMEM((2 * pairs, 2 * core_rows, 1), F32),
            dma((9,)),
            dma((2,)),
            dma((2,)),
            dma,
            dma((2, lines // 2)),
            dma((2, lines // 2)),
            dma((n, pairs)),
            dma,
            dma((n,)),
            dma,
            dma,
            dma((lines, pairs)),
            dma((lines, pairs)),
            dma,
            dma,
            dma((lines, 2, pairs)),
            dma((lines, 2, pairs)),
        ],
        compiler_params=pltpu.CompilerParams(
            collective_id=0, has_side_effects=True, vmem_limit_bytes=60 << 20
        ),
    )(
        suffix_len,
        prompt_id,
        queries,
        step_keys,
        step_values,
        sample_keys,
        sample_values,
        document_keys,
        document_values,
    )
    return result.reshape(samples, QUERY_HEADS, steps, HEAD_SIZE).transpose(0, 2, 1, 3).reshape(queries.shape)


def solution(mesh):
    return jax.shard_map(
        body,
        mesh=mesh,
        in_specs=(
            P(("groups", "seq"), None, None),
            P(("groups", "seq"), None, None),
            P(("groups", "seq"), None, None),
            P(("groups", "seq"), None, None),
            P(("groups", "seq"), None, None),
            P(("groups", "seq")),
            P(("groups", "seq")),
            P("groups", "seq", None),
            P("groups", "seq", None),
        ),
        out_specs=P(("groups", "seq"), None, None),
        check_vma=False,
    )
```

```python
import functools

import jax
import jax.numpy as jnp
from jax import lax
from jax.experimental import pallas as pl
from jax.experimental.pallas import tpu as pltpu
from jax.sharding import PartitionSpec as P

QUERY_HEADS = 64
KEY_VALUE_HEADS = 8
HEAD_SIZE = 128
HALF = KEY_VALUE_HEADS // 2
GROUP = QUERY_HEADS // KEY_VALUE_HEADS
LOG2E = 1.4426950408889634
FACTOR = (HEAD_SIZE ** (-0.5)) * LOG2E
LEVELS = 32767.0
MESH = pl.DeviceIdType.MESH
NT = (((1,), (1,)), ((), ()))
NN = (((1,), (0,)), ((), ()))
F32, BF16, I16 = jnp.float32, jnp.bfloat16, jnp.int16


def quantize(values):
    scale = jnp.maximum(jnp.max(jnp.abs(values), axis=0, keepdims=True), 1e-30)
    return jnp.round(values * (LEVELS / scale)).astype(jnp.int32).astype(I16), scale


def kernel(
    n,
    lengths,
    prompt_id,
    queries,
    step_keys,
    step_values,
    sample_keys,
    sample_values,
    document_keys,
    document_values,
    out_ref,
    len_ref,
    id_ref,
    query_ref,
    step_key_ref,
    step_value_ref,
    key_buf,
    value_buf,
    doc_keys,
    doc_values,
    value_t,
    query_msg,
    query_pair,
    query_buf,
    mark_msg,
    mark_buf,
    own_part,
    own_stat,
    y_send,
    y_send_stat,
    y_got,
    y_got_stat,
    z_send,
    z_send_stat,
    z_got,
    z_got_stat,
    sum_part,
    sum_stat,
    suffix_out,
    suffix_max,
    suffix_total,
    local_sem,
    doc_send,
    doc_recv,
    query_send,
    forward_sem,
    hop_sem,
    query_recv,
    mark_send,
    mark_recv,
    y_send_sem,
    y_stat_sem,
    y_recv,
    y_stat_recv,
    z_send_sem,
    z_stat_sem,
    z_recv,
    z_stat_recv,
):
    me = lax.axis_index("seq")
    core = lax.rem(me, 2)
    row = lax.rem(lax.div(me, 2), 2)
    line = lax.div(me, 4)
    lines = n // 4
    samples, cache = sample_keys.shape[0], sample_keys.shape[1]
    steps = step_keys.shape[1]
    rows = steps * GROUP
    core_rows = samples * rows
    chip_rows = 2 * core_rows
    prompts, block = document_keys.shape[:2]
    half_width = HALF * HEAD_SIZE
    padded = key_buf.shape[1]

    def device(at_line, at_row, at_core):
        return at_line * 4 + at_row * 2 + at_core

    couples = lines // 2
    couple, member = lax.div(line, 2), lax.rem(line, 2)
    mate = line + 1 - 2 * member

    def wraps(turn):
        return lax.div(couple + turn, couples)

    def couple_at(turn):
        return couple + turn - wraps(turn) * couples

    def turn_at(step):
        return lax.div(step, 2)

    def line_at(step):
        turn, second = turn_at(step), lax.rem(step, 2)
        first = wraps(turn) + (1 - jnp.minimum(turn, 1)) * member
        return couple_at(turn) * 2 + first + second - 2 * first * second

    def gateway(turn):
        return (turn >= 1) & (member == 1 - wraps(turn))

    inner = gateway(1)
    upper = wraps(1) == 1

    def remote(source, target, send, recv, other):
        return pltpu.make_async_remote_copy(
            src_ref=source,
            dst_ref=target,
            send_sem=send,
            recv_sem=recv,
            device_id={"seq": other},
            device_id_type=MESH,
        )

    def arrived(ref, sem):
        pltpu.make_async_copy(ref, ref, sem).wait()

    def query_arrived(source, pair):
        if pair == 0:
            arrived(mark_buf.at[source], mark_recv.at[source])
        arrived(query_buf.at[source, pair], query_recv.at[source, pair])

    partner = device(line, row, 1 - core)
    across = device(line, 1 - row, core)

    barrier = pltpu.get_barrier_semaphore()

    def greet(other):
        pl.semaphore_signal(barrier, inc=1, device_id={"seq": other}, device_id_type=MESH)

    greet(partner)
    for c in range(2):
        greet(device(line, 1 - row, c))

    for c in range(2):
        greet(device(mate, row, c))

    def greet_far(turn, carry):
        @pl.when(gateway(turn))
        def _():
            for at in range(2):
                for c in range(2):
                    greet(device(couple_at(turn) * 2 + at, row, c))

        return carry

    lax.fori_loop(1, couples, greet_far, 0)

    def half_of(ref, half):
        return ref.at[:, :, pl.ds(pl.multiple_of(half * half_width, half_width), half_width)]

    def own_rows(ref):
        return ref.at[:, pl.ds(pl.multiple_of(core * block, block), block), :]

    small = [
        pltpu.make_async_copy(queries, query_ref, local_sem.at[4]),
        pltpu.make_async_copy(step_keys, step_key_ref, local_sem.at[5]),
        pltpu.make_async_copy(step_values, step_value_ref, local_sem.at[6]),
        pltpu.make_async_copy(prompt_id, id_ref, local_sem.at[7]),
        pltpu.make_async_copy(lengths, len_ref, local_sem.at[8]),
    ]
    local = [
        pltpu.make_async_copy(half_of(document_keys, core), own_rows(doc_keys), local_sem.at[0]),
        pltpu.make_async_copy(half_of(document_values, core), own_rows(doc_values), local_sem.at[1]),
        pltpu.make_async_copy(sample_keys, key_buf.at[:, pl.ds(0, cache), :], local_sem.at[2]),
        pltpu.make_async_copy(sample_values, value_buf.at[:, pl.ds(0, cache), :], local_sem.at[3]),
    ]
    for copy in small + local:
        copy.start()

    small[0].wait()
    query_pair[...] = jnp.zeros(query_pair.shape, BF16)
    for s in range(samples):
        for g in range(KEY_VALUE_HEADS):
            first = g * GROUP
            part = jnp.concatenate(
                [
                    query_ref[s, :, (first + r) * HEAD_SIZE : (first + r + 1) * HEAD_SIZE].astype(F32)
                    for r in range(GROUP)
                ],
                axis=0,
            ).astype(BF16)
            query_msg[
                g // HALF, (g % HALF) // 2, pl.ds((g % 2) * core_rows + s * rows, rows), :
            ] = part
            side = g % 2
            query_pair[
                g // 2, s, pl.ds(side * rows, rows), pl.ds(side * HEAD_SIZE, HEAD_SIZE)
            ] = part
    small[3].wait()
    mark_lane = lax.rem(lax.broadcasted_iota(jnp.int32, (1, HEAD_SIZE), 1), core_rows) // rows
    marks = jnp.zeros((1, HEAD_SIZE), F32)
    for s in range(samples):
        marks = jnp.where(mark_lane == s, id_ref[s].astype(F32), marks)
    mark_msg[...] = marks

    pl.semaphore_wait(barrier, 2 * couples + 3)

    def send_query(half, pair, other):
        if pair == 0:
            remote(mark_msg, mark_buf.at[me], mark_send, mark_recv.at[me], other).start()
        remote(
            query_msg.at[half, pair],
            query_buf.at[me, pair],
            query_send,
            query_recv.at[me, pair],
            other,
        ).start()

    def send_chip(at_line, at_row):
        for pair in range(HALF // 2):
            for c in range(2):
                send_query(c, pair, device(at_line, at_row, c))

    send_chip(line, 1 - row)
    send_chip(mate, row)

    def send_far(turn, carry):
        send_chip(couple_at(turn) * 2 + wraps(turn), row)
        return carry

    lax.fori_loop(1, couples, send_far, 0)
    for pair in range(HALF // 2):
        send_query(1 - core, pair, partner)
    swaps = [
        remote(half_of(source, 1 - core), own_rows(target), doc_send.at[k], doc_recv.at[k], partner)
        for k, (source, target) in enumerate(
            ((document_keys, doc_keys), (document_values, doc_values))
        )
    ]
    for copy in swaps:
        copy.start()

    query_buf[me] = query_msg[core]
    mark_buf[me] = marks
    small[1].wait()
    small[2].wait()
    small[4].wait()
    for s in range(samples):
        for buf, step_ref in ((key_buf, step_key_ref), (value_buf, step_value_ref)):
            buf[s, pl.ds(cache, padded - cache), :] = jnp.zeros(
                (padded - cache, buf.shape[2]), buf.dtype
            )
            buf[s, pl.ds(cache, steps), :] = step_ref[s]
    local[2].wait()
    local[3].wait()

    slot = lax.broadcasted_iota(jnp.int32, (2 * rows, padded), 1)
    now = lax.rem(lax.broadcasted_iota(jnp.int32, (2 * rows, padded), 0), steps)
    fresh = (slot >= cache) & (slot - cache <= now)

    def suffix(pair, carry=0):
        wide = pl.ds(pl.multiple_of(pair * 2 * HEAD_SIZE, 2 * HEAD_SIZE), 2 * HEAD_SIZE)
        for s in range(samples):
            scores = lax.dot_general(
                query_pair[pair, s], key_buf[s, :, wide], NT, preferred_element_type=F32
            )
            scores = jnp.where((slot < len_ref[s]) | fresh, scores, -jnp.inf)
            peak = jnp.max(scores, axis=1, keepdims=True)
            expo = jnp.exp2((scores - peak) * FACTOR)
            total = jnp.sum(expo, axis=1, keepdims=True)
            result = lax.dot_general(
                expo.astype(BF16), value_buf[s, :, wide], NN, preferred_element_type=F32
            )
            for side in range(2):
                part = pl.ds(side * core_rows + s * rows, rows)
                cut = slice(side * rows, (side + 1) * rows)
                suffix_max[pair, part, :] = peak[cut]
                suffix_total[pair, part, :] = total[cut]
                suffix_out[pair, part, :] = result[
                    cut, side * HEAD_SIZE : (side + 1) * HEAD_SIZE
                ]
        return carry

    lax.fori_loop(0, HALF // 2, suffix, 0)

    local[0].wait()
    local[1].wait()
    for copy in swaps:
        copy.wait_recv()
    for h in range(HALF):
        for p in range(prompts):
            value_t[h, pl.ds(p * HEAD_SIZE, HEAD_SIZE), :] = doc_values[
                p, :, h * HEAD_SIZE : (h + 1) * HEAD_SIZE
            ].T

    lane = lax.broadcasted_iota(jnp.int32, (1, chip_rows), 1)

    def pass_on(source, pair, query_sem, mark_sem, other):
        if pair == 0:
            remote(
                mark_buf.at[source], mark_buf.at[source], mark_sem, mark_recv.at[source], other
            ).start()
        remote(
            query_buf.at[source, pair],
            query_buf.at[source, pair],
            query_sem,
            query_recv.at[source, pair],
            other,
        ).start()

    def is_far(step):
        return (step >= 2) & (lax.rem(step, 2) == 1)

    def relay(step):
        turn = turn_at(step)
        sources = [device(line_at(step), row, c) for c in range(2)]
        for pair in range(HALF // 2):
            for source in sources:
                query_arrived(source, pair)

                @pl.when(gateway(turn))
                def _():
                    pass_on(
                        source,
                        pair,
                        forward_sem.at[0, turn],
                        forward_sem.at[1, turn],
                        device(mate, row, core),
                    )

                @pl.when(jnp.logical_not(is_far(step)))
                def _():
                    pass_on(source, pair, query_send, mark_send, across)

    def hop_out():
        for pair in range(HALF // 2):
            for c in range(2):
                source = device(line, 1 - row, c)
                query_arrived(source, pair)
                for turn in range(1, couples):

                    @pl.when(jnp.logical_not(gateway(turn)))
                    def _():
                        pass_on(
                            source,
                            pair,
                            hop_sem.at[0, turn],
                            hop_sem.at[1, turn],
                            device(couple_at(turn) * 2 + wraps(turn), row, core),
                        )

    def hop_on(step):
        turn = turn_at(step)
        for pair in range(HALF // 2):
            for c in range(2):
                source = device(line_at(step), 1 - row, c)
                query_arrived(source, pair)
                pass_on(
                    source,
                    pair,
                    forward_sem.at[0, turn],
                    forward_sem.at[1, turn],
                    device(mate, row, core),
                )

    def attend(step):
        there = line_at(step)
        mine = [device(there, row, c) for c in range(2)]
        theirs = [device(there, 1 - row, c) for c in range(2)]

        sources = mine + theirs
        hopped = is_far(step) & gateway(turn_at(step))

        @pl.when(hopped)
        def _():
            hop_on(step)

        for pair in range(HALF // 2):

            @pl.when(step == 0)
            def _():
                query_arrived(partner, pair)

            @pl.when((step != 0) & jnp.logical_not(hopped))
            def _():
                for source in theirs:
                    query_arrived(source, pair)

            if pair == 0:
                marked = [mark_buf[source] for source in sources]
                masks = [
                    jnp.concatenate(
                        [
                            jnp.broadcast_to(
                                jnp.where(mark[:, s * rows : s * rows + 1] == p, 1.0, 0.0),
                                (rows, HEAD_SIZE),
                            )
                            for mark in marked
                            for s in range(samples)
                        ],
                        axis=0,
                    ).astype(BF16)
                    for p in range(prompts)
                ]
                marks = jnp.concatenate(
                    [
                        jnp.where(lane < core_rows, marked[2 * k], marked[2 * k + 1])
                        for k in range(2)
                    ],
                    axis=1,
                )
            stats = []
            for h in (2 * pair, 2 * pair + 1):
                query = jnp.concatenate(
                    [
                        query_buf[source, pair, pl.ds((h % 2) * core_rows, core_rows), :]
                        for source in sources
                    ],
                    axis=0,
                )
                query = jnp.concatenate([query * mask for mask in masks], axis=1)
                cols = slice(h * HEAD_SIZE, (h + 1) * HEAD_SIZE)
                keys = jnp.concatenate([doc_keys[p, :, cols] for p in range(prompts)], axis=1)
                scores = lax.dot_general(keys, query, NT, preferred_element_type=F32)
                peak = jnp.max(scores, axis=0, keepdims=True)
                expo = jnp.exp2((scores - peak) * FACTOR)
                total = jnp.sum(expo, axis=0, keepdims=True)
                both = lax.dot_general(
                    value_t[h], expo.astype(BF16), NN, preferred_element_type=F32
                )
                result = both[:HEAD_SIZE]
                for p in range(1, prompts):
                    result = jnp.where(
                        marks == p, both[p * HEAD_SIZE : (p + 1) * HEAD_SIZE], result
                    )
                own_part[step, h] = result[:, :chip_rows]
                own_stat[step, h, 0:1, :] = peak[:, :chip_rows]
                own_stat[step, h, 1:2, :] = total[:, :chip_rows]
                y_send[step, h], scale = quantize(result[:, chip_rows:])
                stats += [peak[:, chip_rows:], total[:, chip_rows:], scale]
            for k, stat in enumerate(stats):
                y_send_stat[step, pair, k % 3, k // 3 : k // 3 + 1, :] = stat
            heads = pl.ds(2 * pair, 2)
            remote(
                y_send.at[step, heads],
                y_got.at[step, heads],
                y_send_sem,
                y_recv.at[step, pair],
                across,
            ).start()
            remote(
                y_send_stat.at[step, pair],
                y_got_stat.at[step, pair],
                y_stat_sem,
                y_stat_recv.at[step, pair],
                across,
            ).start()

    def give(source, target, send, recv, other):
        @pl.when(other != me)
        def _():
            remote(source, target, send, recv, other).start()

        @pl.when(other == me)
        def _():
            pltpu.make_async_copy(source, target, recv).start()

    def combine(step):
        there = line_at(step)
        place = 2 * turn_at(step) + member
        for pair in range(HALF // 2):
            arrived(y_got.at[step, pl.ds(2 * pair, 2)], y_recv.at[step, pair])
            arrived(y_got_stat.at[step, pair], y_stat_recv.at[step, pair])
            merged = []
            for side in range(2):
                h = 2 * pair + side
                peak_a, total_a = own_stat[step, h, 0:1, :], own_stat[step, h, 1:2, :]
                peak_b, total_b, scale_b = (
                    y_got_stat[step, pair, k, side : side + 1, :] for k in range(3)
                )
                top = jnp.maximum(peak_a, peak_b)
                weight_a = jnp.exp2((peak_a - top) * FACTOR)
                weight_b = jnp.exp2((peak_b - top) * FACTOR)
                result = own_part[step, h] * weight_a + y_got[step, h].astype(jnp.int32).astype(
                    F32
                ) * (weight_b * (scale_b * (1.0 / LEVELS)))
                merged.append((result, top, total_a * weight_a + total_b * weight_b))
            for c in range(2):
                mixed = []
                for low, high in zip(*merged):
                    wide = jnp.broadcast_to(low, (max(8, low.shape[0]), chip_rows))
                    wide_high = jnp.broadcast_to(high, wide.shape)
                    if c == 0:
                        wide_high = pltpu.roll(wide_high, core_rows, 1)
                    else:
                        wide = pltpu.roll(wide, core_rows, 1)
                    mixed.append(
                        jnp.where(lane < core_rows, wide, wide_high)[: low.shape[0]]
                    )
                result, top, total = mixed
                at = (step * 2 + c) * 2 + pair
                z_send[at], scale = quantize(result)
                z_send_stat[at, 0:1, :] = top
                z_send_stat[at, 1:2, :] = total
                z_send_stat[at, 2:3, :] = scale
                give(
                    z_send.at[at],
                    z_got.at[place, core, pair],
                    z_send_sem,
                    z_recv.at[place, core, pair],
                    device(there, row, c),
                )
                give(
                    z_send_stat.at[at],
                    z_got_stat.at[place, core, pair],
                    z_stat_sem,
                    z_stat_recv.at[place, core, pair],
                    device(there, row, c),
                )

    far = list(range(2, lines))
    swapped = [step + 1 - 2 * (step % 2) for step in far]

    def pick(order, trip):
        chosen = order[-1]
        for k in range(lines - 1):
            chosen = jnp.where(trip == k, order[k], chosen)
        return chosen

    def attend_at(trip):
        low = jnp.where(inner, pick(far + [1, 0], trip), pick([0, 1] + far, trip))
        high = jnp.where(inner, pick(far + [1, 0], trip), pick([0] + swapped[:1] + [1] + swapped[1:], trip))
        return jnp.where(upper, high, low)

    def relay_at(index):
        within = jnp.where(index == 0, 2, jnp.where(index == 1, 1, index + 1))
        return jnp.where(inner, within, index + 1)

    def advance(trip, carry):
        turned = ((trip == 0) == inner) & (trip <= 1)

        @pl.when(turned)
        def _():
            suffix(HALF // 2)

        @pl.when(turned & inner)
        def _():
            suffix(HALF // 2 + 1)

        @pl.when(turned)
        def _():
            relay(relay_at(1))

        @pl.when(turned & jnp.logical_not(inner))
        def _():
            suffix(HALF // 2 + 1)

        index = jnp.where(inner, trip + 2, jnp.where(upper & (trip >= 1), trip + 1, trip))

        @pl.when((index >= 2) & (index <= lines - 2))
        def _():
            relay(relay_at(index))

        attend(attend_at(trip))

        @pl.when(trip >= 1)
        def _():
            combine(attend_at(trip - 1))

        return carry

    relay(relay_at(0))
    hop_out()
    lax.fori_loop(0, lines, advance, 0)
    combine(attend_at(lines - 1))

    last = jnp.where(inner, 2 + member, 1 - member)

    def gather(place, at, half, pair):
        arrived(z_got_stat.at[place, half, pair], z_stat_recv.at[place, half, pair])
        arrived(z_got.at[place, half, pair], z_recv.at[place, half, pair])
        peak = z_got_stat[place, half, pair, 0:1, :]
        total = z_got_stat[place, half, pair, 1:2, :]
        scale = z_got_stat[place, half, pair, 2:3, :]
        before = sum_stat[at, 0:1, :]
        top = jnp.maximum(before, peak)
        old = jnp.exp2((before - top) * FACTOR)
        new = jnp.exp2((peak - top) * FACTOR)
        above = sum_part[at] * old + z_got[place, half, pair].astype(jnp.int32).astype(F32) * (
            new * (scale * (1.0 / LEVELS))
        )
        return above, top, sum_stat[at, 1:2, :] * old + total * new

    def tiles(place, use):
        for pair in range(HALF // 2):
            for half in range(2):
                at = half * (HALF // 2) + pair
                use(at, *gather(place, at, half, pair))

    def keep(at, above, top, total):
        sum_part[at] = above
        sum_stat[at, 0:1, :] = top
        sum_stat[at, 1:2, :] = total

    def finish(at, above, top, total):
        turned = jnp.concatenate([top, total, jnp.zeros((6, chip_rows), F32)], axis=0).T
        peak, total = turned[:, 0:1], turned[:, 1:2]
        top = jnp.maximum(peak, suffix_max[at])
        weight = jnp.exp2((peak - top) * FACTOR)
        weight_own = jnp.exp2((suffix_max[at] - top) * FACTOR)
        result = (above.T * weight + suffix_out[at] * weight_own) / (
            total * weight + suffix_total[at] * weight_own
        )
        for side in range(2):
            for s in range(samples):
                first = side * core_rows + s * rows
                target = (s * KEY_VALUE_HEADS + 2 * at + side) * rows
                out_ref[pl.ds(target, rows), :] = result[first : first + rows].astype(
                    out_ref.dtype
                )

    for at in range(2 * (HALF // 2)):
        keep(
            at,
            jnp.zeros((HEAD_SIZE, chip_rows), F32),
            jnp.full((1, chip_rows), -1e30, F32),
            jnp.zeros((1, chip_rows), F32),
        )

    def add(step, carry):
        tiles(lax.rem(last + 1 + step, lines), keep)
        return carry

    lax.fori_loop(0, lines - 1, add, 0)
    tiles(last, finish)

    for kind, (buf, sem) in enumerate(((query_buf, query_send), (mark_buf, mark_send))):
        arrived(buf.at[pl.ds(0, 4 * couples + 3)], sem)
        for turn in range(1, couples):

            @pl.when(gateway(turn))
            def _():
                arrived(buf.at[pl.ds(0, 6)], forward_sem.at[kind, turn])

            @pl.when(jnp.logical_not(gateway(turn)))
            def _():
                arrived(buf.at[pl.ds(0, 2)], hop_sem.at[kind, turn])

    pltpu.make_async_copy(y_send, y_send, y_send_sem).wait()
    pltpu.make_async_copy(y_send_stat, y_send_stat, y_stat_sem).wait()
    sent = z_send.at[pl.ds(0, 4 * lines - 2)]
    pltpu.make_async_copy(sent, sent, z_send_sem).wait()
    sent = z_send_stat.at[pl.ds(0, 4 * lines - 2)]
    pltpu.make_async_copy(sent, sent, z_stat_sem).wait()
    for copy in swaps:
        copy.wait_send()


def body(
    queries,
    step_keys,
    step_values,
    sample_keys,
    sample_values,
    suffix_len,
    prompt_id,
    document_keys,
    document_values,
):
    n = lax.axis_size("seq")
    samples, steps = queries.shape[:2]
    cache = sample_keys.shape[1]
    width = KEY_VALUE_HEADS * HEAD_SIZE
    half_width = HALF * HEAD_SIZE
    prompts, block = document_keys.shape[:2]
    rows = steps * GROUP
    core_rows = samples * rows
    chip_rows = 2 * core_rows
    lines = n // 4
    padded = cache + 128
    pairs = HALF // 2
    vmem = pl.BlockSpec(memory_space=pltpu.VMEM)
    hbm = pl.BlockSpec(memory_space=pl.ANY)
    dma = pltpu.SemaphoreType.DMA
    result = pl.pallas_call(
        functools.partial(kernel, n),
        out_shape=pltpu.VMEM((samples * QUERY_HEADS * steps, HEAD_SIZE), BF16),
        in_specs=[hbm, hbm, hbm, hbm, hbm, hbm, hbm, hbm, hbm],
        out_specs=vmem,
        scratch_shapes=[
            pltpu.SMEM(suffix_len.shape, jnp.int32),
            pltpu.SMEM(prompt_id.shape, jnp.int32),
            pltpu.VMEM(queries.shape, BF16),
            pltpu.VMEM(step_keys.shape, BF16),
            pltpu.VMEM(step_values.shape, BF16),
            pltpu.VMEM((samples, padded, width), BF16),
            pltpu.VMEM((samples, padded, width), BF16),
            pltpu.VMEM((prompts, 2 * block, half_width), BF16),
            pltpu.VMEM((prompts, 2 * block, half_width), BF16),
            pltpu.VMEM((HALF, prompts * HEAD_SIZE, 2 * block), BF16),
            pltpu.VMEM((2, pairs, 2 * core_rows, HEAD_SIZE), BF16),
            pltpu.VMEM((2 * pairs, samples, 2 * rows, 2 * HEAD_SIZE), BF16),
            pltpu.VMEM((n, pairs, 2 * core_rows, HEAD_SIZE), BF16),
            pltpu.VMEM((1, HEAD_SIZE), F32),
            pltpu.VMEM((n, 1, HEAD_SIZE), F32),
            pltpu.VMEM((lines, HALF, HEAD_SIZE, chip_rows), F32),
            pltpu.VMEM((lines, HALF, 8, chip_rows), F32),
            pltpu.VMEM((lines, HALF, HEAD_SIZE, chip_rows), I16),
            pltpu.VMEM((lines, pairs, 3, 2, chip_rows), F32),
            pltpu.VMEM((lines, HALF, HEAD_SIZE, chip_rows), I16),
            pltpu.VMEM((lines, pairs, 3, 2, chip_rows), F32),
            pltpu.VMEM((lines * 2 * pairs, HEAD_SIZE, chip_rows), I16),
            pltpu.VMEM((lines * 2 * pairs, 4, chip_rows), F32),
            pltpu.VMEM((lines, 2, pairs, HEAD_SIZE, chip_rows), I16),
            pltpu.VMEM((lines, 2, pairs, 4, chip_rows), F32),
            pltpu.VMEM((2 * pairs, HEAD_SIZE, chip_rows), F32),
            pltpu.VMEM((2 * pairs, 8, chip_rows), F32),
            pltpu.VMEM((2 * pairs, 2 * core_rows, HEAD_SIZE), F32),
            pltpu.VMEM((2 * pairs, 2 * core_rows, 1), F32),
            pltpu.VMEM((2 * pairs, 2 * core_rows, 1), F32),
            dma((9,)),
            dma((2,)),
            dma((2,)),
            dma,
            dma((2, lines // 2)),
            dma((2, lines // 2)),
            dma((n, pairs)),
            dma,
            dma((n,)),
            dma,
            dma,
            dma((lines, pairs)),
            dma((lines, pairs)),
            dma,
            dma,
            dma((lines, 2, pairs)),
            dma((lines, 2, pairs)),
        ],
        compiler_params=pltpu.CompilerParams(
            collective_id=0, has_side_effects=True, vmem_limit_bytes=60 << 20
        ),
    )(
        suffix_len,
        prompt_id,
        queries,
        step_keys,
        step_values,
        sample_keys,
        sample_values,
        document_keys,
        document_values,
    )
    return result.reshape(samples, QUERY_HEADS, steps, HEAD_SIZE).transpose(0, 2, 1, 3).reshape(queries.shape)


def solution(mesh):
    return jax.shard_map(
        body,
        mesh=mesh,
        in_specs=(
            P(("groups", "seq"), None, None),
            P(("groups", "seq"), None, None),
            P(("groups", "seq"), None, None),
            P(("groups", "seq"), None, None),
            P(("groups", "seq"), None, None),
            P(("groups", "seq")),
            P(("groups", "seq")),
            P("groups", "seq", None),
            P("groups", "seq", None),
        ),
        out_specs=P(("groups", "seq"), None, None),
        check_vma=False,
    )
```

```python
import functools

import jax
import jax.numpy as jnp
from jax import lax
from jax.experimental import pallas as pl
from jax.experimental.pallas import tpu as pltpu
from jax.sharding import PartitionSpec as P

QUERY_HEADS = 64
KEY_VALUE_HEADS = 8
HEAD_SIZE = 128
HALF = KEY_VALUE_HEADS // 2
GROUP = QUERY_HEADS // KEY_VALUE_HEADS
LOG2E = 1.4426950408889634
FACTOR = (HEAD_SIZE ** (-0.5)) * LOG2E
LEVELS = 32767.0
MESH = pl.DeviceIdType.MESH
NT = (((1,), (1,)), ((), ()))
NN = (((1,), (0,)), ((), ()))
F32, BF16, I16 = jnp.float32, jnp.bfloat16, jnp.int16


def quantize(values):
    scale = jnp.maximum(jnp.max(jnp.abs(values), axis=0, keepdims=True), 1e-30)
    return jnp.round(values * (LEVELS / scale)).astype(jnp.int32).astype(I16), scale


def kernel(
    n,
    lengths,
    prompt_id,
    queries,
    step_keys,
    step_values,
    sample_keys,
    sample_values,
    document_keys,
    document_values,
    out_ref,
    len_ref,
    id_ref,
    query_ref,
    step_key_ref,
    step_value_ref,
    key_buf,
    value_buf,
    doc_keys,
    doc_values,
    value_t,
    query_msg,
    query_pair,
    query_buf,
    mark_msg,
    mark_buf,
    own_part,
    own_stat,
    y_send,
    y_send_stat,
    y_got,
    y_got_stat,
    z_send,
    z_send_stat,
    z_got,
    z_got_stat,
    sum_part,
    sum_stat,
    suffix_out,
    suffix_max,
    suffix_total,
    local_sem,
    doc_send,
    doc_recv,
    query_send,
    forward_sem,
    hop_sem,
    query_recv,
    mark_send,
    mark_recv,
    y_send_sem,
    y_stat_sem,
    y_recv,
    y_stat_recv,
    z_send_sem,
    z_stat_sem,
    z_recv,
    z_stat_recv,
):
    me = lax.axis_index("seq")
    core = lax.rem(me, 2)
    row = lax.rem(lax.div(me, 2), 2)
    line = lax.div(me, 4)
    lines = n // 4
    samples, cache = sample_keys.shape[0], sample_keys.shape[1]
    steps = step_keys.shape[1]
    rows = steps * GROUP
    core_rows = samples * rows
    chip_rows = 2 * core_rows
    prompts, block = document_keys.shape[:2]
    half_width = HALF * HEAD_SIZE
    padded = key_buf.shape[1]

    def device(at_line, at_row, at_core):
        return at_line * 4 + at_row * 2 + at_core

    couples = lines // 2
    couple, member = lax.div(line, 2), lax.rem(line, 2)
    mate = line + 1 - 2 * member

    def wraps(turn):
        return lax.div(couple + turn, couples)

    def couple_at(turn):
        return couple + turn - wraps(turn) * couples

    def turn_at(step):
        return lax.div(step, 2)

    def line_at(step):
        turn, second = turn_at(step), lax.rem(step, 2)
        first = wraps(turn) + (1 - jnp.minimum(turn, 1)) * member
        return couple_at(turn) * 2 + first + second - 2 * first * second

    def gateway(turn):
        return (turn >= 1) & (member == 1 - wraps(turn))

    inner = gateway(1)
    upper = wraps(1) == 1

    def remote(source, target, send, recv, other):
        return pltpu.make_async_remote_copy(
            src_ref=source,
            dst_ref=target,
            send_sem=send,
            recv_sem=recv,
            device_id={"seq": other},
            device_id_type=MESH,
        )

    def arrived(ref, sem):
        pltpu.make_async_copy(ref, ref, sem).wait()

    def query_arrived(source, pair):
        if pair == 0:
            arrived(mark_buf.at[source], mark_recv.at[source])
        arrived(query_buf.at[source, pair], query_recv.at[source, pair])

    partner = device(line, row, 1 - core)
    across = device(line, 1 - row, core)

    barrier = pltpu.get_barrier_semaphore()

    def greet(other):
        pl.semaphore_signal(barrier, inc=1, device_id={"seq": other}, device_id_type=MESH)

    greet(partner)
    for c in range(2):
        greet(device(line, 1 - row, c))

    for c in range(2):
        greet(device(mate, row, c))

    def greet_far(turn, carry):
        @pl.when(gateway(turn))
        def _():
            for at in range(2):
                for c in range(2):
                    greet(device(couple_at(turn) * 2 + at, row, c))

        return carry

    lax.fori_loop(1, couples, greet_far, 0)

    def half_of(ref, half):
        return ref.at[:, :, pl.ds(pl.multiple_of(half * half_width, half_width), half_width)]

    def own_rows(ref):
        return ref.at[:, pl.ds(pl.multiple_of(core * block, block), block), :]

    small = [
        pltpu.make_async_copy(queries, query_ref, local_sem.at[4]),
        pltpu.make_async_copy(step_keys, step_key_ref, local_sem.at[5]),
        pltpu.make_async_copy(step_values, step_value_ref, local_sem.at[6]),
        pltpu.make_async_copy(prompt_id, id_ref, local_sem.at[7]),
        pltpu.make_async_copy(lengths, len_ref, local_sem.at[8]),
    ]
    local = [
        pltpu.make_async_copy(half_of(document_keys, core), own_rows(doc_keys), local_sem.at[0]),
        pltpu.make_async_copy(half_of(document_values, core), own_rows(doc_values), local_sem.at[1]),
        pltpu.make_async_copy(sample_keys, key_buf.at[:, pl.ds(0, cache), :], local_sem.at[2]),
        pltpu.make_async_copy(sample_values, value_buf.at[:, pl.ds(0, cache), :], local_sem.at[3]),
    ]
    for copy in small + local:
        copy.start()

    small[0].wait()
    query_pair[...] = jnp.zeros(query_pair.shape, BF16)
    for s in range(samples):
        for g in range(KEY_VALUE_HEADS):
            first = g * GROUP
            part = jnp.concatenate(
                [
                    query_ref[s, :, (first + r) * HEAD_SIZE : (first + r + 1) * HEAD_SIZE].astype(F32)
                    for r in range(GROUP)
                ],
                axis=0,
            ).astype(BF16)
            query_msg[
                g // HALF, (g % HALF) // 2, pl.ds((g % 2) * core_rows + s * rows, rows), :
            ] = part
            side = g % 2
            query_pair[
                g // 2, s, pl.ds(side * rows, rows), pl.ds(side * HEAD_SIZE, HEAD_SIZE)
            ] = part
    small[3].wait()
    mark_lane = lax.rem(lax.broadcasted_iota(jnp.int32, (1, HEAD_SIZE), 1), core_rows) // rows
    marks = jnp.zeros((1, HEAD_SIZE), F32)
    for s in range(samples):
        marks = jnp.where(mark_lane == s, id_ref[s].astype(F32), marks)
    mark_msg[...] = marks

    pl.semaphore_wait(barrier, 2 * couples + 3)

    def send_query(half, pair, other):
        if pair == 0:
            remote(mark_msg, mark_buf.at[me], mark_send, mark_recv.at[me], other).start()
        remote(
            query_msg.at[half, pair],
            query_buf.at[me, pair],
            query_send,
            query_recv.at[me, pair],
            other,
        ).start()

    def send_chip(at_line, at_row):
        for pair in range(HALF // 2):
            for c in range(2):
                send_query(c, pair, device(at_line, at_row, c))

    send_chip(line, 1 - row)
    send_chip(mate, row)

    def send_far(turn, carry):
        send_chip(couple_at(turn) * 2 + wraps(turn), row)
        return carry

    lax.fori_loop(1, couples, send_far, 0)
    for pair in range(HALF // 2):
        send_query(1 - core, pair, partner)
    swaps = [
        remote(half_of(source, 1 - core), own_rows(target), doc_send.at[k], doc_recv.at[k], partner)
        for k, (source, target) in enumerate(
            ((document_keys, doc_keys), (document_values, doc_values))
        )
    ]
    for copy in swaps:
        copy.start()

    query_buf[me] = query_msg[core]
    mark_buf[me] = marks
    small[1].wait()
    small[2].wait()
    small[4].wait()
    for s in range(samples):
        for buf, step_ref in ((key_buf, step_key_ref), (value_buf, step_value_ref)):
            buf[s, pl.ds(cache, padded - cache), :] = jnp.zeros(
                (padded - cache, buf.shape[2]), buf.dtype
            )
            buf[s, pl.ds(cache, steps), :] = step_ref[s]
    local[2].wait()
    local[3].wait()

    slot = lax.broadcasted_iota(jnp.int32, (2 * rows, padded), 1)
    now = lax.rem(lax.broadcasted_iota(jnp.int32, (2 * rows, padded), 0), steps)
    fresh = (slot >= cache) & (slot - cache <= now)

    def suffix(pair, carry=0):
        wide = pl.ds(pl.multiple_of(pair * 2 * HEAD_SIZE, 2 * HEAD_SIZE), 2 * HEAD_SIZE)
        for s in range(samples):
            scores = lax.dot_general(
                query_pair[pair, s], key_buf[s, :, wide], NT, preferred_element_type=F32
            )
            scores = jnp.where((slot < len_ref[s]) | fresh, scores, -jnp.inf)
            peak = jnp.max(scores, axis=1, keepdims=True)
            expo = jnp.exp2((scores - peak) * FACTOR)
            total = jnp.sum(expo, axis=1, keepdims=True)
            result = lax.dot_general(
                expo.astype(BF16), value_buf[s, :, wide], NN, preferred_element_type=F32
            )
            for side in range(2):
                part = pl.ds(side * core_rows + s * rows, rows)
                cut = slice(side * rows, (side + 1) * rows)
                suffix_max[pair, part, :] = peak[cut]
                suffix_total[pair, part, :] = total[cut]
                suffix_out[pair, part, :] = result[
                    cut, side * HEAD_SIZE : (side + 1) * HEAD_SIZE
                ]
        return carry

    lax.fori_loop(0, HALF // 2, suffix, 0)

    local[0].wait()
    local[1].wait()
    for copy in swaps:
        copy.wait_recv()
    for h in range(HALF):
        for p in range(prompts):
            value_t[h, pl.ds(p * HEAD_SIZE, HEAD_SIZE), :] = doc_values[
                p, :, h * HEAD_SIZE : (h + 1) * HEAD_SIZE
            ].T

    lane = lax.broadcasted_iota(jnp.int32, (1, chip_rows), 1)

    def pass_on(source, pair, query_sem, mark_sem, other):
        if pair == 0:
            remote(
                mark_buf.at[source], mark_buf.at[source], mark_sem, mark_recv.at[source], other
            ).start()
        remote(
            query_buf.at[source, pair],
            query_buf.at[source, pair],
            query_sem,
            query_recv.at[source, pair],
            other,
        ).start()

    def is_far(step):
        return (step >= 2) & (lax.rem(step, 2) == 1)

    def relay(step):
        turn = turn_at(step)
        sources = [device(line_at(step), row, c) for c in range(2)]
        for pair in range(HALF // 2):
            for source in sources:
                query_arrived(source, pair)

                @pl.when(gateway(turn))
                def _():
                    pass_on(
                        source,
                        pair,
                        forward_sem.at[0, turn],
                        forward_sem.at[1, turn],
                        device(mate, row, core),
                    )

                @pl.when(jnp.logical_not(is_far(step)))
                def _():
                    pass_on(source, pair, query_send, mark_send, across)

    def hop_out():
        for pair in range(HALF // 2):
            for c in range(2):
                source = device(line, 1 - row, c)
                query_arrived(source, pair)
                for turn in range(1, couples):

                    @pl.when(jnp.logical_not(gateway(turn)))
                    def _():
                        pass_on(
                            source,
                            pair,
                            hop_sem.at[0, turn],
                            hop_sem.at[1, turn],
                            device(couple_at(turn) * 2 + wraps(turn), row, core),
                        )

    def hop_on(step):
        turn = turn_at(step)
        for pair in range(HALF // 2):
            for c in range(2):
                source = device(line_at(step), 1 - row, c)
                query_arrived(source, pair)
                pass_on(
                    source,
                    pair,
                    forward_sem.at[0, turn],
                    forward_sem.at[1, turn],
                    device(mate, row, core),
                )

    def attend(step):
        there = line_at(step)
        mine = [device(there, row, c) for c in range(2)]
        theirs = [device(there, 1 - row, c) for c in range(2)]

        sources = mine + theirs
        hopped = is_far(step) & gateway(turn_at(step))

        @pl.when(hopped)
        def _():
            hop_on(step)

        for pair in range(HALF // 2):

            @pl.when(step == 0)
            def _():
                query_arrived(partner, pair)

            @pl.when((step != 0) & jnp.logical_not(hopped))
            def _():
                for source in theirs:
                    query_arrived(source, pair)

            if pair == 0:
                marked = [mark_buf[source] for source in sources]
                masks = [
                    jnp.concatenate(
                        [
                            jnp.broadcast_to(
                                jnp.where(mark[:, s * rows : s * rows + 1] == p, 1.0, 0.0),
                                (rows, HEAD_SIZE),
                            )
                            for mark in marked
                            for s in range(samples)
                        ],
                        axis=0,
                    ).astype(BF16)
                    for p in range(prompts)
                ]
                marks = jnp.concatenate(
                    [
                        jnp.where(lane < core_rows, marked[2 * k], marked[2 * k + 1])
                        for k in range(2)
                    ],
                    axis=1,
                )
            stats = []
            for h in (2 * pair, 2 * pair + 1):
                query = jnp.concatenate(
                    [
                        query_buf[source, pair, pl.ds((h % 2) * core_rows, core_rows), :]
                        for source in sources
                    ],
                    axis=0,
                )
                query = jnp.concatenate([query * mask for mask in masks], axis=1)
                cols = slice(h * HEAD_SIZE, (h + 1) * HEAD_SIZE)
                keys = jnp.concatenate([doc_keys[p, :, cols] for p in range(prompts)], axis=1)
                scores = lax.dot_general(keys, query, NT, preferred_element_type=F32)
                peak = jnp.max(scores, axis=0, keepdims=True)
                expo = jnp.exp2((scores - peak) * FACTOR)
                total = jnp.sum(expo, axis=0, keepdims=True)
                both = lax.dot_general(
                    value_t[h], expo.astype(BF16), NN, preferred_element_type=F32
                )
                result = both[:HEAD_SIZE]
                for p in range(1, prompts):
                    result = jnp.where(
                        marks == p, both[p * HEAD_SIZE : (p + 1) * HEAD_SIZE], result
                    )
                own_part[step, h] = result[:, :chip_rows]
                own_stat[step, h, 0:1, :] = peak[:, :chip_rows]
                own_stat[step, h, 1:2, :] = total[:, :chip_rows]
                y_send[step, h], scale = quantize(result[:, chip_rows:])
                stats += [peak[:, chip_rows:], total[:, chip_rows:], scale]
            for k, stat in enumerate(stats):
                y_send_stat[step, pair, k % 3, k // 3 : k // 3 + 1, :] = stat
            heads = pl.ds(2 * pair, 2)
            remote(
                y_send.at[step, heads],
                y_got.at[step, heads],
                y_send_sem,
                y_recv.at[step, pair],
                across,
            ).start()
            remote(
                y_send_stat.at[step, pair],
                y_got_stat.at[step, pair],
                y_stat_sem,
                y_stat_recv.at[step, pair],
                across,
            ).start()

    def give(source, target, send, recv, other):
        @pl.when(other != me)
        def _():
            remote(source, target, send, recv, other).start()

        @pl.when(other == me)
        def _():
            pltpu.make_async_copy(source, target, recv).start()

    def combine(step):
        there = line_at(step)
        place = 2 * turn_at(step) + member
        for pair in range(HALF // 2):
            arrived(y_got.at[step, pl.ds(2 * pair, 2)], y_recv.at[step, pair])
            arrived(y_got_stat.at[step, pair], y_stat_recv.at[step, pair])
            merged = []
            for side in range(2):
                h = 2 * pair + side
                peak_a, total_a = own_stat[step, h, 0:1, :], own_stat[step, h, 1:2, :]
                peak_b, total_b, scale_b = (
                    y_got_stat[step, pair, k, side : side + 1, :] for k in range(3)
                )
                top = jnp.maximum(peak_a, peak_b)
                weight_a = jnp.exp2((peak_a - top) * FACTOR)
                weight_b = jnp.exp2((peak_b - top) * FACTOR)
                result = own_part[step, h] * weight_a + y_got[step, h].astype(jnp.int32).astype(
                    F32
                ) * (weight_b * (scale_b * (1.0 / LEVELS)))
                merged.append((result, top, total_a * weight_a + total_b * weight_b))
            for c in range(2):
                mixed = []
                for low, high in zip(*merged):
                    wide = jnp.broadcast_to(low, (max(8, low.shape[0]), chip_rows))
                    wide_high = jnp.broadcast_to(high, wide.shape)
                    if c == 0:
                        wide_high = pltpu.roll(wide_high, core_rows, 1)
                    else:
                        wide = pltpu.roll(wide, core_rows, 1)
                    mixed.append(
                        jnp.where(lane < core_rows, wide, wide_high)[: low.shape[0]]
                    )
                result, top, total = mixed
                at = (step * 2 + c) * 2 + pair
                z_send[at], scale = quantize(result)
                z_send_stat[at, 0] = top
                z_send_stat[at, 1] = total
                z_send_stat[at, 2] = scale
                give(
                    z_send.at[at],
                    z_got.at[place, core, pair],
                    z_send_sem,
                    z_recv.at[place, core, pair],
                    device(there, row, c),
                )
                give(
                    z_send_stat.at[at],
                    z_got_stat.at[place, core, pair],
                    z_stat_sem,
                    z_stat_recv.at[place, core, pair],
                    device(there, row, c),
                )

    far = list(range(2, lines))
    swapped = [step + 1 - 2 * (step % 2) for step in far]

    def pick(order, trip):
        chosen = order[-1]
        for k in range(lines - 1):
            chosen = jnp.where(trip == k, order[k], chosen)
        return chosen

    def attend_at(trip):
        low = jnp.where(inner, pick(far + [1, 0], trip), pick([0, 1] + far, trip))
        high = jnp.where(inner, pick(far + [1, 0], trip), pick([0] + swapped[:1] + [1] + swapped[1:], trip))
        return jnp.where(upper, high, low)

    def relay_at(index):
        within = jnp.where(index == 0, 2, jnp.where(index == 1, 1, index + 1))
        return jnp.where(inner, within, index + 1)

    def advance(trip, carry):
        turned = ((trip == 0) == inner) & (trip <= 1)

        @pl.when(turned)
        def _():
            suffix(HALF // 2)

        @pl.when(turned & inner)
        def _():
            suffix(HALF // 2 + 1)

        @pl.when(turned)
        def _():
            relay(relay_at(1))

        @pl.when(turned & jnp.logical_not(inner))
        def _():
            suffix(HALF // 2 + 1)

        index = jnp.where(inner, trip + 2, jnp.where(upper & (trip >= 1), trip + 1, trip))

        @pl.when((index >= 2) & (index <= lines - 2))
        def _():
            relay(relay_at(index))

        attend(attend_at(trip))

        @pl.when(trip >= 1)
        def _():
            combine(attend_at(trip - 1))

        return carry

    relay(relay_at(0))
    hop_out()
    lax.fori_loop(0, lines, advance, 0)
    combine(attend_at(lines - 1))

    last = jnp.where(inner, 2 + member, 1 - member)

    def gather(place, at, half, pair):
        arrived(z_got_stat.at[place, half, pair], z_stat_recv.at[place, half, pair])
        arrived(z_got.at[place, half, pair], z_recv.at[place, half, pair])
        peak = z_got_stat[place, half, pair, 0]
        total = z_got_stat[place, half, pair, 1]
        scale = z_got_stat[place, half, pair, 2]
        before = sum_stat[at, 0:1, :]
        top = jnp.maximum(before, peak)
        old = jnp.exp2((before - top) * FACTOR)
        new = jnp.exp2((peak - top) * FACTOR)
        above = sum_part[at] * old + z_got[place, half, pair].astype(jnp.int32).astype(F32) * (
            new * (scale * (1.0 / LEVELS))
        )
        return above, top, sum_stat[at, 1:2, :] * old + total * new

    def tiles(place, use):
        for pair in range(HALF // 2):
            for half in range(2):
                at = half * (HALF // 2) + pair
                use(at, *gather(place, at, half, pair))

    def keep(at, above, top, total):
        sum_part[at] = above
        sum_stat[at, 0:1, :] = top
        sum_stat[at, 1:2, :] = total

    def finish(at, above, top, total):
        turned = jnp.concatenate([top, total, jnp.zeros((6, chip_rows), F32)], axis=0).T
        peak, total = turned[:, 0:1], turned[:, 1:2]
        top = jnp.maximum(peak, suffix_max[at])
        weight = jnp.exp2((peak - top) * FACTOR)
        weight_own = jnp.exp2((suffix_max[at] - top) * FACTOR)
        result = (above.T * weight + suffix_out[at] * weight_own) / (
            total * weight + suffix_total[at] * weight_own
        )
        for side in range(2):
            for s in range(samples):
                first = side * core_rows + s * rows
                target = (s * KEY_VALUE_HEADS + 2 * at + side) * rows
                out_ref[pl.ds(target, rows), :] = result[first : first + rows].astype(
                    out_ref.dtype
                )

    for at in range(2 * (HALF // 2)):
        keep(
            at,
            jnp.zeros((HEAD_SIZE, chip_rows), F32),
            jnp.full((1, chip_rows), -1e30, F32),
            jnp.zeros((1, chip_rows), F32),
        )

    def add(step, carry):
        tiles(lax.rem(last + 1 + step, lines), keep)
        return carry

    lax.fori_loop(0, lines - 1, add, 0)
    tiles(last, finish)

    for kind, (buf, sem) in enumerate(((query_buf, query_send), (mark_buf, mark_send))):
        arrived(buf.at[pl.ds(0, 4 * couples + 3)], sem)
        for turn in range(1, couples):

            @pl.when(gateway(turn))
            def _():
                arrived(buf.at[pl.ds(0, 6)], forward_sem.at[kind, turn])

            @pl.when(jnp.logical_not(gateway(turn)))
            def _():
                arrived(buf.at[pl.ds(0, 2)], hop_sem.at[kind, turn])

    pltpu.make_async_copy(y_send, y_send, y_send_sem).wait()
    pltpu.make_async_copy(y_send_stat, y_send_stat, y_stat_sem).wait()
    sent = z_send.at[pl.ds(0, 4 * lines - 2)]
    pltpu.make_async_copy(sent, sent, z_send_sem).wait()
    sent = z_send_stat.at[pl.ds(0, 4 * lines - 2)]
    pltpu.make_async_copy(sent, sent, z_stat_sem).wait()
    for copy in swaps:
        copy.wait_send()


def body(
    queries,
    step_keys,
    step_values,
    sample_keys,
    sample_values,
    suffix_len,
    prompt_id,
    document_keys,
    document_values,
):
    n = lax.axis_size("seq")
    samples, steps = queries.shape[:2]
    cache = sample_keys.shape[1]
    width = KEY_VALUE_HEADS * HEAD_SIZE
    half_width = HALF * HEAD_SIZE
    prompts, block = document_keys.shape[:2]
    rows = steps * GROUP
    core_rows = samples * rows
    chip_rows = 2 * core_rows
    lines = n // 4
    padded = cache + 128
    pairs = HALF // 2
    vmem = pl.BlockSpec(memory_space=pltpu.VMEM)
    hbm = pl.BlockSpec(memory_space=pl.ANY)
    dma = pltpu.SemaphoreType.DMA
    result = pl.pallas_call(
        functools.partial(kernel, n),
        out_shape=pltpu.VMEM((samples * QUERY_HEADS * steps, HEAD_SIZE), BF16),
        in_specs=[hbm, hbm, hbm, hbm, hbm, hbm, hbm, hbm, hbm],
        out_specs=vmem,
        scratch_shapes=[
            pltpu.SMEM(suffix_len.shape, jnp.int32),
            pltpu.SMEM(prompt_id.shape, jnp.int32),
            pltpu.VMEM(queries.shape, BF16),
            pltpu.VMEM(step_keys.shape, BF16),
            pltpu.VMEM(step_values.shape, BF16),
            pltpu.VMEM((samples, padded, width), BF16),
            pltpu.VMEM((samples, padded, width), BF16),
            pltpu.VMEM((prompts, 2 * block, half_width), BF16),
            pltpu.VMEM((prompts, 2 * block, half_width), BF16),
            pltpu.VMEM((HALF, prompts * HEAD_SIZE, 2 * block), BF16),
            pltpu.VMEM((2, pairs, 2 * core_rows, HEAD_SIZE), BF16),
            pltpu.VMEM((2 * pairs, samples, 2 * rows, 2 * HEAD_SIZE), BF16),
            pltpu.VMEM((n, pairs, 2 * core_rows, HEAD_SIZE), BF16),
            pltpu.VMEM((1, HEAD_SIZE), F32),
            pltpu.VMEM((n, 1, HEAD_SIZE), F32),
            pltpu.VMEM((lines, HALF, HEAD_SIZE, chip_rows), F32),
            pltpu.VMEM((lines, HALF, 8, chip_rows), F32),
            pltpu.VMEM((lines, HALF, HEAD_SIZE, chip_rows), I16),
            pltpu.VMEM((lines, pairs, 3, 2, chip_rows), F32),
            pltpu.VMEM((lines, HALF, HEAD_SIZE, chip_rows), I16),
            pltpu.VMEM((lines, pairs, 3, 2, chip_rows), F32),
            pltpu.VMEM((lines * 2 * pairs, HEAD_SIZE, chip_rows), I16),
            pltpu.VMEM((lines * 2 * pairs, 3, 1, chip_rows), F32),
            pltpu.VMEM((lines, 2, pairs, HEAD_SIZE, chip_rows), I16),
            pltpu.VMEM((lines, 2, pairs, 3, 1, chip_rows), F32),
            pltpu.VMEM((2 * pairs, HEAD_SIZE, chip_rows), F32),
            pltpu.VMEM((2 * pairs, 8, chip_rows), F32),
            pltpu.VMEM((2 * pairs, 2 * core_rows, HEAD_SIZE), F32),
            pltpu.VMEM((2 * pairs, 2 * core_rows, 1), F32),
            pltpu.VMEM((2 * pairs, 2 * core_rows, 1), F32),
            dma((9,)),
            dma((2,)),
            dma((2,)),
            dma,
            dma((2, lines // 2)),
            dma((2, lines // 2)),
            dma((n, pairs)),
            dma,
            dma((n,)),
            dma,
            dma,
            dma((lines, pairs)),
            dma((lines, pairs)),
            dma,
            dma,
            dma((lines, 2, pairs)),
            dma((lines, 2, pairs)),
        ],
        compiler_params=pltpu.CompilerParams(
            collective_id=0,
            has_side_effects=True,
            vmem_limit_bytes=60 << 20,
        ),
    )(
        suffix_len,
        prompt_id,
        queries,
        step_keys,
        step_values,
        sample_keys,
        sample_values,
        document_keys,
        document_values,
    )
    return result.reshape(samples, QUERY_HEADS, steps, HEAD_SIZE).transpose(0, 2, 1, 3).reshape(queries.shape)


def solution(mesh):
    return jax.shard_map(
        body,
        mesh=mesh,
        in_specs=(
            P(("groups", "seq"), None, None),
            P(("groups", "seq"), None, None),
            P(("groups", "seq"), None, None),
            P(("groups", "seq"), None, None),
            P(("groups", "seq"), None, None),
            P(("groups", "seq")),
            P(("groups", "seq")),
            P("groups", "seq", None),
            P("groups", "seq", None),
        ),
        out_specs=P(("groups", "seq"), None, None),
        check_vma=False,
    )
```

```python
import functools

import jax
import jax.numpy as jnp
from jax import lax
from jax.experimental import pallas as pl
from jax.experimental.pallas import tpu as pltpu
from jax.sharding import PartitionSpec as P

QUERY_HEADS = 64
KEY_VALUE_HEADS = 8
HEAD_SIZE = 128
HALF = KEY_VALUE_HEADS // 2
GROUP = QUERY_HEADS // KEY_VALUE_HEADS
LOG2E = 1.4426950408889634
FACTOR = (HEAD_SIZE ** (-0.5)) * LOG2E
LEVELS = 32767.0
MESH = pl.DeviceIdType.MESH
NT = (((1,), (1,)), ((), ()))
NN = (((1,), (0,)), ((), ()))
F32, BF16, I16 = jnp.float32, jnp.bfloat16, jnp.int16


def quantize(values):
    scale = jnp.maximum(jnp.max(jnp.abs(values), axis=0, keepdims=True), 1e-30)
    return jnp.round(values * (LEVELS / scale)).astype(jnp.int32).astype(I16), scale


def kernel(
    n,
    lengths,
    prompt_id,
    queries,
    step_keys,
    step_values,
    sample_keys,
    sample_values,
    document_keys,
    document_values,
    out_ref,
    len_ref,
    id_ref,
    query_ref,
    step_key_ref,
    step_value_ref,
    key_buf,
    value_buf,
    doc_keys,
    doc_values,
    value_t,
    query_msg,
    query_pair,
    query_buf,
    mark_msg,
    mark_buf,
    own_part,
    own_stat,
    y_send,
    y_send_stat,
    y_got,
    y_got_stat,
    z_send,
    z_send_stat,
    z_got,
    z_got_stat,
    sum_part,
    sum_stat,
    suffix_out,
    suffix_max,
    suffix_total,
    local_sem,
    doc_send,
    doc_recv,
    query_send,
    forward_sem,
    hop_sem,
    query_recv,
    mark_send,
    mark_recv,
    y_send_sem,
    y_stat_sem,
    y_recv,
    y_stat_recv,
    z_send_sem,
    z_stat_sem,
    z_recv,
    z_stat_recv,
):
    me = lax.axis_index("seq")
    core = lax.rem(me, 2)
    row = lax.rem(lax.div(me, 2), 2)
    line = lax.div(me, 4)
    lines = n // 4
    samples, cache = sample_keys.shape[0], sample_keys.shape[1]
    steps = step_keys.shape[1]
    rows = steps * GROUP
    core_rows = samples * rows
    chip_rows = 2 * core_rows
    prompts, block = document_keys.shape[:2]
    half_width = HALF * HEAD_SIZE
    padded = key_buf.shape[1]

    def device(at_line, at_row, at_core):
        return at_line * 4 + at_row * 2 + at_core

    couples = lines // 2
    couple, member = lax.div(line, 2), lax.rem(line, 2)
    mate = line + 1 - 2 * member

    def wraps(turn):
        return lax.div(couple + turn, couples)

    def couple_at(turn):
        return couple + turn - wraps(turn) * couples

    def turn_at(step):
        return lax.div(step, 2)

    def line_at(step):
        turn, second = turn_at(step), lax.rem(step, 2)
        first = wraps(turn) + (1 - jnp.minimum(turn, 1)) * member
        return couple_at(turn) * 2 + first + second - 2 * first * second

    def gateway(turn):
        return (turn >= 1) & (member == 1 - wraps(turn))

    inner = gateway(1)
    upper = wraps(1) == 1

    def remote(source, target, send, recv, other):
        return pltpu.make_async_remote_copy(
            src_ref=source,
            dst_ref=target,
            send_sem=send,
            recv_sem=recv,
            device_id={"seq": other},
            device_id_type=MESH,
        )

    def arrived(ref, sem):
        pltpu.make_async_copy(ref, ref, sem).wait()

    def query_arrived(source, pair):
        if pair == 0:
            arrived(mark_buf.at[source], mark_recv.at[source])
        arrived(query_buf.at[source, pair], query_recv.at[source, pair])

    partner = device(line, row, 1 - core)
    across = device(line, 1 - row, core)

    barrier = pltpu.get_barrier_semaphore()

    def greet(other):
        pl.semaphore_signal(barrier, inc=1, device_id={"seq": other}, device_id_type=MESH)

    greet(partner)
    for c in range(2):
        greet(device(line, 1 - row, c))

    for c in range(2):
        greet(device(mate, row, c))

    def greet_far(turn, carry):
        @pl.when(gateway(turn))
        def _():
            for at in range(2):
                for c in range(2):
                    greet(device(couple_at(turn) * 2 + at, row, c))

        return carry

    lax.fori_loop(1, couples, greet_far, 0)

    def half_of(ref, half):
        return ref.at[:, :, pl.ds(pl.multiple_of(half * half_width, half_width), half_width)]

    def own_rows(ref):
        return ref.at[:, pl.ds(pl.multiple_of(core * block, block), block), :]

    small = [
        pltpu.make_async_copy(queries, query_ref, local_sem.at[4]),
        pltpu.make_async_copy(step_keys, step_key_ref, local_sem.at[5]),
        pltpu.make_async_copy(step_values, step_value_ref, local_sem.at[6]),
        pltpu.make_async_copy(prompt_id, id_ref, local_sem.at[7]),
        pltpu.make_async_copy(lengths, len_ref, local_sem.at[8]),
    ]
    local = [
        pltpu.make_async_copy(half_of(document_keys, core), own_rows(doc_keys), local_sem.at[0]),
        pltpu.make_async_copy(half_of(document_values, core), own_rows(doc_values), local_sem.at[1]),
        pltpu.make_async_copy(sample_keys, key_buf.at[:, pl.ds(0, cache), :], local_sem.at[2]),
        pltpu.make_async_copy(sample_values, value_buf.at[:, pl.ds(0, cache), :], local_sem.at[3]),
    ]
    for copy in small + local:
        copy.start()

    small[0].wait()
    query_pair[...] = jnp.zeros(query_pair.shape, BF16)
    for s in range(samples):
        for g in range(KEY_VALUE_HEADS):
            first = g * GROUP
            part = jnp.concatenate(
                [
                    query_ref[s, :, (first + r) * HEAD_SIZE : (first + r + 1) * HEAD_SIZE].astype(F32)
                    for r in range(GROUP)
                ],
                axis=0,
            ).astype(BF16)
            query_msg[
                g // HALF, (g % HALF) // 2, pl.ds((g % 2) * core_rows + s * rows, rows), :
            ] = part
            side = g % 2
            query_pair[
                g // 2, s, pl.ds(side * rows, rows), pl.ds(side * HEAD_SIZE, HEAD_SIZE)
            ] = part
    small[3].wait()
    mark_lane = lax.rem(lax.broadcasted_iota(jnp.int32, (1, HEAD_SIZE), 1), core_rows) // rows
    marks = jnp.zeros((1, HEAD_SIZE), F32)
    for s in range(samples):
        marks = jnp.where(mark_lane == s, id_ref[s].astype(F32), marks)
    mark_msg[...] = marks

    pl.semaphore_wait(barrier, 2 * couples + 3)

    def send_query(half, pair, other):
        if pair == 0:
            remote(mark_msg, mark_buf.at[me], mark_send, mark_recv.at[me], other).start()
        remote(
            query_msg.at[half, pair],
            query_buf.at[me, pair],
            query_send,
            query_recv.at[me, pair],
            other,
        ).start()

    def send_chip(at_line, at_row):
        for pair in range(HALF // 2):
            for c in range(2):
                send_query(c, pair, device(at_line, at_row, c))

    send_chip(line, 1 - row)
    send_chip(mate, row)

    def send_far(turn, carry):
        send_chip(couple_at(turn) * 2 + wraps(turn), row)
        return carry

    lax.fori_loop(1, couples, send_far, 0)
    for pair in range(HALF // 2):
        send_query(1 - core, pair, partner)
    swaps = [
        remote(half_of(source, 1 - core), own_rows(target), doc_send.at[k], doc_recv.at[k], partner)
        for k, (source, target) in enumerate(
            ((document_keys, doc_keys), (document_values, doc_values))
        )
    ]
    for copy in swaps:
        copy.start()

    query_buf[me] = query_msg[core]
    mark_buf[me] = marks
    small[1].wait()
    small[2].wait()
    small[4].wait()
    for s in range(samples):
        for buf, step_ref in ((key_buf, step_key_ref), (value_buf, step_value_ref)):
            buf[s, pl.ds(cache, padded - cache), :] = jnp.zeros(
                (padded - cache, buf.shape[2]), buf.dtype
            )
            buf[s, pl.ds(cache, steps), :] = step_ref[s]
    local[2].wait()
    local[3].wait()

    slot = lax.broadcasted_iota(jnp.int32, (2 * rows, padded), 1)
    now = lax.rem(lax.broadcasted_iota(jnp.int32, (2 * rows, padded), 0), steps)
    fresh = (slot >= cache) & (slot - cache <= now)

    def suffix(pair, carry=0):
        wide = pl.ds(pl.multiple_of(pair * 2 * HEAD_SIZE, 2 * HEAD_SIZE), 2 * HEAD_SIZE)
        for s in range(samples):
            scores = lax.dot_general(
                query_pair[pair, s], key_buf[s, :, wide], NT, preferred_element_type=F32
            )
            scores = jnp.where((slot < len_ref[s]) | fresh, scores, -jnp.inf)
            peak = jnp.max(scores, axis=1, keepdims=True)
            expo = jnp.exp2((scores - peak) * FACTOR)
            total = jnp.sum(expo, axis=1, keepdims=True)
            result = lax.dot_general(
                expo.astype(BF16), value_buf[s, :, wide], NN, preferred_element_type=F32
            )
            for side in range(2):
                part = pl.ds(side * core_rows + s * rows, rows)
                cut = slice(side * rows, (side + 1) * rows)
                suffix_max[pair, part, :] = peak[cut]
                suffix_total[pair, part, :] = total[cut]
                suffix_out[pair, part, :] = result[
                    cut, side * HEAD_SIZE : (side + 1) * HEAD_SIZE
                ]
        return carry

    lax.fori_loop(0, HALF // 2, suffix, 0)

    local[0].wait()
    local[1].wait()
    for copy in swaps:
        copy.wait_recv()
    for h in range(HALF):
        for p in range(prompts):
            value_t[h, pl.ds(p * HEAD_SIZE, HEAD_SIZE), :] = doc_values[
                p, :, h * HEAD_SIZE : (h + 1) * HEAD_SIZE
            ].T

    lane = lax.broadcasted_iota(jnp.int32, (1, chip_rows), 1)

    def pass_on(source, pair, query_sem, mark_sem, other):
        if pair == 0:
            remote(
                mark_buf.at[source], mark_buf.at[source], mark_sem, mark_recv.at[source], other
            ).start()
        remote(
            query_buf.at[source, pair],
            query_buf.at[source, pair],
            query_sem,
            query_recv.at[source, pair],
            other,
        ).start()

    def is_far(step):
        return (step >= 2) & (lax.rem(step, 2) == 1)

    def relay(step):
        turn = turn_at(step)
        sources = [device(line_at(step), row, c) for c in range(2)]
        for pair in range(HALF // 2):
            for source in sources:
                query_arrived(source, pair)

                @pl.when(gateway(turn))
                def _():
                    pass_on(
                        source,
                        pair,
                        forward_sem.at[0, turn],
                        forward_sem.at[1, turn],
                        device(mate, row, core),
                    )

                @pl.when(jnp.logical_not(is_far(step)))
                def _():
                    pass_on(source, pair, query_send, mark_send, across)

    def hop_out():
        for pair in range(HALF // 2):
            for c in range(2):
                source = device(line, 1 - row, c)
                query_arrived(source, pair)
                for turn in range(1, couples):

                    @pl.when(jnp.logical_not(gateway(turn)))
                    def _():
                        pass_on(
                            source,
                            pair,
                            hop_sem.at[0, turn],
                            hop_sem.at[1, turn],
                            device(couple_at(turn) * 2 + wraps(turn), row, core),
                        )

    def hop_on(step):
        turn = turn_at(step)
        for pair in range(HALF // 2):
            for c in range(2):
                source = device(line_at(step), 1 - row, c)
                query_arrived(source, pair)
                pass_on(
                    source,
                    pair,
                    forward_sem.at[0, turn],
                    forward_sem.at[1, turn],
                    device(mate, row, core),
                )

    def attend(step):
        there = line_at(step)
        mine = [device(there, row, c) for c in range(2)]
        theirs = [device(there, 1 - row, c) for c in range(2)]

        sources = mine + theirs
        hopped = is_far(step) & gateway(turn_at(step))

        @pl.when(hopped)
        def _():
            hop_on(step)

        for pair in range(HALF // 2):

            @pl.when(step == 0)
            def _():
                query_arrived(partner, pair)

            @pl.when((step != 0) & jnp.logical_not(hopped))
            def _():
                for source in theirs:
                    query_arrived(source, pair)

            if pair == 0:
                marked = [mark_buf[source] for source in sources]
                masks = [
                    jnp.concatenate(
                        [
                            jnp.broadcast_to(
                                jnp.where(mark[:, s * rows : s * rows + 1] == p, 1.0, 0.0),
                                (rows, HEAD_SIZE),
                            )
                            for mark in marked
                            for s in range(samples)
                        ],
                        axis=0,
                    ).astype(BF16)
                    for p in range(prompts)
                ]
                marks = jnp.concatenate(
                    [
                        jnp.where(lane < core_rows, marked[2 * k], marked[2 * k + 1])
                        for k in range(2)
                    ],
                    axis=1,
                )
            stats = []
            for h in (2 * pair, 2 * pair + 1):
                query = jnp.concatenate(
                    [
                        query_buf[source, pair, pl.ds((h % 2) * core_rows, core_rows), :]
                        for source in sources
                    ],
                    axis=0,
                )
                query = jnp.concatenate([query * mask for mask in masks], axis=1)
                cols = slice(h * HEAD_SIZE, (h + 1) * HEAD_SIZE)
                keys = jnp.concatenate([doc_keys[p, :, cols] for p in range(prompts)], axis=1)
                scores = lax.dot_general(keys, query, NT, preferred_element_type=F32)
                peak = jnp.max(scores, axis=0, keepdims=True)
                expo = jnp.exp2((scores - peak) * FACTOR)
                total = jnp.sum(expo, axis=0, keepdims=True)
                both = lax.dot_general(
                    value_t[h], expo.astype(BF16), NN, preferred_element_type=F32
                )
                result = both[:HEAD_SIZE]
                for p in range(1, prompts):
                    result = jnp.where(
                        marks == p, both[p * HEAD_SIZE : (p + 1) * HEAD_SIZE], result
                    )
                own_part[step, h] = result[:, :chip_rows]
                own_stat[step, h, 0:1, :] = peak[:, :chip_rows]
                own_stat[step, h, 1:2, :] = total[:, :chip_rows]
                y_send[step, h], scale = quantize(result[:, chip_rows:])
                stats += [peak[:, chip_rows:], total[:, chip_rows:], scale]
            for k, stat in enumerate(stats):
                y_send_stat[step, pair, k % 3, k // 3 : k // 3 + 1, :] = stat
            heads = pl.ds(2 * pair, 2)
            remote(
                y_send.at[step, heads],
                y_got.at[step, heads],
                y_send_sem,
                y_recv.at[step, pair],
                across,
            ).start()
            remote(
                y_send_stat.at[step, pair],
                y_got_stat.at[step, pair],
                y_stat_sem,
                y_stat_recv.at[step, pair],
                across,
            ).start()

    def give(source, target, send, recv, other):
        @pl.when(other != me)
        def _():
            remote(source, target, send, recv, other).start()

        @pl.when(other == me)
        def _():
            pltpu.make_async_copy(source, target, recv).start()

    def combine(step):
        there = line_at(step)
        place = 2 * turn_at(step) + member
        for pair in range(HALF // 2):
            arrived(y_got.at[step, pl.ds(2 * pair, 2)], y_recv.at[step, pair])
            arrived(y_got_stat.at[step, pair], y_stat_recv.at[step, pair])
            merged = []
            for side in range(2):
                h = 2 * pair + side
                peak_a, total_a = own_stat[step, h, 0:1, :], own_stat[step, h, 1:2, :]
                peak_b, total_b, scale_b = (
                    y_got_stat[step, pair, k, side : side + 1, :] for k in range(3)
                )
                top = jnp.maximum(peak_a, peak_b)
                weight_a = jnp.exp2((peak_a - top) * FACTOR)
                weight_b = jnp.exp2((peak_b - top) * FACTOR)
                result = own_part[step, h] * weight_a + y_got[step, h].astype(jnp.int32).astype(
                    F32
                ) * (weight_b * (scale_b * (1.0 / LEVELS)))
                merged.append((result, top, total_a * weight_a + total_b * weight_b))
            for c in range(2):
                mixed = []
                for low, high in zip(*merged):
                    wide = jnp.broadcast_to(low, (max(8, low.shape[0]), chip_rows))
                    wide_high = jnp.broadcast_to(high, wide.shape)
                    if c == 0:
                        wide_high = pltpu.roll(wide_high, core_rows, 1)
                    else:
                        wide = pltpu.roll(wide, core_rows, 1)
                    mixed.append(
                        jnp.where(lane < core_rows, wide, wide_high)[: low.shape[0]]
                    )
                result, top, total = mixed
                at = (step * 2 + c) * 2 + pair
                z_send[at], scale = quantize(result)
                z_send_stat[at, 0] = top
                z_send_stat[at, 1] = total
                z_send_stat[at, 2] = scale
                give(
                    z_send.at[at],
                    z_got.at[place, core, pair],
                    z_send_sem,
                    z_recv.at[place, core, pair],
                    device(there, row, c),
                )
                give(
                    z_send_stat.at[at],
                    z_got_stat.at[place, core, pair],
                    z_stat_sem,
                    z_stat_recv.at[place, core, pair],
                    device(there, row, c),
                )

    far = list(range(2, lines))
    swapped = [step + 1 - 2 * (step % 2) for step in far]

    def pick(order, trip):
        chosen = order[-1]
        for k in range(lines - 1):
            chosen = jnp.where(trip == k, order[k], chosen)
        return chosen

    def attend_at(trip):
        low = jnp.where(inner, pick(far + [1, 0], trip), pick([0, 1] + far, trip))
        high = jnp.where(inner, pick(far + [1, 0], trip), pick([0] + swapped[:1] + [1] + swapped[1:], trip))
        return jnp.where(upper, high, low)

    def relay_at(index):
        within = jnp.where(index == 0, 2, jnp.where(index == 1, 1, index + 1))
        return jnp.where(inner, within, index + 1)

    def advance(trip, carry):
        turned = ((trip == 0) == inner) & (trip <= 1)

        @pl.when(turned)
        def _():
            suffix(HALF // 2)

        @pl.when(turned & inner)
        def _():
            suffix(HALF // 2 + 1)

        @pl.when(turned)
        def _():
            relay(relay_at(1))

        @pl.when(turned & jnp.logical_not(inner))
        def _():
            suffix(HALF // 2 + 1)

        index = jnp.where(inner, trip + 2, jnp.where(upper & (trip >= 1), trip + 1, trip))

        @pl.when((index >= 2) & (index <= lines - 2))
        def _():
            relay(relay_at(index))

        attend(attend_at(trip))

        @pl.when(trip >= 1)
        def _():
            combine(attend_at(trip - 1))

        return carry

    relay(relay_at(0))
    hop_out()
    lax.fori_loop(0, lines, advance, 0)
    combine(attend_at(lines - 1))

    last = jnp.where(inner, 2 + member, 1 - member)

    def gather(place, at, half, pair):
        arrived(z_got_stat.at[place, half, pair], z_stat_recv.at[place, half, pair])
        arrived(z_got.at[place, half, pair], z_recv.at[place, half, pair])
        peak = z_got_stat[place, half, pair, 0]
        total = z_got_stat[place, half, pair, 1]
        scale = z_got_stat[place, half, pair, 2]
        before = sum_stat[at, 0:1, :]
        top = jnp.maximum(before, peak)
        old = jnp.exp2((before - top) * FACTOR)
        new = jnp.exp2((peak - top) * FACTOR)
        above = sum_part[at] * old + z_got[place, half, pair].astype(jnp.int32).astype(F32) * (
            new * (scale * (1.0 / LEVELS))
        )
        return above, top, sum_stat[at, 1:2, :] * old + total * new

    def tiles(place, use):
        for pair in range(HALF // 2):
            for half in range(2):
                at = half * (HALF // 2) + pair
                use(at, *gather(place, at, half, pair))

    def keep(at, above, top, total):
        sum_part[at] = above
        sum_stat[at, 0:1, :] = top
        sum_stat[at, 1:2, :] = total

    def finish(at, above, top, total):
        turned = jnp.concatenate([top, total, jnp.zeros((6, chip_rows), F32)], axis=0).T
        peak, total = turned[:, 0:1], turned[:, 1:2]
        top = jnp.maximum(peak, suffix_max[at])
        weight = jnp.exp2((peak - top) * FACTOR)
        weight_own = jnp.exp2((suffix_max[at] - top) * FACTOR)
        share = 1.0 / (total * weight + suffix_total[at] * weight_own)
        result = above.T * (weight * share) + suffix_out[at] * (weight_own * share)
        for side in range(2):
            for s in range(samples):
                first = side * core_rows + s * rows
                target = (s * KEY_VALUE_HEADS + 2 * at + side) * rows
                out_ref[pl.ds(target, rows), :] = result[first : first + rows].astype(
                    out_ref.dtype
                )

    for at in range(2 * (HALF // 2)):
        keep(
            at,
            jnp.zeros((HEAD_SIZE, chip_rows), F32),
            jnp.full((1, chip_rows), -1e30, F32),
            jnp.zeros((1, chip_rows), F32),
        )

    def add(step, carry):
        tiles(lax.rem(last + 1 + step, lines), keep)
        return carry

    lax.fori_loop(0, lines - 1, add, 0)
    tiles(last, finish)

    for kind, (buf, sem) in enumerate(((query_buf, query_send), (mark_buf, mark_send))):
        arrived(buf.at[pl.ds(0, 4 * couples + 3)], sem)
        for turn in range(1, couples):

            @pl.when(gateway(turn))
            def _():
                arrived(buf.at[pl.ds(0, 6)], forward_sem.at[kind, turn])

            @pl.when(jnp.logical_not(gateway(turn)))
            def _():
                arrived(buf.at[pl.ds(0, 2)], hop_sem.at[kind, turn])

    pltpu.make_async_copy(y_send, y_send, y_send_sem).wait()
    pltpu.make_async_copy(y_send_stat, y_send_stat, y_stat_sem).wait()
    sent = z_send.at[pl.ds(0, 4 * lines - 2)]
    pltpu.make_async_copy(sent, sent, z_send_sem).wait()
    sent = z_send_stat.at[pl.ds(0, 4 * lines - 2)]
    pltpu.make_async_copy(sent, sent, z_stat_sem).wait()
    for copy in swaps:
        copy.wait_send()


def body(
    queries,
    step_keys,
    step_values,
    sample_keys,
    sample_values,
    suffix_len,
    prompt_id,
    document_keys,
    document_values,
):
    n = lax.axis_size("seq")
    samples, steps = queries.shape[:2]
    cache = sample_keys.shape[1]
    width = KEY_VALUE_HEADS * HEAD_SIZE
    half_width = HALF * HEAD_SIZE
    prompts, block = document_keys.shape[:2]
    rows = steps * GROUP
    core_rows = samples * rows
    chip_rows = 2 * core_rows
    lines = n // 4
    padded = cache + 128
    pairs = HALF // 2
    vmem = pl.BlockSpec(memory_space=pltpu.VMEM)
    hbm = pl.BlockSpec(memory_space=pl.ANY)
    dma = pltpu.SemaphoreType.DMA
    result = pl.pallas_call(
        functools.partial(kernel, n),
        out_shape=pltpu.VMEM((samples * QUERY_HEADS * steps, HEAD_SIZE), BF16),
        in_specs=[hbm, hbm, hbm, hbm, hbm, hbm, hbm, hbm, hbm],
        out_specs=vmem,
        scratch_shapes=[
            pltpu.SMEM(suffix_len.shape, jnp.int32),
            pltpu.SMEM(prompt_id.shape, jnp.int32),
            pltpu.VMEM(queries.shape, BF16),
            pltpu.VMEM(step_keys.shape, BF16),
            pltpu.VMEM(step_values.shape, BF16),
            pltpu.VMEM((samples, padded, width), BF16),
            pltpu.VMEM((samples, padded, width), BF16),
            pltpu.VMEM((prompts, 2 * block, half_width), BF16),
            pltpu.VMEM((prompts, 2 * block, half_width), BF16),
            pltpu.VMEM((HALF, prompts * HEAD_SIZE, 2 * block), BF16),
            pltpu.VMEM((2, pairs, 2 * core_rows, HEAD_SIZE), BF16),
            pltpu.VMEM((2 * pairs, samples, 2 * rows, 2 * HEAD_SIZE), BF16),
            pltpu.VMEM((n, pairs, 2 * core_rows, HEAD_SIZE), BF16),
            pltpu.VMEM((1, HEAD_SIZE), F32),
            pltpu.VMEM((n, 1, HEAD_SIZE), F32),
            pltpu.VMEM((lines, HALF, HEAD_SIZE, chip_rows), F32),
            pltpu.VMEM((lines, HALF, 8, chip_rows), F32),
            pltpu.VMEM((lines, HALF, HEAD_SIZE, chip_rows), I16),
            pltpu.VMEM((lines, pairs, 3, 2, chip_rows), F32),
            pltpu.VMEM((lines, HALF, HEAD_SIZE, chip_rows), I16),
            pltpu.VMEM((lines, pairs, 3, 2, chip_rows), F32),
            pltpu.VMEM((lines * 2 * pairs, HEAD_SIZE, chip_rows), I16),
            pltpu.VMEM((lines * 2 * pairs, 3, 1, chip_rows), F32),
            pltpu.VMEM((lines, 2, pairs, HEAD_SIZE, chip_rows), I16),
            pltpu.VMEM((lines, 2, pairs, 3, 1, chip_rows), F32),
            pltpu.VMEM((2 * pairs, HEAD_SIZE, chip_rows), F32),
            pltpu.VMEM((2 * pairs, 8, chip_rows), F32),
            pltpu.VMEM((2 * pairs, 2 * core_rows, HEAD_SIZE), F32),
            pltpu.VMEM((2 * pairs, 2 * core_rows, 1), F32),
            pltpu.VMEM((2 * pairs, 2 * core_rows, 1), F32),
            dma((9,)),
            dma((2,)),
            dma((2,)),
            dma,
            dma((2, lines // 2)),
            dma((2, lines // 2)),
            dma((n, pairs)),
            dma,
            dma((n,)),
            dma,
            dma,
            dma((lines, pairs)),
            dma((lines, pairs)),
            dma,
            dma,
            dma((lines, 2, pairs)),
            dma((lines, 2, pairs)),
        ],
        compiler_params=pltpu.CompilerParams(
            collective_id=0,
            has_side_effects=True,
            vmem_limit_bytes=60 << 20,
        ),
    )(
        suffix_len,
        prompt_id,
        queries,
        step_keys,
        step_values,
        sample_keys,
        sample_values,
        document_keys,
        document_values,
    )
    return result.reshape(samples, QUERY_HEADS, steps, HEAD_SIZE).transpose(0, 2, 1, 3).reshape(queries.shape)


def solution(mesh):
    return jax.shard_map(
        body,
        mesh=mesh,
        in_specs=(
            P(("groups", "seq"), None, None),
            P(("groups", "seq"), None, None),
            P(("groups", "seq"), None, None),
            P(("groups", "seq"), None, None),
            P(("groups", "seq"), None, None),
            P(("groups", "seq")),
            P(("groups", "seq")),
            P("groups", "seq", None),
            P("groups", "seq", None),
        ),
        out_specs=P(("groups", "seq"), None, None),
        check_vma=False,
    )
```
